32 devices in a mesh: dp: 8 (over y, x, core), tensor: 4 (over z).
Axes of the slice: x: 2, y: 2, z: 4, core: 2. Of those that a mesh axis runs over, the one named last changes fastest.
Arguments:
- tokens: bfloat16 [3072, 1536], P('dp'), may hold values from -6 to 6
- cotangent: bfloat16 [3072, 1536], P('dp'), may hold values from -6 to 6
- dest: int32 [3072], P('dp'), may hold values from 0 to 3071, as said below
- source: int32 [3072], P('dp'), may hold values from 0 to 3071, as said below
- lengths: int32 [24, 4], P('dp'), may hold values from 1 to 96, 128 in all within a row
- persist: bfloat16 [64, 1536], P(None, 'dp'), may hold values from -6 to 6
- gain_attn: bfloat16 [1536], P('dp'), may hold values from 0.5 to 1.5
- w_query_mem: bfloat16 [1536, 1536], P('tensor', 'dp'), may hold values from -0.15625 to 0.15625
- mem_in: bfloat16 [1536, 6144], P('dp', 'tensor'), may hold values from -0.15625 to 0.15625
- mem_out: bfloat16 [6144, 1536], P('tensor', 'dp'), may hold values from -0.078125 to 0.078125
- w_query: bfloat16 [1536, 1536], P('dp', 'tensor'), may hold values from -0.15625 to 0.15625
- w_key: bfloat16 [1536, 1536], P('dp', 'tensor'), may hold values from -0.15625 to 0.15625
- w_value: bfloat16 [1536, 1536], P('dp', 'tensor'), may hold values from -0.15625 to 0.15625
- w_output: bfloat16 [1536, 1536], P('tensor', 'dp'), may hold values from -0.4375 to 0.4375
- gain_mem: bfloat16 [1536], P('dp'), may hold values from 0.5 to 1.5
- w_key_mem: bfloat16 [1536, 1536], P('tensor', 'dp'), may hold values from -0.15625 to 0.15625
- w_value_mem: bfloat16 [1536, 1536], P('tensor', 'dp'), may hold values from -0.15625 to 0.15625
- w_rate: bfloat16 [1536], P('dp'), may hold values from -0.3125 to 0.3125
- gain_ffn: bfloat16 [1536], P('dp'), may hold values from 0.5 to 1.5
- w_gate: bfloat16 [1536, 4096], P('dp', 'tensor'), may hold values from -0.15625 to 0.15625
- w_up: bfloat16 [1536, 4096], P('dp', 'tensor'), may hold values from -0.15625 to 0.15625
- w_down: bfloat16 [4096, 1536], P('tensor', 'dp'), may hold values from -0.09375 to 0.09375
Outputs:
- output: bfloat16 [3072, 1536], P('dp')
- grad_tokens: bfloat16 [3072, 1536], P('dp')
- grad_persist: float32 [64, 1536], P(None, 'dp')
- grad_gain_attn: float32 [1536], P('dp')
- grad_w_query_mem: float32 [1536, 1536], P('tensor', 'dp')
- grad_mem_in: float32 [1536, 6144], P('dp', 'tensor')
- grad_mem_out: float32 [6144, 1536], P('tensor', 'dp')
- grad_w_query: float32 [1536, 1536], P('dp', 'tensor')
- grad_w_key: float32 [1536, 1536], P('dp', 'tensor')
- grad_w_value: float32 [1536, 1536], P('dp', 'tensor')
- grad_w_output: float32 [1536, 1536], P('tensor', 'dp')
- grad_gain_mem: float32 [1536], P('dp')
- grad_w_key_mem: float32 [1536, 1536], P('tensor', 'dp')
- grad_w_value_mem: float32 [1536, 1536], P('tensor', 'dp')
- grad_w_rate: float32 [1536], P('dp')
- grad_gain_ffn: float32 [1536], P('dp')
- grad_w_gate: float32 [1536, 4096], P('dp', 'tensor')
- grad_w_up: float32 [1536, 4096], P('dp', 'tensor')
- grad_w_down: float32 [4096, 1536], P('tensor', 'dp')
The draws below stay inside these ranges and needn't reach their ends.
Inputs may be any that keep to these rules, and one draw needn't show every extreme that they name: A permutation of the 3072 positions: dest gives each token's place in the dealt order, in which index d of dp holds places d * 384 to (d + 1) * 384 - 1. The tokens that one index of dp holds go exactly 48 to each index of dp. `source`: the inverse permutation of dest. `lengths`: each row sums to 128; its longest sequence has exactly 96 tokens.
All inputs are finite; a program needn't handle non-finite values.
Results may differ from the reference program's by a relative error of at most 0.025.
Values may be sent and summed in bfloat16 or wider, within the bound.
A program may use at most 320 MiB of HBM per device.

```python
import math
import jax
import jax.numpy as jnp
import numpy as np
from jax import lax

D = 1536
HD = 96
NP = 64
MH = 6144
FF = 4096
R = 128
NSEQ = 4
SEQ_MAX = 96
TOK_DEV = 384
TOKENS = 3072
GROUPS = 24
N_DP = 8


def deal_tables(key):
    per_peer = TOK_DEV // N_DP
    first_key, second_key = jax.random.split(jax.random.fold_in(key, 7))
    senders_base = jnp.repeat(jnp.arange(N_DP, dtype=jnp.int32), per_peer)

    def shuffle_senders(sub_key):
        return jax.random.permutation(sub_key, senders_base)

    def shuffle_local(sub_key):
        return jax.random.permutation(sub_key, jnp.arange(TOK_DEV, dtype=jnp.int32))
    senders = jax.vmap(shuffle_senders)(jax.random.split(first_key, N_DP)).reshape(-1)
    ordering = jnp.argsort(senders, stable=True).astype(jnp.int32)
    shuffled = jax.vmap(shuffle_local)(jax.random.split(second_key, N_DP)).reshape(-1)
    anchor = jnp.arange(TOKENS, dtype=jnp.int32) // TOK_DEV * TOK_DEV + shuffled
    source_table = jnp.zeros((TOKENS,), jnp.int32).at[ordering].set(anchor)
    dest_table = jnp.zeros((TOKENS,), jnp.int32).at[source_table].set(jnp.arange(TOKENS, dtype=jnp.int32))
    return (dest_table, source_table)


def draw_dest(key, part):
    return deal_tables(key)[0]


def draw_source(key, part):
    return deal_tables(key)[1]


def levels(rng, extent, pieces, least, top_value):
    gain, own = 1.0, jax.random.fold_in(rng, 6)
    for axis_at, shards_of in pieces:
        draws = jnp.exp(jax.random.uniform(jax.random.fold_in(own, axis_at), (shards_of,), jnp.float32, least / len(pieces), top_value / len(pieces)))
        gain = gain * jnp.repeat(draws, extent[axis_at] // shards_of).reshape([-1 if axis == axis_at else 1 for axis in range(len(extent))])
    return gain


def length_profile(count, total, reach, skew):
    weights = [(1 << 20) // math.isqrt(rank ** skew) + 1 for rank in range(2, count + 1)]
    rest, counts = total - reach - (count - 1), [1] * (count - 1)
    while rest > 0:
        candidates = [i for i in range(count - 1) if counts[i] < reach]
        pool, left = sum([weights[i] for i in candidates]), rest
        for i in candidates:
            extra = min(reach - counts[i], max(1, left * weights[i] // pool), rest)
            counts[i] = counts[i] + extra
            rest = rest - extra
    return np.array([reach] + counts)


def ragged_sizes(rng, amount, total, most, slope):
    if amount == 2:
        one = jax.random.randint(rng, (), max(1, total - most), min(most, total - 1) + 1)
        return jnp.stack([one, total - one])
    sizes = jnp.asarray(length_profile(amount, total, most, slope), jnp.int32)
    couples = (amount - 1) // 2
    source_of, taker = sizes[1:1 + 2 * couples:2], sizes[2:2 + 2 * couples:2]
    room = jnp.minimum(source_of - 1, most - taker)
    moved = jax.random.randint(jax.random.fold_in(rng, 1), (couples,), 0, 1 << 20) % (room + 1)
    sizes = sizes.at[1:1 + 2 * couples:2].set(source_of - moved).at[2:2 + 2 * couples:2].set(taker + moved)
    return sizes[jax.random.permutation(jax.random.fold_in(rng, 2), amount)]


def bell_draw(own_key, dims, spread, bound, pieces=(), kind=jnp.bfloat16):
    entries = spread * jax.random.normal(own_key, dims, jnp.float32)
    if pieces:
        entries = entries * levels(own_key, dims, pieces, -0.22, 0.18)
    return jnp.clip(entries, -bound, bound).astype(kind)


def setup_inputs(seed: int = 0) -> dict:
    seeds = jax.random.split(jax.random.key(seed), 23)
    return {
        "tokens": bell_draw(seeds[0], (TOKENS, D), 1.0, 6.0, ((0, 8),)),
        "cotangent": bell_draw(seeds[1], (TOKENS, D), 1.0, 6.0, ((0, 8),)),
        "dest": draw_dest(jax.random.fold_in(seeds[22], 71), 0),
        "source": draw_source(jax.random.fold_in(seeds[22], 71), 0),
        "lengths": jax.vmap(lambda own: ragged_sizes(own, NSEQ, R, SEQ_MAX, 2))(jax.random.split(seeds[4], GROUPS)).reshape((GROUPS, NSEQ)).astype(jnp.int32),
        "persist": bell_draw(seeds[5], (NP, D), 1.0, 6.0, ((1, 8),)),
        "gain_attn": jnp.clip(1.0 + 0.1 * jax.random.normal(seeds[6], (D,), jnp.float32), 0.5, 1.5).astype(jnp.bfloat16),
        "w_query_mem": bell_draw(seeds[7], (D, D), D ** -0.5, 0.15625, ((0, 4), (1, 8))),
        "mem_in": bell_draw(seeds[8], (D, MH), D ** -0.5, 0.15625, ((0, 8), (1, 4))),
        "mem_out": bell_draw(seeds[9], (MH, D), MH ** -0.5, 0.078125, ((0, 4), (1, 8))),
        "w_query": bell_draw(seeds[10], (D, D), D ** -0.5, 0.15625, ((0, 8), (1, 4))),
        "w_key": bell_draw(seeds[11], (D, D), D ** -0.5, 0.15625, ((0, 8), (1, 4))),
        "w_value": bell_draw(seeds[12], (D, D), D ** -0.5, 0.15625, ((0, 8), (1, 4))),
        "w_output": bell_draw(seeds[13], (D, D), (D // 8) ** -0.5, 0.4375, ((0, 4), (1, 8))),
        "gain_mem": jnp.clip(1.0 + 0.1 * jax.random.normal(seeds[14], (D,), jnp.float32), 0.5, 1.5).astype(jnp.bfloat16),
        "w_key_mem": bell_draw(seeds[15], (D, D), D ** -0.5, 0.15625, ((0, 4), (1, 8))),
        "w_value_mem": bell_draw(seeds[16], (D, D), D ** -0.5, 0.15625, ((0, 4), (1, 8))),
        "w_rate": bell_draw(seeds[17], (D,), (D // 4) ** -0.5, 0.3125, ((0, 8),)),
        "gain_ffn": jnp.clip(1.0 + 0.1 * jax.random.normal(seeds[18], (D,), jnp.float32), 0.5, 1.5).astype(jnp.bfloat16),
        "w_gate": bell_draw(seeds[19], (D, FF), D ** -0.5, 0.15625, ((0, 8), (1, 4))),
        "w_up": bell_draw(seeds[20], (D, FF), D ** -0.5, 0.15625, ((0, 8), (1, 4))),
        "w_down": bell_draw(seeds[21], (FF, D), FF ** -0.5, 0.09375, ((0, 4), (1, 8))),
    }


EPSILON = 1e-06
RATE_SCALE = 4e-05
NEG_LARGE = -1e+30
HIGH = lax.Precision.HIGHEST

@jax.custom_vjp
def low(v):
    return lax.optimization_barrier(v.astype(jnp.bfloat16)).astype(jnp.float32)

@jax.custom_vjp
def low_back(v):
    return v

def low_keep(v):
    return (low(v), None)

def low_pass(kept, grad):
    return (grad,)

def back_keep(v):
    return (v, None)

def back_low(kept, grad):
    return (low(grad),)
low.defvjp(low_keep, low_pass)
low_back.defvjp(back_keep, back_low)

def round_both(operand):
    return low(low_back(operand))

def matmul(left_side, right_side):
    return jnp.dot(left_side, right_side, precision=HIGH, preferred_element_type=jnp.float32)

def rms_norm(operand, scaling):
    return operand * lax.rsqrt(lax.optimization_barrier(jnp.mean(operand * operand, axis=-1, keepdims=True)) + EPSILON) * scaling

def silu_slope(operand):
    sigma = jax.nn.sigmoid(operand)
    return sigma * (1.0 + operand * (1.0 - sigma))

def causal_mask(lens_row, row_count):
    position = jnp.arange(row_count, dtype=jnp.int32)
    bounds = jnp.cumsum(lens_row).astype(jnp.int32)
    segment = lax.optimization_barrier(jnp.sum((position[:, None] >= bounds[None, :]).astype(jnp.int32), axis=1))
    same = segment[:, None] == segment[None, :]
    return same & (position[None, :] <= position[:, None])

def attend(normed_in, memory_tokens, persistent, w_query, w_key, w_value, w_output, causal):
    row_count = normed_in.shape[0]
    head_count = w_query.shape[1] // HD
    query = round_both(matmul(normed_in, w_query)).reshape(row_count, head_count, HD)
    context = jnp.concatenate([persistent, memory_tokens, normed_in], axis=0)
    keys = round_both(matmul(context, w_key)).reshape(-1, head_count, HD)
    values = round_both(matmul(context, w_value)).reshape(-1, head_count, HD)
    allowed = jnp.concatenate([jnp.ones((row_count, persistent.shape[0]), dtype=bool), causal, causal], axis=1)
    scores = jnp.einsum('qhd,khd->hqk', query, keys, precision=HIGH) * HD ** (-0.5)
    scores = low_back(scores)
    scores = jnp.where(allowed[None], scores, NEG_LARGE)
    weights = jax.nn.softmax(scores, axis=-1)
    mixed = jnp.einsum('hqk,khd->qhd', low(weights), values, precision=HIGH).reshape(row_count, head_count * HD)
    return matmul(round_both(mixed), w_output)

def group_forward(inputs, lens_row, params):
    persist, gain_attn, w_query_mem, mem_in, mem_out, w_query, w_key, w_value, w_output, gain_mem, w_key_mem, w_value_mem, w_rate, gain_ffn, w_gate, w_up, w_down = params
    causal = causal_mask(lens_row, inputs.shape[0])
    normed_in = low(rms_norm(inputs, gain_attn))
    query_mem = round_both(matmul(normed_in, w_query_mem))
    hidden_read = low(jax.nn.silu(low_back(matmul(query_mem, mem_in))))
    memory_tokens = round_both(matmul(hidden_read, mem_out))
    attended = attend(normed_in, memory_tokens, low(persist), w_query, w_key, w_value, w_output, causal)
    after_attn = inputs + low_back(attended)
    normed_mid = rms_norm(after_attn, gain_mem)
    rate = RATE_SCALE * 2.0 * jax.nn.sigmoid(jnp.dot(normed_mid, w_rate, precision=HIGH))
    normed_low = low(normed_mid)
    key_mem = round_both(matmul(normed_low, w_key_mem))
    value_mem = matmul(normed_low, w_value_mem)
    key_hidden = low_back(matmul(key_mem, mem_in))
    key_act = low(jax.nn.silu(key_hidden))
    predicted = matmul(key_act, mem_out)
    error_step = round_both(rate[:, None] * (predicted - value_mem))
    back_hidden = round_both(matmul(error_step, mem_out.T) * silu_slope(key_hidden))
    gram = jnp.where(causal, matmul(key_mem, key_mem.T), 0.0)
    new_hidden = low_back(key_hidden - matmul(gram, back_hidden))
    new_act = low(jax.nn.silu(new_hidden))
    pair_act = jnp.where(causal, matmul(new_act, key_act.T), 0.0)
    memory_read = matmul(new_act, mem_out) - matmul(pair_act, error_step)
    after_mem = after_attn + low_back(memory_read)
    normed_ffn = low(rms_norm(after_mem, gain_ffn))
    gate = low_back(matmul(normed_ffn, w_gate))
    up_part = low_back(matmul(normed_ffn, w_up))
    hidden_ffn = low(jax.nn.silu(gate) * up_part)
    return after_mem + low_back(matmul(hidden_ffn, w_down))

def reference(tokens, cotangent, dest, source, lengths, persist, gain_attn, w_query_mem, mem_in, mem_out, w_query, w_key, w_value, w_output, gain_mem, w_key_mem, w_value_mem, w_rate, gain_ffn, w_gate, w_up, w_down):
    params = tuple((member.astype(jnp.float32) for member in (persist, gain_attn, w_query_mem, mem_in, mem_out, w_query, w_key, w_value, w_output, gain_mem, w_key_mem, w_value_mem, w_rate, gain_ffn, w_gate, w_up, w_down)))
    dealt = tokens.astype(jnp.float32)[source].reshape(GROUPS, R, D)
    dealt_cot = cotangent.astype(jnp.float32)[source].reshape(GROUPS, R, D)

    def whole(inputs, weights):

        def advance(carry, entry):
            return (carry, jax.checkpoint(group_forward)(entry[0], entry[1], weights))
        _, results = lax.scan(advance, jnp.zeros((), jnp.float32), (inputs, lengths))
        return results
    results, pull = jax.vjp(whole, dealt, params)
    grad_dealt, grad_params = pull(dealt_cot)
    output = results.reshape(TOKENS, D)[dest].astype(jnp.bfloat16)
    grad_tokens = grad_dealt.reshape(TOKENS, D)[dest].astype(jnp.bfloat16)
    return (output, grad_tokens, grad_params[0], grad_params[1], grad_params[2], grad_params[3], grad_params[4], grad_params[5], grad_params[6], grad_params[7], grad_params[8], grad_params[9], grad_params[10], grad_params[11], grad_params[12], grad_params[13], grad_params[14], grad_params[15], grad_params[16])
```

```python
import functools

import jax
import jax.numpy as jnp
from jax import lax
from jax.experimental import pallas as pl
from jax.experimental.pallas import tpu as pltpu
from jax.sharding import PartitionSpec as P

HD = 96
EPSILON = 1e-06
RATE_SCALE = 8e-05
NEG_LARGE = -1e30
BF = jnp.bfloat16
F32 = jnp.float32
MESH = pl.DeviceIdType.MESH
TILE = 128


def chain_sum_kernel(pieces, layout, x_ref, *refs):
    given = sum(len(widths) for _, parts in layout for widths in parts)
    fills, refs = refs[:given], refs[given:]
    o_ref, refs = refs[0], refs[1:]
    if layout:
        g_ref, refs = refs[0], refs[1:]
    from_outer, from_inner, part, sent_a, got_up, sent_b, got_across, got_total = refs[:8]
    me = lax.axis_index("tensor")
    step = x_ref.shape[0] // pieces
    low = me < 2
    outer = jnp.logical_or(me == 0, me == 3)
    inner = jnp.logical_not(outer)
    outer_peer = jnp.where(low, 0, 3)
    inner_peer = jnp.where(low, 2, 1)
    toward = jnp.where(low, 1, 2)
    barrier = pltpu.get_barrier_semaphore()

    def tell(peer):
        pl.semaphore_signal(barrier, inc=1, device_id={"tensor": peer}, device_id_type=MESH)

    def at(piece):
        return pl.ds(pl.multiple_of(piece * step, step), step)

    def send(src, dst, send_sem, recv_sem, peer):
        return pltpu.make_async_remote_copy(
            src_ref=src,
            dst_ref=dst,
            send_sem=send_sem,
            recv_sem=recv_sem,
            device_id={"tensor": peer},
            device_id_type=MESH,
        )

    def up(p):
        return send(x_ref.at[at(p)], from_outer.at[at(p)], sent_a.at[p], got_up.at[p], toward)

    def across(p):
        return send(part.at[at(p)], from_inner.at[at(p)], sent_b.at[p], got_across.at[p], inner_peer)

    def down(p):
        return send(o_ref.at[at(p)], o_ref.at[at(p)], sent_a.at[p], got_total.at[p], outer_peer)

    def put(tile):
        stage, put_sem = refs[8], refs[9]
        rows = pl.ds(pl.multiple_of(tile * TILE, TILE), TILE)
        slot = lax.rem(tile, 2)
        return pltpu.make_async_copy(stage.at[slot], g_ref.at[rows], put_sem.at[slot])

    def fill(tile):
        stage = refs[8]
        columns = pl.ds(pl.multiple_of(tile * TILE, TILE), TILE)
        slot = lax.rem(tile, 2)

        @pl.when(tile >= 2)
        def _():
            put(tile - 2).wait()

        first, offset = 0, 0
        for width, parts in layout:
            for start in range(0, width, 512):
                span = min(512, width - start)
                total, index = None, first
                for part_sizes in parts:
                    if len(part_sizes) == 1:
                        term = fills[index][columns, start : start + span].astype(F32)
                    else:
                        term = lax.dot_general(
                            fills[index][:, columns],
                            fills[index + 1][:, start : start + span],
                            (((0,), (0,)), ((), ())),
                            preferred_element_type=F32,
                        )
                    total = term if total is None else total + term
                    index += len(part_sizes)
                stage[slot, :, offset + start : offset + start + span] = total.astype(BF)
            first, offset = index, offset + width
        put(tile).start()

    @pl.when(outer)
    def _():
        tell(toward)
        pl.semaphore_wait(barrier, 1)

        @pl.loop(0, pieces)
        def _(p):
            up(p).start()

    @pl.when(inner)
    def _():
        tell(outer_peer)
        tell(inner_peer)
        pl.semaphore_wait(barrier, 2)

    def first_add(p):
        up(p).wait_recv()
        part[at(p), :] = (
            x_ref[at(p), :].astype(F32) + from_outer[at(p), :].astype(F32)
        ).astype(part.dtype)
        across(p).start()

    def second_add(p):
        across(p).wait_recv()
        o_ref[at(p), :] = (
            part[at(p), :].astype(F32) + from_inner[at(p), :].astype(F32)
        ).astype(o_ref.dtype)
        down(p).start()

    tiles = g_ref.shape[0] // TILE if layout else 0

    @pl.loop(0, max(pieces + 1, tiles))
    def _(p):
        @pl.when(jnp.logical_and(inner, p < pieces))
        def _():
            first_add(p)

        @pl.when(jnp.logical_and(inner, jnp.logical_and(p >= 1, p <= pieces)))
        def _():
            second_add(p - 1)

        if layout:

            @pl.when(p < tiles)
            def _():
                fill(p)

    if layout:
        put(tiles - 2).wait()
        put(tiles - 1).wait()

    @pl.when(outer)
    def _():
        @pl.loop(0, pieces)
        def _(p):
            down(p).wait_recv()
            up(p).wait_send()

    @pl.when(inner)
    def _():
        @pl.loop(0, pieces)
        def _(p):
            across(p).wait_send()
            down(p).wait_send()


def chain_sum(x, call_id=1, products=()):
    rows, cols = x.shape
    pieces = rows // 32
    dma = pltpu.SemaphoreType.DMA
    vmem = pl.BlockSpec(memory_space=pltpu.VMEM)
    layout = tuple(
        (pairs[0][1].shape[1], tuple((0,) * len(pair) for pair in pairs)) for pairs in products
    )
    fills = [array for pairs in products for pair in pairs for array in pair]
    out_shape = [jax.ShapeDtypeStruct((rows, cols), BF)]
    out_specs = [vmem]
    scratch = [pltpu.VMEM((rows, cols), BF)] * 3 + [dma((pieces,))] * 5
    if products:
        width, high = sum(w for w, _ in layout), products[0][0][0].shape[1]
        out_shape.append(jax.ShapeDtypeStruct((high, width), BF))
        out_specs.append(pl.BlockSpec(memory_space=pl.ANY))
        scratch += [pltpu.VMEM((2, TILE, width), BF), dma((2,))]
    out = pl.pallas_call(
        functools.partial(chain_sum_kernel, pieces, layout),
        out_shape=out_shape,
        in_specs=[vmem] * (1 + len(fills)),
        out_specs=out_specs,
        scratch_shapes=scratch,
        compiler_params=pltpu.CompilerParams(collective_id=call_id, has_side_effects=True),
        cost_estimate=pl.CostEstimate(flops=0, bytes_accessed=10**8, transcendentals=0),
        name="chain_sum",
    )(x.astype(BF), *fills)
    return out if products else out[0]


def dot(left, right):
    return lax.dot_general(left, right, (((1,), (0,)), ((), ())), preferred_element_type=F32)


def dot_t(left, right):
    return lax.dot_general(left, right, (((1,), (1,)), ((), ())), preferred_element_type=F32)


def t_dot(left, right):
    return lax.dot_general(left, right, (((0,), (0,)), ((), ())), preferred_element_type=F32)


def batch_dot(spec, left, right):
    return jnp.einsum(spec, left, right, preferred_element_type=F32)


def together(*values):
    return lax.optimization_barrier(values)


def rms(v):
    return lax.rsqrt(jnp.mean(v * v, axis=-1, keepdims=True) + EPSILON)


def rms_back(v, r, gain, grad):
    scaled = grad * gain
    inner = jnp.sum(scaled * v, axis=-1, keepdims=True)
    return r * scaled - v * (r * r * r) * (inner / v.shape[-1])


def silu_parts(z):
    s = jax.nn.sigmoid(z)
    return s, z * s, s * (1.0 + z * (1.0 - s))


def per_device(
    tokens,
    cotangent,
    dest,
    source,
    lengths,
    persist,
    gain_attn,
    w_query_mem,
    mem_in,
    mem_out,
    w_query,
    w_key,
    w_value,
    w_output,
    gain_mem,
    w_key_mem,
    w_value_mem,
    w_rate,
    gain_ffn,
    w_gate,
    w_up,
    w_down,
):
    count, width = tokens.shape
    shard = gain_attn.shape[0]
    ranks = width // shard
    batches, _ = lengths.shape
    rows = count // batches
    hidden = mem_in.shape[1]
    inner = w_query.shape[1]
    heads = inner // HD
    slots = persist.shape[0]
    me = lax.axis_index("tensor")

    def gather(*parts):
        packed = jnp.concatenate(parts, axis=1)
        whole = lax.all_gather(packed, "dp", axis=0, tiled=True)
        out, low = [], 0
        for part in parts:
            out.append(whole[:, low : low + part.shape[1]])
            low += part.shape[1]
        return out

    vectors = jnp.stack([gain_attn, gain_mem, gain_ffn, w_rate], axis=1)
    pad = jnp.zeros((shard, 128 - slots - 4), BF)
    small, wqm_t = gather(jnp.concatenate([persist.T, vectors, pad], axis=1), w_query_mem.T)
    w_in, w_out_t = gather(mem_in, mem_out.T)
    persistent = small[:, :slots].T
    gains = small[:, slots : slots + 4].astype(F32).T
    g_attn, g_mem, g_ffn, rate_w = (gains[i][None, :] for i in range(4))

    ends = lax.axis_size("tensor")
    columns = jnp.concatenate([w_key_mem, w_value_mem], axis=1)
    before, after = [columns], [columns]
    for _ in range(ends - 1):
        before.append(lax.ppermute(before[-1], "tensor", [(i, i + 1) for i in range(ends - 1)]))
        after.append(lax.ppermute(after[-1], "tensor", [(i + 1, i) for i in range(ends - 1)]))
    line = jnp.concatenate(before[:0:-1] + after, axis=0)
    high = columns.shape[0]
    tall = lax.dynamic_slice_in_dim(line, (ends - 1 - me) * high, ends * high, 0)

    place = jnp.arange(count, dtype=jnp.int32)
    home = dest // count
    earlier = (home[None, :] == home[:, None]) & (place[None, :] < place[:, None])
    sent_at = home * (count // ranks) + jnp.sum(earlier.astype(jnp.int32), axis=1)
    came_at = jnp.sum((source[None, :] < source[:, None]).astype(jnp.int32), axis=1)
    send_m = (sent_at[None, :] == place[:, None]).astype(BF)
    deal_m = (came_at[:, None] == place[None, :]).astype(BF)

    def exchange(v):
        return lax.all_to_all(
            dot(send_m, v).astype(BF), "dp", split_axis=0, concat_axis=0, tiled=True
        )

    def give_back(v):
        back = lax.all_to_all(
            t_dot(deal_m, v.astype(BF)).astype(BF), "dp", split_axis=0, concat_axis=0, tiled=True
        )
        return t_dot(send_m, back).astype(BF)

    dealt = dot(deal_m, exchange(tokens)).astype(BF)
    dealt, later, late_query, late_key, late_value, late_output = together(
        dealt, cotangent, w_query, w_key, w_value, w_output
    )
    wq, wk, wv, wo_t = gather(late_query, late_key, late_value, late_output.T)
    cotangent_arrived = exchange(later)
    x = dealt.astype(F32)

    position = jnp.arange(rows, dtype=jnp.int32)
    bounds = jnp.cumsum(lengths, axis=1)
    segment = jnp.sum((position[None, :, None] >= bounds[:, None, :]).astype(jnp.int32), axis=2)
    causal = (segment[:, :, None] == segment[:, None, :]) & (
        position[None, None, :] <= position[None, :, None]
    )

    def split(v):
        return v.reshape(batches, rows, v.shape[-1])

    def join(v):
        return v.reshape(count, v.shape[-1])

    def own(v):
        return lax.dynamic_slice_in_dim(v, me * inner, inner, 1)

    def in_own(v):
        return lax.dynamic_update_slice_in_dim(
            jnp.zeros((v.shape[0], width), v.dtype), v, me * inner, 1
        )

    r1 = rms(x)
    n1 = (x * r1 * g_attn).astype(BF)
    n1_own = own(n1)
    query_mem = chain_sum(dot_t(n1_own, wqm_t))
    query_mem, cotangent_arrived, tall = together(query_mem, cotangent_arrived, tall)
    wkm_t, wvm_t = gather(tall[:, :shard].T, tall[:, shard:].T)
    d_out_low = dot(deal_m, cotangent_arrived).astype(BF)
    read_s, read_act, read_slope = silu_parts(dot(query_mem, w_in))
    read_low = read_act.astype(BF)
    memory = chain_sum(dot_t(read_low, w_out_t))

    query = dot(n1, wq).astype(BF)
    key_p, value_p = dot(persistent, wk).astype(BF), dot(persistent, wv).astype(BF)
    key_m, value_m = dot(memory, wk).astype(BF), dot(memory, wv).astype(BF)
    key_x, value_x = dot(n1, wk).astype(BF), dot(n1, wv).astype(BF)

    def context(p, m, t):
        wide = jnp.broadcast_to(p[None], (batches,) + p.shape)
        all_rows = jnp.concatenate([wide, split(m), split(t)], axis=1)
        return all_rows.reshape(batches, -1, heads, HD)

    keys, values = context(key_p, key_m, key_x), context(value_p, value_m, value_x)
    allowed = jnp.concatenate(
        [jnp.ones((batches, rows, slots), dtype=bool), causal, causal], axis=2
    )[:, None]
    query4 = query.reshape(batches, rows, heads, HD)
    scores = batch_dot("bqhd,bkhd->bhqk", query4, keys) * HD ** (-0.5)
    weights = jax.nn.softmax(jnp.where(allowed, scores, NEG_LARGE), axis=-1)
    weights_low = weights.astype(BF)
    mixed = batch_dot("bhqk,bkhd->bqhd", weights_low, values).astype(BF).reshape(count, inner)
    mixed, late_gate, late_up, late_down = together(mixed, w_gate, w_up, w_down)
    wg, wu, wd_t = gather(late_gate, late_up, late_down.T)
    after_attn = x + chain_sum(dot_t(mixed, wo_t)).astype(F32)

    r2 = rms(after_attn)
    n2 = after_attn * r2 * g_mem
    rate_s = jax.nn.sigmoid(jnp.sum(n2 * rate_w, axis=1, keepdims=True))
    rate = RATE_SCALE * rate_s
    n2_low = n2.astype(BF)
    n2_own = own(n2_low)
    key_mem = dot_t(n2_low, wkm_t).astype(BF)
    value_part = dot_t(n2_own, own(wvm_t))
    key_hidden = dot(key_mem, w_in)
    key_s, key_silu, key_slope = silu_parts(key_hidden)
    key_act = key_silu.astype(BF)
    miss = chain_sum(dot_t(key_act, w_out_t) - value_part).astype(F32)
    error = (rate * miss).astype(BF)
    back_pre = dot(error, w_out_t)
    back_hidden = (back_pre * key_slope).astype(BF)
    gram = jnp.where(causal, batch_dot("bik,bjk->bij", split(key_mem), split(key_mem)), 0.0).astype(BF)
    new_hidden = key_hidden - join(batch_dot("bij,bjk->bik", gram, split(back_hidden)))
    _, new_silu, new_slope = silu_parts(new_hidden)
    new_act = new_silu.astype(BF)
    pair = jnp.where(causal, batch_dot("bik,bjk->bij", split(new_act), split(key_act)), 0.0).astype(BF)
    update = dot_t(new_act, w_out_t) - join(batch_dot("bij,bjk->bik", pair, split(error)))
    after_mem = after_attn + chain_sum(update).astype(F32)

    r3 = rms(after_mem)
    n3 = (after_mem * r3 * g_ffn).astype(BF)
    gate, up = dot(n3, wg), dot(n3, wu)
    _, gate_silu, gate_slope = silu_parts(gate)
    ffn_act = (gate_silu * up).astype(BF)
    ffn_own = lax.psum_scatter(
        dot_t(ffn_act, wd_t).astype(BF), "tensor", scatter_dimension=1, tiled=True
    )

    d_ffn = dot(d_out_low, wd_t)
    d_gate = (d_ffn * up * gate_slope).astype(BF)
    d_up = (d_ffn * gate_silu).astype(BF)
    d_n3, gw_ffn = chain_sum(
        dot_t(d_gate, wg) + dot_t(d_up, wu),
        2,
        [[(d_out_low, ffn_act)], [(n3, d_gate)], [(n3, d_up)]],
    )
    d_n3 = d_n3.astype(F32)
    gg_ffn = jnp.sum(d_n3 * after_mem * r3, axis=0)
    d_after_mem = d_out_low.astype(F32) + rms_back(after_mem, r3, g_ffn, d_n3)
    d_update = d_after_mem.astype(BF)

    d_pair = jnp.where(
        causal, -batch_dot("bik,bjk->bij", split(d_update), split(error)), 0.0
    ).astype(BF)
    d_new_act = dot(d_update, w_out_t) + join(batch_dot("bij,bjk->bik", d_pair, split(key_act)))
    d_key_act = join(batch_dot("bij,bik->bjk", d_pair, split(new_act)))
    d_new_hidden = (d_new_act * new_slope).astype(BF)
    d_gram = jnp.where(
        causal, -batch_dot("bik,bjk->bij", split(d_new_hidden), split(back_hidden)), 0.0
    ).astype(BF)
    d_back = (-join(batch_dot("bij,bik->bjk", gram, split(d_new_hidden)))).astype(BF).astype(F32)
    d_back_pre = (d_back * key_slope).astype(BF)
    slope_grad = key_s * (1.0 - key_s) * (2.0 + key_hidden * (1.0 - 2.0 * key_s))
    d_hidden_part = d_new_hidden.astype(F32) + d_back * back_pre * slope_grad
    d_error_part = dot_t(d_back_pre, w_out_t) - join(
        batch_dot("bij,bik->bjk", pair, split(d_update))
    )
    share_ffn = lax.psum_scatter(gw_ffn, "dp", scatter_dimension=0, tiled=True)
    d_error = chain_sum(d_error_part).astype(F32)
    d_rate = jnp.sum(d_error * miss, axis=1, keepdims=True)
    d_miss = (rate * d_error).astype(BF)
    d_key_act = d_key_act + dot(d_miss, w_out_t)
    d_key_hidden = (d_hidden_part + d_key_act * key_slope).astype(BF)
    d_key_part = dot_t(d_key_hidden, w_in) + join(
        batch_dot("bij,bjk->bik", d_gram, split(key_mem))
        + batch_dot("bij,bik->bjk", d_gram, split(key_mem))
    )
    d_key_part, ffn_own = together(d_key_part.astype(BF), ffn_own)
    result_own = give_back(own(after_mem) + ffn_own.astype(F32))
    d_key, gw_out_early = chain_sum(
        d_key_part, 6, [[(d_update, new_act), (error, d_back_pre)]]
    )
    d_n2 = dot(d_key, wkm_t) - dot(d_miss, wvm_t)
    d_logit = d_rate * rate * (1.0 - rate_s)
    gg_rate = jnp.sum(n2 * d_logit, axis=0)
    d_n2 = d_n2 + d_logit * rate_w
    gg_mem = jnp.sum(d_n2 * after_attn * r2, axis=0)
    d_after_attn = d_after_mem + rms_back(after_attn, r2, g_mem, d_n2)
    d_attn = d_after_attn.astype(BF)

    d_mixed = dot(d_attn, wo_t).astype(BF)
    d_mixed4 = d_mixed.reshape(batches, rows, heads, HD)
    d_weights = batch_dot("bqhd,bkhd->bhqk", d_mixed4, values)
    d_values = batch_dot("bhqk,bqhd->bkhd", weights_low, d_mixed4)
    d_scores = (
        weights * (d_weights - jnp.sum(weights * d_weights, axis=-1, keepdims=True))
    ).astype(BF)
    d_query = batch_dot("bhqk,bkhd->bqhd", d_scores, keys) * HD ** (-0.5)
    d_keys = batch_dot("bhqk,bqhd->bkhd", d_scores, query4) * HD ** (-0.5)
    d_query = d_query.astype(BF).reshape(count, inner)

    def apart(v):
        v = v.reshape(batches, -1, inner)
        return (
            jnp.sum(v[:, :slots], axis=0).astype(BF),
            join(v[:, slots : slots + rows]).astype(BF),
            join(v[:, slots + rows :]).astype(BF),
        )

    dk_p, dk_m, dk_x = apart(d_keys)
    dv_p, dv_m, dv_x = apart(d_values)
    d_memory_part, share_ffn, result_own = together(
        (dot_t(dk_m, wk) + dot_t(dv_m, wv)).astype(BF), share_ffn, result_own
    )
    output = lax.all_gather(result_own, "tensor", axis=1, tiled=True)
    d_memory, gw_attn = chain_sum(
        d_memory_part,
        3,
        [
            [(d_key, n2_own)],
            [(d_miss, n2_own)],
            [(d_attn, mixed)],
            [(n1, d_query)],
            [(persistent, dk_p), (memory, dk_m), (n1, dk_x)],
            [(persistent, dv_p), (memory, dv_m), (n1, dv_x)],
        ],
    )
    d_n1_part = dot_t(d_query, wq) + dot_t(dk_x, wk) + dot_t(dv_x, wv)
    d_persist_part = dot_t(dk_p, wk) + dot_t(dv_p, wv)

    share_attn = lax.psum_scatter(gw_attn, "dp", scatter_dimension=0, tiled=True)
    d_read = (dot(d_memory, w_out_t) * read_slope).astype(BF)
    d_query_mem, gw_mem = chain_sum(
        dot_t(d_read, w_in),
        4,
        [
            [(key_mem, d_key_hidden), (query_mem, d_read)],
            [(d_miss, key_act), (d_memory, read_low), (gw_out_early,)],
        ],
    )
    share_mem = lax.psum_scatter(gw_mem, "dp", scatter_dimension=0, tiled=True)
    d_n1_part = d_n1_part + in_own(dot(d_query_mem, wqm_t))
    d_n1_part, share_attn, output = together(d_n1_part.astype(BF), share_attn, output)
    last, gw_query_mem = chain_sum(
        jnp.concatenate([d_n1_part, d_persist_part.astype(BF)], axis=0), 5, [[(d_query_mem, n1_own)]]
    )
    d_n1 = last[:count].astype(F32)
    g_persist = last[count:]
    gg_attn = jnp.sum(d_n1 * x * r1, axis=0)
    d_x = d_after_attn + rms_back(x, r1, g_attn, d_n1)

    def cut(share, *widths):
        out, low = [], 0
        for part in widths:
            out.append(share[:, low : low + part].astype(F32))
            low += part
        return out

    s_down, s_gate, s_up = cut(share_ffn, *[w_gate.shape[1]] * 3)
    s_key_mem, s_value_mem, s_output, s_query, s_key, s_value = cut(share_attn, *[inner] * 6)
    s_in, s_out = cut(share_mem, hidden, hidden)
    grad_vectors = jnp.stack([gg_attn, gg_mem, gg_ffn, gg_rate], axis=1)
    rest = jnp.concatenate(
        [
            gw_query_mem,
            g_persist.T,
            grad_vectors.astype(BF),
            jnp.zeros((width, 128 - slots - 4), BF),
        ],
        axis=1,
    ).reshape(ranks, -1, width)
    turned = t_dot(deal_m, d_x.astype(BF)).astype(BF).reshape(ranks, -1, width)
    came = lax.all_to_all(
        jnp.concatenate([turned, rest], axis=1), "dp", split_axis=0, concat_axis=0, tiled=True
    )
    seats = count // ranks
    grad_tokens = t_dot(send_m, came[:, :seats].reshape(count, width)).astype(BF)
    share_rest = jnp.sum(came[:, seats:].astype(F32), axis=0).reshape(shard, -1)
    s_query_mem, s_small = cut(share_rest, inner, 128)
    s_vectors = s_small[:, slots : slots + 4].T

    return (
        output,
        grad_tokens,
        s_small[:, :slots].T,
        s_vectors[0],
        s_query_mem.T,
        s_in,
        s_out.T,
        s_query,
        s_key,
        s_value,
        s_output.T,
        s_vectors[1],
        s_key_mem.T,
        -s_value_mem.T,
        s_vectors[3],
        s_vectors[2],
        s_gate,
        s_up,
        s_down.T,
    )


def solution(mesh):
    rows = P("dp", None)
    vector = P("dp")
    across = P("tensor", "dp")
    along = P("dp", "tensor")
    return jax.shard_map(
        per_device,
        mesh=mesh,
        in_specs=(
            rows,
            rows,
            vector,
            vector,
            rows,
            P(None, "dp"),
            vector,
            across,
            along,
            across,
            along,
            along,
            along,
            across,
            vector,
            across,
            across,
            vector,
            vector,
            along,
            along,
            across,
        ),
        out_specs=(
            rows,
            rows,
            P(None, "dp"),
            vector,
            across,
            along,
            across,
            along,
            along,
            along,
            across,
            vector,
            across,
            across,
            vector,
            vector,
            along,
            along,
            across,
        ),
        check_vma=False,
    )
```

```python
import functools

import jax
import jax.numpy as jnp
from jax import lax
from jax.experimental import pallas as pl
from jax.experimental.pallas import tpu as pltpu
from jax.sharding import PartitionSpec as P

HD = 96
EPSILON = 1e-06
RATE_SCALE = 8e-05
NEG_LARGE = -1e30
BF = jnp.bfloat16
F32 = jnp.float32
MESH = pl.DeviceIdType.MESH
TILE = 128


def chain_sum_kernel(pieces, layout, x_ref, *refs):
    given = sum(len(widths) for _, parts in layout for widths in parts)
    fills, refs = refs[:given], refs[given:]
    o_ref, refs = refs[0], refs[1:]
    if layout:
        g_ref, refs = refs[0], refs[1:]
    from_outer, from_inner, part, sent_a, got_up, sent_b, got_across, got_total = refs[:8]
    me = lax.axis_index("tensor")
    step = x_ref.shape[0] // pieces
    low = me < 2
    outer = jnp.logical_or(me == 0, me == 3)
    inner = jnp.logical_not(outer)
    outer_peer = jnp.where(low, 0, 3)
    inner_peer = jnp.where(low, 2, 1)
    toward = jnp.where(low, 1, 2)
    barrier = pltpu.get_barrier_semaphore()

    def tell(peer):
        pl.semaphore_signal(barrier, inc=1, device_id={"tensor": peer}, device_id_type=MESH)

    def at(piece):
        return pl.ds(pl.multiple_of(piece * step, step), step)

    def send(src, dst, send_sem, recv_sem, peer):
        return pltpu.make_async_remote_copy(
            src_ref=src,
            dst_ref=dst,
            send_sem=send_sem,
            recv_sem=recv_sem,
            device_id={"tensor": peer},
            device_id_type=MESH,
        )

    def up(p):
        return send(x_ref.at[at(p)], from_outer.at[at(p)], sent_a.at[p], got_up.at[p], toward)

    def across(p):
        return send(part.at[at(p)], from_inner.at[at(p)], sent_b.at[p], got_across.at[p], inner_peer)

    def down(p):
        return send(o_ref.at[at(p)], o_ref.at[at(p)], sent_a.at[p], got_total.at[p], outer_peer)

    def put(tile):
        stage, put_sem = refs[8], refs[9]
        rows = pl.ds(pl.multiple_of(tile * TILE, TILE), TILE)
        slot = lax.rem(tile, 2)
        target = g_ref.at[rows, pl.ds(0, stage.shape[2])]
        return pltpu.make_async_copy(stage.at[slot], target, put_sem.at[slot])

    def fill(tile):
        stage = refs[8]
        columns = pl.ds(pl.multiple_of(tile * TILE, TILE), TILE)
        slot = lax.rem(tile, 2)

        @pl.when(tile >= 2)
        def _():
            put(tile - 2).wait()

        first, offset = 0, 0
        for width, parts in layout:
            for start in range(0, width, 512):
                span = min(512, width - start)
                total, index = None, first
                for part_sizes in parts:
                    if len(part_sizes) == 1:
                        term = fills[index][columns, start : start + span].astype(F32)
                    else:
                        term = lax.dot_general(
                            fills[index][:, columns],
                            fills[index + 1][:, start : start + span],
                            (((0,), (0,)), ((), ())),
                            preferred_element_type=F32,
                        )
                    total = term if total is None else total + term
                    index += len(part_sizes)
                stage[slot, :, offset + start : offset + start + span] = total.astype(BF)
            first, offset = index, offset + width
        put(tile).start()

    @pl.when(outer)
    def _():
        tell(toward)
        pl.semaphore_wait(barrier, 1)

        @pl.loop(0, pieces)
        def _(p):
            up(p).start()

    @pl.when(inner)
    def _():
        tell(outer_peer)
        tell(inner_peer)
        pl.semaphore_wait(barrier, 2)

    def first_add(p):
        up(p).wait_recv()
        part[at(p), :] = (
            x_ref[at(p), :].astype(F32) + from_outer[at(p), :].astype(F32)
        ).astype(part.dtype)
        across(p).start()

    def second_add(p):
        across(p).wait_recv()
        o_ref[at(p), :] = (
            part[at(p), :].astype(F32) + from_inner[at(p), :].astype(F32)
        ).astype(o_ref.dtype)
        down(p).start()

    tiles = g_ref.shape[0] // TILE if layout else 0

    per = 2 if layout else 1
    turns = pieces // per

    @pl.loop(0, max(turns + 1, tiles))
    def _(p):
        @pl.when(jnp.logical_and(inner, p < turns))
        def _():
            for k in range(per):
                first_add(p * per + k)

        @pl.when(jnp.logical_and(inner, jnp.logical_and(p >= 1, p <= turns)))
        def _():
            for k in range(per):
                second_add((p - 1) * per + k)

        if layout:

            @pl.when(p < tiles)
            def _():
                fill(p)

    if layout:
        put(tiles - 2).wait()
        put(tiles - 1).wait()

    @pl.when(outer)
    def _():
        @pl.loop(0, pieces)
        def _(p):
            down(p).wait_recv()
            up(p).wait_send()

    @pl.when(inner)
    def _():
        @pl.loop(0, pieces)
        def _(p):
            across(p).wait_send()
            down(p).wait_send()


def chain_sum(x, call_id=1, products=(), room=0):
    rows, cols = x.shape
    pieces = rows // 16
    dma = pltpu.SemaphoreType.DMA
    vmem = pl.BlockSpec(memory_space=pltpu.VMEM)
    layout = tuple(
        (pairs[0][1].shape[1], tuple((0,) * len(pair) for pair in pairs)) for pairs in products
    )
    fills = [array for pairs in products for pair in pairs for array in pair]
    out_shape = [jax.ShapeDtypeStruct((rows, cols), BF)]
    out_specs = [vmem]
    scratch = [pltpu.VMEM((rows, cols), BF)] * 3 + [dma((pieces,))] * 5
    if products:
        width, high = sum(w for w, _ in layout), products[0][0][0].shape[1]
        out_shape.append(jax.ShapeDtypeStruct((high, width + room), BF))
        out_specs.append(pl.BlockSpec(memory_space=pl.ANY))
        scratch += [pltpu.VMEM((2, TILE, width), BF), dma((2,))]
    out = pl.pallas_call(
        functools.partial(chain_sum_kernel, pieces, layout),
        out_shape=out_shape,
        in_specs=[vmem] * (1 + len(fills)),
        out_specs=out_specs,
        scratch_shapes=scratch,
        compiler_params=pltpu.CompilerParams(collective_id=call_id, has_side_effects=True),
        cost_estimate=pl.CostEstimate(flops=0, bytes_accessed=10**8, transcendentals=0),
        name="chain_sum",
    )(x.astype(BF), *fills)
    return out if products else out[0]


def dot(left, right):
    return lax.dot_general(left, right, (((1,), (0,)), ((), ())), preferred_element_type=F32)


def dot_t(left, right):
    return lax.dot_general(left, right, (((1,), (1,)), ((), ())), preferred_element_type=F32)


def t_dot(left, right):
    return lax.dot_general(left, right, (((0,), (0,)), ((), ())), preferred_element_type=F32)


def batch_dot(spec, left, right):
    return jnp.einsum(spec, left, right, preferred_element_type=F32)


def together(*values):
    return lax.optimization_barrier(values)


def rms(v):
    return lax.rsqrt(jnp.mean(v * v, axis=-1, keepdims=True) + EPSILON)


def rms_back(v, r, gain, grad):
    scaled = grad * gain
    inner = jnp.sum(scaled * v, axis=-1, keepdims=True)
    return r * scaled - v * (r * r * r) * (inner / v.shape[-1])


def silu_parts(z):
    s = jax.nn.sigmoid(z)
    return s, z * s, s * (1.0 + z * (1.0 - s))


def per_device(
    tokens,
    cotangent,
    dest,
    source,
    lengths,
    persist,
    gain_attn,
    w_query_mem,
    mem_in,
    mem_out,
    w_query,
    w_key,
    w_value,
    w_output,
    gain_mem,
    w_key_mem,
    w_value_mem,
    w_rate,
    gain_ffn,
    w_gate,
    w_up,
    w_down,
):
    count, width = tokens.shape
    shard = gain_attn.shape[0]
    ranks = width // shard
    batches, _ = lengths.shape
    rows = count // batches
    hidden = mem_in.shape[1]
    inner = w_query.shape[1]
    heads = inner // HD
    slots = persist.shape[0]
    me = lax.axis_index("tensor")

    def gather(*parts):
        packed = jnp.concatenate(parts, axis=1)
        whole = lax.all_gather(packed, "dp", axis=0, tiled=True)
        out, low = [], 0
        for part in parts:
            out.append(whole[:, low : low + part.shape[1]])
            low += part.shape[1]
        return out

    vectors = jnp.stack([gain_attn, gain_mem, gain_ffn, w_rate], axis=1)
    pad = jnp.zeros((shard, 128 - slots - 4), BF)
    small, wqm_t, wq, wk, wv, wo_t = gather(
        jnp.concatenate([persist.T, vectors, pad], axis=1),
        w_query_mem.T,
        w_query,
        w_key,
        w_value,
        w_output.T,
    )
    persistent = small[:, :slots].T
    gains = small[:, slots : slots + 4].astype(F32).T
    g_attn, g_mem, g_ffn, rate_w = (gains[i][None, :] for i in range(4))

    place = jnp.arange(count, dtype=jnp.int32)
    home = dest // count
    earlier = (home[None, :] == home[:, None]) & (place[None, :] < place[:, None])
    sent_at = home * (count // ranks) + jnp.sum(earlier.astype(jnp.int32), axis=1)
    came_at = jnp.sum((source[None, :] < source[:, None]).astype(jnp.int32), axis=1)
    send_m = (sent_at[None, :] == place[:, None]).astype(BF)
    deal_m = (came_at[:, None] == place[None, :]).astype(BF)

    def exchange(v):
        return lax.all_to_all(
            dot(send_m, v).astype(BF), "dp", split_axis=0, concat_axis=0, tiled=True
        )

    def give_back(v):
        back = lax.all_to_all(
            t_dot(deal_m, v.astype(BF)).astype(BF), "dp", split_axis=0, concat_axis=0, tiled=True
        )
        return t_dot(send_m, back).astype(BF)

    dealt = dot(deal_m, exchange(tokens)).astype(BF)
    dealt, later, late_in, late_mem_out = together(dealt, cotangent, mem_in, mem_out)
    w_in, w_out_t = gather(late_in, late_mem_out.T)
    cotangent_arrived = exchange(later)
    x = dealt.astype(F32)

    position = jnp.arange(rows, dtype=jnp.int32)
    bounds = jnp.cumsum(lengths, axis=1)
    segment = jnp.sum((position[None, :, None] >= bounds[:, None, :]).astype(jnp.int32), axis=2)
    causal = (segment[:, :, None] == segment[:, None, :]) & (
        position[None, None, :] <= position[None, :, None]
    )

    def split(v):
        return v.reshape(batches, rows, v.shape[-1])

    def join(v):
        return v.reshape(count, v.shape[-1])

    def own(v):
        return lax.dynamic_slice_in_dim(v, me * inner, inner, 1)

    def in_own(v):
        return lax.dynamic_update_slice_in_dim(
            jnp.zeros((v.shape[0], width), v.dtype), v, me * inner, 1
        )

    r1 = rms(x)
    n1 = (x * r1 * g_attn).astype(BF)
    n1_own = own(n1)
    query_mem = chain_sum(dot_t(n1_own, wqm_t))
    columns = jnp.concatenate([w_key_mem, w_value_mem], axis=1)
    query_mem, cotangent_arrived, columns = together(query_mem, cotangent_arrived, columns)
    tall = lax.all_gather(columns, "tensor", axis=0, tiled=True)
    d_out_low = dot(deal_m, cotangent_arrived).astype(BF)
    query = dot(n1, wq).astype(BF)
    key_p, value_p = dot(persistent, wk).astype(BF), dot(persistent, wv).astype(BF)
    key_x, value_x = dot(n1, wk).astype(BF), dot(n1, wv).astype(BF)
    w_in, query, key_p, value_p, key_x, value_x = together(w_in, query, key_p, value_p, key_x, value_x)
    read_s, read_act, read_slope = silu_parts(dot(query_mem, w_in))
    read_low = read_act.astype(BF)
    memory = chain_sum(dot_t(read_low, w_out_t))
    memory, tall = together(memory, tall)
    wkm_t, wvm_t = gather(tall[:, :shard].T, tall[:, shard:].T)

    key_m, value_m = dot(memory, wk).astype(BF), dot(memory, wv).astype(BF)

    def context(p, m, t):
        wide = jnp.broadcast_to(p[None], (batches,) + p.shape)
        all_rows = jnp.concatenate([wide, split(m), split(t)], axis=1)
        return all_rows.reshape(batches, -1, heads, HD)

    keys, values = context(key_p, key_m, key_x), context(value_p, value_m, value_x)
    allowed = jnp.concatenate(
        [jnp.ones((batches, rows, slots), dtype=bool), causal, causal], axis=2
    )[:, None]
    query4 = query.reshape(batches, rows, heads, HD)
    scores = batch_dot("bqhd,bkhd->bhqk", query4, keys) * HD ** (-0.5)
    weights = jax.nn.softmax(jnp.where(allowed, scores, NEG_LARGE), axis=-1)
    weights_low = weights.astype(BF)
    mixed = batch_dot("bhqk,bkhd->bqhd", weights_low, values).astype(BF).reshape(count, inner)
    mixed, late_gate, late_up, late_down = together(mixed, w_gate, w_up, w_down)
    wg, wu, wd_t = gather(late_gate, late_up, late_down.T)
    after_attn = x + chain_sum(dot_t(mixed, wo_t)).astype(F32)

    r2 = rms(after_attn)
    n2 = after_attn * r2 * g_mem
    rate_s = jax.nn.sigmoid(jnp.sum(n2 * rate_w, axis=1, keepdims=True))
    rate = RATE_SCALE * rate_s
    n2_low = n2.astype(BF)
    n2_own = own(n2_low)
    key_mem = dot_t(n2_low, wkm_t).astype(BF)
    value_part = dot_t(n2_own, own(wvm_t))
    key_hidden = dot(key_mem, w_in)
    key_s, key_silu, key_slope = silu_parts(key_hidden)
    key_act = key_silu.astype(BF)
    miss = chain_sum(dot_t(key_act, w_out_t) - value_part).astype(F32)
    error = (rate * miss).astype(BF)
    back_pre = dot(error, w_out_t)
    back_hidden = (back_pre * key_slope).astype(BF)
    gram = jnp.where(causal, batch_dot("bik,bjk->bij", split(key_mem), split(key_mem)), 0.0).astype(BF)
    new_hidden = key_hidden - join(batch_dot("bij,bjk->bik", gram, split(back_hidden)))
    _, new_silu, new_slope = silu_parts(new_hidden)
    new_act = new_silu.astype(BF)
    pair = jnp.where(causal, batch_dot("bik,bjk->bij", split(new_act), split(key_act)), 0.0).astype(BF)
    update = dot_t(new_act, w_out_t) - join(batch_dot("bij,bjk->bik", pair, split(error)))
    after_mem = after_attn + chain_sum(update).astype(F32)

    r3 = rms(after_mem)
    n3 = (after_mem * r3 * g_ffn).astype(BF)
    gate, up = dot(n3, wg), dot(n3, wu)
    _, gate_silu, gate_slope = silu_parts(gate)
    ffn_act = (gate_silu * up).astype(BF)
    ffn_own = lax.psum_scatter(
        dot_t(ffn_act, wd_t).astype(BF), "tensor", scatter_dimension=1, tiled=True
    )

    d_ffn = dot(d_out_low, wd_t)
    d_gate = (d_ffn * up * gate_slope).astype(BF)
    d_up = (d_ffn * gate_silu).astype(BF)
    d_n3, gw_ffn = chain_sum(
        dot_t(d_gate, wg) + dot_t(d_up, wu),
        2,
        [[(d_out_low, ffn_act)], [(n3, d_gate)], [(n3, d_up)]],
    )
    d_n3 = d_n3.astype(F32)
    gg_ffn = jnp.sum(d_n3 * after_mem * r3, axis=0)
    d_after_mem = d_out_low.astype(F32) + rms_back(after_mem, r3, g_ffn, d_n3)
    d_update = d_after_mem.astype(BF)

    d_pair = jnp.where(
        causal, -batch_dot("bik,bjk->bij", split(d_update), split(error)), 0.0
    ).astype(BF)
    d_new_act = dot(d_update, w_out_t) + join(batch_dot("bij,bjk->bik", d_pair, split(key_act)))
    d_key_act = join(batch_dot("bij,bik->bjk", d_pair, split(new_act)))
    d_new_hidden = (d_new_act * new_slope).astype(BF)
    d_gram = jnp.where(
        causal, -batch_dot("bik,bjk->bij", split(d_new_hidden), split(back_hidden)), 0.0
    ).astype(BF)
    d_back = (-join(batch_dot("bij,bik->bjk", gram, split(d_new_hidden)))).astype(BF).astype(F32)
    d_back_pre = (d_back * key_slope).astype(BF)
    slope_grad = key_s * (1.0 - key_s) * (2.0 + key_hidden * (1.0 - 2.0 * key_s))
    d_hidden_part = d_new_hidden.astype(F32) + d_back * back_pre * slope_grad
    d_error_part = dot_t(d_back_pre, w_out_t) - join(
        batch_dot("bij,bik->bjk", pair, split(d_update))
    )
    share_ffn = lax.psum_scatter(gw_ffn, "dp", scatter_dimension=0, tiled=True)
    d_error = chain_sum(d_error_part).astype(F32)
    d_rate = jnp.sum(d_error * miss, axis=1, keepdims=True)
    d_miss = (rate * d_error).astype(BF)
    d_key_act = d_key_act + dot(d_miss, w_out_t)
    d_key_hidden = (d_hidden_part + d_key_act * key_slope).astype(BF)
    d_key_part = dot_t(d_key_hidden, w_in) + join(
        batch_dot("bij,bjk->bik", d_gram, split(key_mem))
        + batch_dot("bij,bik->bjk", d_gram, split(key_mem))
    )
    d_key_part, ffn_own = together(d_key_part.astype(BF), ffn_own)
    result_own = give_back(own(after_mem) + ffn_own.astype(F32))
    d_key, gw_out_early = chain_sum(
        d_key_part, 6, [[(d_update, new_act), (error, d_back_pre)]]
    )
    d_n2 = dot(d_key, wkm_t) - dot(d_miss, wvm_t)
    d_logit = d_rate * rate * (1.0 - rate_s)
    gg_rate = jnp.sum(n2 * d_logit, axis=0)
    d_n2 = d_n2 + d_logit * rate_w
    gg_mem = jnp.sum(d_n2 * after_attn * r2, axis=0)
    d_after_attn = d_after_mem + rms_back(after_attn, r2, g_mem, d_n2)
    d_attn = d_after_attn.astype(BF)

    d_mixed = dot(d_attn, wo_t).astype(BF)
    d_mixed4 = d_mixed.reshape(batches, rows, heads, HD)
    d_weights = batch_dot("bqhd,bkhd->bhqk", d_mixed4, values)
    d_values = batch_dot("bhqk,bqhd->bkhd", weights_low, d_mixed4)
    d_scores = (
        weights * (d_weights - jnp.sum(weights * d_weights, axis=-1, keepdims=True))
    ).astype(BF)
    d_query = batch_dot("bhqk,bkhd->bqhd", d_scores, keys) * HD ** (-0.5)
    d_keys = batch_dot("bhqk,bqhd->bkhd", d_scores, query4) * HD ** (-0.5)
    d_query = d_query.astype(BF).reshape(count, inner)

    def apart(v):
        v = v.reshape(batches, -1, inner)
        return (
            jnp.sum(v[:, :slots], axis=0).astype(BF),
            join(v[:, slots : slots + rows]).astype(BF),
            join(v[:, slots + rows :]).astype(BF),
        )

    dk_p, dk_m, dk_x = apart(d_keys)
    dv_p, dv_m, dv_x = apart(d_values)
    d_memory_part, share_ffn, result_own = together(
        (dot_t(dk_m, wk) + dot_t(dv_m, wv)).astype(BF), share_ffn, result_own
    )
    output = lax.all_gather(result_own, "tensor", axis=1, tiled=True)
    d_memory, gw_attn = chain_sum(
        d_memory_part,
        3,
        [
            [(d_key, n2_own)],
            [(d_miss, n2_own)],
            [(d_attn, mixed)],
            [(n1, d_query)],
            [(persistent, dk_p), (memory, dk_m), (n1, dk_x)],
            [(persistent, dv_p), (memory, dv_m), (n1, dv_x)],
        ],
    )
    d_n1_part = dot_t(d_query, wq) + dot_t(dk_x, wk) + dot_t(dv_x, wv)
    d_persist_part = dot_t(dk_p, wk) + dot_t(dv_p, wv)

    share_attn = lax.psum_scatter(gw_attn, "dp", scatter_dimension=0, tiled=True)
    d_read = (dot(d_memory, w_out_t) * read_slope).astype(BF)
    d_query_mem, gw_mem = chain_sum(
        dot_t(d_read, w_in),
        4,
        [
            [(key_mem, d_key_hidden), (query_mem, d_read)],
            [(d_miss, key_act), (d_memory, read_low), (gw_out_early,)],
        ],
        inner,
    )
    gw_query_mem = t_dot(d_query_mem, n1_own).astype(BF)
    gw_mem = lax.dynamic_update_slice(gw_mem, gw_query_mem, (0, 2 * hidden))
    share_mem = lax.psum_scatter(gw_mem, "dp", scatter_dimension=0, tiled=True)
    d_n1_part = d_n1_part + in_own(dot(d_query_mem, wqm_t))
    d_n1_part, share_attn, output = together(d_n1_part.astype(BF), share_attn, output)
    last = chain_sum(jnp.concatenate([d_n1_part, d_persist_part.astype(BF)], axis=0), 5)
    d_n1 = last[:count].astype(F32)
    g_persist = last[count:]
    gg_attn = jnp.sum(d_n1 * x * r1, axis=0)
    d_x = d_after_attn + rms_back(x, r1, g_attn, d_n1)

    def cut(share, *widths):
        out, low = [], 0
        for part in widths:
            out.append(share[:, low : low + part].astype(F32))
            low += part
        return out

    s_down, s_gate, s_up = cut(share_ffn, *[w_gate.shape[1]] * 3)
    s_key_mem, s_value_mem, s_output, s_query, s_key, s_value = cut(share_attn, *[inner] * 6)
    s_in, s_out, s_query_mem = cut(share_mem, hidden, hidden, inner)
    grad_vectors = jnp.stack([gg_attn, gg_mem, gg_ffn, gg_rate], axis=1)
    rest = jnp.concatenate(
        [
            g_persist.T,
            grad_vectors.astype(BF),
            jnp.zeros((width, 128 - slots - 4), BF),
        ],
        axis=1,
    ).reshape(ranks, -1, width)
    turned = t_dot(deal_m, d_x.astype(BF)).astype(BF).reshape(ranks, -1, width)
    came = lax.all_to_all(
        jnp.concatenate([turned, rest], axis=1), "dp", split_axis=0, concat_axis=0, tiled=True
    )
    seats = count // ranks
    grad_tokens = t_dot(send_m, came[:, :seats].reshape(count, width)).astype(BF)
    share_rest = jnp.sum(came[:, seats:].astype(F32), axis=0).reshape(shard, -1)
    s_small = share_rest
    s_vectors = s_small[:, slots : slots + 4].T

    return (
        output,
        grad_tokens,
        s_small[:, :slots].T,
        s_vectors[0],
        s_query_mem.T,
        s_in,
        s_out.T,
        s_query,
        s_key,
        s_value,
        s_output.T,
        s_vectors[1],
        s_key_mem.T,
        -s_value_mem.T,
        s_vectors[3],
        s_vectors[2],
        s_gate,
        s_up,
        s_down.T,
    )


def solution(mesh):
    rows = P("dp", None)
    vector = P("dp")
    across = P("tensor", "dp")
    along = P("dp", "tensor")
    return jax.shard_map(
        per_device,
        mesh=mesh,
        in_specs=(
            rows,
            rows,
            vector,
            vector,
            rows,
            P(None, "dp"),
            vector,
            across,
            along,
            across,
            along,
            along,
            along,
            across,
            vector,
            across,
            across,
            vector,
            vector,
            along,
            along,
            across,
        ),
        out_specs=(
            rows,
            rows,
            P(None, "dp"),
            vector,
            across,
            along,
            across,
            along,
            along,
            along,
            across,
            vector,
            across,
            across,
            vector,
            vector,
            along,
            along,
            across,
        ),
        check_vma=False,
    )
```

```python
import functools

import jax
import jax.numpy as jnp
from jax import lax
from jax.experimental import pallas as pl
from jax.experimental.pallas import tpu as pltpu
from jax.sharding import PartitionSpec as P

HD = 96
EPSILON = 1e-06
RATE_SCALE = 8e-05
NEG_LARGE = -1e30
BF = jnp.bfloat16
F32 = jnp.float32
MESH = pl.DeviceIdType.MESH
TILE = 128


def chain_sum_kernel(pieces, layout, x_ref, *refs):
    given = sum(len(widths) for _, parts in layout for widths in parts)
    fills, refs = refs[:given], refs[given:]
    o_ref, refs = refs[0], refs[1:]
    if layout:
        g_ref, refs = refs[0], refs[1:]
    from_outer, from_inner, part, sent_a, got_up, sent_b, got_across, got_total = refs[:8]
    me = lax.axis_index("tensor")
    step = x_ref.shape[0] // pieces
    low = me < 2
    outer = jnp.logical_or(me == 0, me == 3)
    inner = jnp.logical_not(outer)
    outer_peer = jnp.where(low, 0, 3)
    inner_peer = jnp.where(low, 2, 1)
    toward = jnp.where(low, 1, 2)
    barrier = pltpu.get_barrier_semaphore()

    def tell(peer):
        pl.semaphore_signal(barrier, inc=1, device_id={"tensor": peer}, device_id_type=MESH)

    def at(piece):
        return pl.ds(pl.multiple_of(piece * step, step), step)

    def send(src, dst, send_sem, recv_sem, peer):
        return pltpu.make_async_remote_copy(
            src_ref=src,
            dst_ref=dst,
            send_sem=send_sem,
            recv_sem=recv_sem,
            device_id={"tensor": peer},
            device_id_type=MESH,
        )

    def up(p):
        return send(x_ref.at[at(p)], from_outer.at[at(p)], sent_a.at[p], got_up.at[p], toward)

    def across(p):
        return send(part.at[at(p)], from_inner.at[at(p)], sent_b.at[p], got_across.at[p], inner_peer)

    def down(p):
        return send(o_ref.at[at(p)], o_ref.at[at(p)], sent_a.at[p], got_total.at[p], outer_peer)

    def put(tile):
        stage, put_sem = refs[8], refs[9]
        rows = pl.ds(pl.multiple_of(tile * TILE, TILE), TILE)
        slot = lax.rem(tile, 2)
        target = g_ref.at[rows, pl.ds(0, stage.shape[2])]
        return pltpu.make_async_copy(stage.at[slot], target, put_sem.at[slot])

    def fill(tile):
        stage = refs[8]
        columns = pl.ds(pl.multiple_of(tile * TILE, TILE), TILE)
        slot = lax.rem(tile, 2)

        @pl.when(tile >= 2)
        def _():
            put(tile - 2).wait()

        first, offset = 0, 0
        for width, parts in layout:
            for start in range(0, width, 512):
                span = min(512, width - start)
                total, index = None, first
                for part_sizes in parts:
                    if len(part_sizes) == 1:
                        term = fills[index][columns, start : start + span].astype(F32)
                    else:
                        term = lax.dot_general(
                            fills[index][:, columns],
                            fills[index + 1][:, start : start + span],
                            (((0,), (0,)), ((), ())),
                            preferred_element_type=F32,
                        )
                    total = term if total is None else total + term
                    index += len(part_sizes)
                stage[slot, :, offset + start : offset + start + span] = total.astype(BF)
            first, offset = index, offset + width
        put(tile).start()

    @pl.when(outer)
    def _():
        tell(toward)
        pl.semaphore_wait(barrier, 1)

        @pl.loop(0, pieces)
        def _(p):
            up(p).start()

    @pl.when(inner)
    def _():
        tell(outer_peer)
        tell(inner_peer)
        pl.semaphore_wait(barrier, 2)

    def first_add(p):
        up(p).wait_recv()
        part[at(p), :] = (
            x_ref[at(p), :].astype(F32) + from_outer[at(p), :].astype(F32)
        ).astype(part.dtype)
        across(p).start()

    def second_add(p):
        across(p).wait_recv()
        o_ref[at(p), :] = (
            part[at(p), :].astype(F32) + from_inner[at(p), :].astype(F32)
        ).astype(o_ref.dtype)
        down(p).start()

    tiles = g_ref.shape[0] // TILE if layout else 0

    per, lag = (2, 2) if layout else (1, 3)
    turns = pieces // per

    @pl.loop(0, max(turns + lag, tiles))
    def _(p):
        @pl.when(jnp.logical_and(inner, p < turns))
        def _():
            for k in range(per):
                first_add(p * per + k)

        @pl.when(jnp.logical_and(inner, jnp.logical_and(p >= lag, p < turns + lag)))
        def _():
            for k in range(per):
                second_add((p - lag) * per + k)

        if layout:

            @pl.when(p < tiles)
            def _():
                fill(p)

    if layout:
        put(tiles - 2).wait()
        put(tiles - 1).wait()

    @pl.when(outer)
    def _():
        @pl.loop(0, pieces)
        def _(p):
            down(p).wait_recv()
            up(p).wait_send()

    @pl.when(inner)
    def _():
        @pl.loop(0, pieces)
        def _(p):
            across(p).wait_send()
            down(p).wait_send()


def chain_sum(x, call_id=1, products=(), room=0):
    rows, cols = x.shape
    pieces = rows // 16
    dma = pltpu.SemaphoreType.DMA
    vmem = pl.BlockSpec(memory_space=pltpu.VMEM)
    layout = tuple(
        (pairs[0][1].shape[1], tuple((0,) * len(pair) for pair in pairs)) for pairs in products
    )
    fills = [array for pairs in products for pair in pairs for array in pair]
    out_shape = [jax.ShapeDtypeStruct((rows, cols), BF)]
    out_specs = [vmem]
    scratch = [pltpu.VMEM((rows, cols), BF)] * 3 + [dma((pieces,))] * 5
    if products:
        width, high = sum(w for w, _ in layout), products[0][0][0].shape[1]
        out_shape.append(jax.ShapeDtypeStruct((high, width + room), BF))
        out_specs.append(pl.BlockSpec(memory_space=pl.ANY))
        scratch += [pltpu.VMEM((2, TILE, width), BF), dma((2,))]
    out = pl.pallas_call(
        functools.partial(chain_sum_kernel, pieces, layout),
        out_shape=out_shape,
        in_specs=[vmem] * (1 + len(fills)),
        out_specs=out_specs,
        scratch_shapes=scratch,
        compiler_params=pltpu.CompilerParams(collective_id=call_id, has_side_effects=True),
        cost_estimate=pl.CostEstimate(flops=0, bytes_accessed=10**8, transcendentals=0),
        name="chain_sum",
    )(x.astype(BF), *fills)
    return out if products else out[0]


def line_gather_kernel(pieces, x_ref, o_ref, sent, got, keep):
    me = lax.axis_index("tensor")
    high = x_ref.shape[0]
    step = high // pieces
    last = 3
    barrier = pltpu.get_barrier_semaphore()
    ways = ((0, me < last, 1), (1, me > 0, -1))

    for _, open_, move in ways:

        @pl.when(open_)
        def _():
            pl.semaphore_signal(
                barrier, inc=1, device_id={"tensor": me + move}, device_id_type=MESH
            )

    at_end = jnp.logical_or(me == 0, me == last)

    @pl.when(at_end)
    def _():
        pl.semaphore_wait(barrier, 1)

    @pl.when(jnp.logical_not(at_end))
    def _():
        pl.semaphore_wait(barrier, 2)

    def copy(way, hop, piece, move, block, first=False):
        rows = pl.ds(pl.multiple_of(block * high + piece * step, step), step)
        return pltpu.make_async_remote_copy(
            src_ref=x_ref.at[pl.ds(piece * step, step)] if first else o_ref.at[rows],
            dst_ref=o_ref.at[rows],
            send_sem=sent.at[way, hop, piece],
            recv_sem=got.at[way, hop, piece],
            device_id={"tensor": jnp.clip(me + move, 0, last)},
            device_id_type=MESH,
        )

    def forward(way, move, hop):
        block = me - move * hop
        return jnp.logical_and(
            jnp.logical_and(me + move >= 0, me + move <= last),
            jnp.logical_and(block >= 0, block <= last),
        )

    def comes(way, move, hop):
        block = me - move * (hop + 1)
        return jnp.logical_and(block >= 0, block <= last)

    def own():
        rows = pl.ds(pl.multiple_of(me * high, high), high)
        return pltpu.make_async_copy(x_ref, o_ref.at[rows], keep.at[0])

    for hop in range(last):
        for piece in range(pieces):
            for way, _, move in ways:

                @pl.when(forward(way, move, hop))
                def _():
                    copy(way, hop, piece, move, me - move * hop, hop == 0).start()

        if hop == 0:
            own().start()
        for piece in range(pieces):
            for way, _, move in ways:

                @pl.when(comes(way, move, hop))
                def _():
                    copy(way, hop, piece, move, me - move * (hop + 1)).wait_recv()

    own().wait()
    for hop in range(last):
        for piece in range(pieces):
            for way, _, move in ways:

                @pl.when(forward(way, move, hop))
                def _():
                    copy(way, hop, piece, move, me - move * hop, hop == 0).wait_send()


def line_gather(x, call_id, pieces=2):
    rows, cols = x.shape
    dma = pltpu.SemaphoreType.DMA
    vmem = pl.BlockSpec(memory_space=pltpu.VMEM)
    return pl.pallas_call(
        functools.partial(line_gather_kernel, pieces),
        out_shape=jax.ShapeDtypeStruct((4 * rows, cols), BF),
        in_specs=[vmem],
        out_specs=vmem,
        scratch_shapes=[dma((2, 3, pieces)), dma((2, 3, pieces)), dma((1,))],
        compiler_params=pltpu.CompilerParams(collective_id=call_id, has_side_effects=True),
        cost_estimate=pl.CostEstimate(flops=0, bytes_accessed=5 * 10**7, transcendentals=0),
        name="line_gather",
    )(x)


def dot(left, right):
    return lax.dot_general(left, right, (((1,), (0,)), ((), ())), preferred_element_type=F32)


def dot_t(left, right):
    return lax.dot_general(left, right, (((1,), (1,)), ((), ())), preferred_element_type=F32)


def t_dot(left, right):
    return lax.dot_general(left, right, (((0,), (0,)), ((), ())), preferred_element_type=F32)


def batch_dot(spec, left, right):
    return jnp.einsum(spec, left, right, preferred_element_type=F32)


def cut_apart(whole, *widths):
    out, low = [], 0
    for width in widths:
        out.append(whole[:, low : low + width])
        low += width
    return out


def together(*values):
    return lax.optimization_barrier(values)


def rms(v):
    return lax.rsqrt(jnp.mean(v * v, axis=-1, keepdims=True) + EPSILON)


def rms_back(v, r, gain, grad):
    scaled = grad * gain
    inner = jnp.sum(scaled * v, axis=-1, keepdims=True)
    return r * scaled - v * (r * r * r) * (inner / v.shape[-1])


def silu_parts(z):
    s = jax.nn.sigmoid(z)
    return s, z * s, s * (1.0 + z * (1.0 - s))


def per_device(
    tokens,
    cotangent,
    dest,
    source,
    lengths,
    persist,
    gain_attn,
    w_query_mem,
    mem_in,
    mem_out,
    w_query,
    w_key,
    w_value,
    w_output,
    gain_mem,
    w_key_mem,
    w_value_mem,
    w_rate,
    gain_ffn,
    w_gate,
    w_up,
    w_down,
):
    count, width = tokens.shape
    shard = gain_attn.shape[0]
    ranks = width // shard
    batches, _ = lengths.shape
    rows = count // batches
    hidden = mem_in.shape[1]
    inner = w_query.shape[1]
    heads = inner // HD
    slots = persist.shape[0]
    me = lax.axis_index("tensor")

    def gather_whole(*parts):
        return lax.all_gather(jnp.concatenate(parts, axis=1), "dp", axis=0, tiled=True)

    def gather(*parts):
        return cut_apart(gather_whole(*parts), *[part.shape[1] for part in parts])

    vectors = jnp.stack([gain_attn, gain_mem, gain_ffn, w_rate], axis=1)
    pad = jnp.zeros((shard, 128 - slots - 4), BF)
    small, wqm_t = gather(jnp.concatenate([persist.T, vectors, pad], axis=1), w_query_mem.T)
    tall = line_gather(jnp.concatenate([w_key_mem, w_value_mem], axis=1), 7)
    persistent = small[:, :slots].T
    gains = small[:, slots : slots + 4].astype(F32).T
    g_attn, g_mem, g_ffn, rate_w = (gains[i][None, :] for i in range(4))

    place = jnp.arange(count, dtype=jnp.int32)
    home = dest // count
    earlier = (home[None, :] == home[:, None]) & (place[None, :] < place[:, None])
    sent_at = home * (count // ranks) + jnp.sum(earlier.astype(jnp.int32), axis=1)
    came_at = jnp.sum((source[None, :] < source[:, None]).astype(jnp.int32), axis=1)
    send_m = (sent_at[None, :] == place[:, None]).astype(BF)
    deal_m = (came_at[:, None] == place[None, :]).astype(BF)

    def exchange(v):
        return lax.all_to_all(
            dot(send_m, v).astype(BF), "dp", split_axis=0, concat_axis=0, tiled=True
        )

    def give_back(v):
        back = lax.all_to_all(
            t_dot(deal_m, v.astype(BF)).astype(BF), "dp", split_axis=0, concat_axis=0, tiled=True
        )
        return t_dot(send_m, back).astype(BF)

    arrived, tall = together(exchange(tokens), tall)
    dealt, later, late_in, late_mem_out = together(
        dot(deal_m, arrived).astype(BF), cotangent, mem_in, mem_out
    )
    w_in, w_out_t = gather(late_in, late_mem_out.T)
    cotangent_arrived = exchange(later)
    x = dealt.astype(F32)

    position = jnp.arange(rows, dtype=jnp.int32)
    bounds = jnp.cumsum(lengths, axis=1)
    segment = jnp.sum((position[None, :, None] >= bounds[:, None, :]).astype(jnp.int32), axis=2)
    causal = (segment[:, :, None] == segment[:, None, :]) & (
        position[None, None, :] <= position[None, :, None]
    )

    def split(v):
        return v.reshape(batches, rows, v.shape[-1])

    def join(v):
        return v.reshape(count, v.shape[-1])

    def own(v):
        return lax.dynamic_slice_in_dim(v, me * inner, inner, 1)

    def in_own(v):
        return lax.dynamic_update_slice_in_dim(
            jnp.zeros((v.shape[0], width), v.dtype), v, me * inner, 1
        )

    r1 = rms(x)
    n1 = (x * r1 * g_attn).astype(BF)
    n1_own = own(n1)
    query_mem = chain_sum(dot_t(n1_own, wqm_t))
    query_mem, cotangent_arrived, late_query, late_key, late_value, late_output = together(
        query_mem, cotangent_arrived, w_query, w_key, w_value, w_output
    )
    w_attn = gather_whole(late_query, late_key, late_value, late_output.T)
    d_out_low = dot(deal_m, cotangent_arrived).astype(BF)
    read_s, read_act, read_slope = silu_parts(dot(query_mem, w_in))
    read_low, tall = together(read_act.astype(BF), tall)
    wkm_t, wvm_t = gather(tall[:, :shard].T, tall[:, shard:].T)
    memory = chain_sum(dot_t(read_low, w_out_t))
    memory, w_attn = together(memory, w_attn)
    wq, wk, wv, wo_t = cut_apart(w_attn, inner, inner, inner, inner)
    query = dot(n1, wq).astype(BF)
    key_p, value_p = dot(persistent, wk).astype(BF), dot(persistent, wv).astype(BF)
    key_x, value_x = dot(n1, wk).astype(BF), dot(n1, wv).astype(BF)

    key_m, value_m = dot(memory, wk).astype(BF), dot(memory, wv).astype(BF)

    def context(p, m, t):
        wide = jnp.broadcast_to(p[None], (batches,) + p.shape)
        all_rows = jnp.concatenate([wide, split(m), split(t)], axis=1)
        return all_rows.reshape(batches, -1, heads, HD)

    keys, values = context(key_p, key_m, key_x), context(value_p, value_m, value_x)
    allowed = jnp.concatenate(
        [jnp.ones((batches, rows, slots), dtype=bool), causal, causal], axis=2
    )[:, None]
    query4 = query.reshape(batches, rows, heads, HD)
    scores = batch_dot("bqhd,bkhd->bhqk", query4, keys) * HD ** (-0.5)
    weights = jax.nn.softmax(jnp.where(allowed, scores, NEG_LARGE), axis=-1)
    weights_low = weights.astype(BF)
    mixed = batch_dot("bhqk,bkhd->bqhd", weights_low, values).astype(BF).reshape(count, inner)
    mixed, late_gate, late_up, late_down = together(mixed, w_gate, w_up, w_down)
    wg, wu, wd_t = gather(late_gate, late_up, late_down.T)
    after_attn = x + chain_sum(dot_t(mixed, wo_t)).astype(F32)

    r2 = rms(after_attn)
    n2 = after_attn * r2 * g_mem
    rate_s = jax.nn.sigmoid(jnp.sum(n2 * rate_w, axis=1, keepdims=True))
    rate = RATE_SCALE * rate_s
    n2_low = n2.astype(BF)
    n2_own = own(n2_low)
    key_mem = dot_t(n2_low, wkm_t).astype(BF)
    value_part = dot_t(n2_own, own(wvm_t))
    key_hidden = dot(key_mem, w_in)
    key_s, key_silu, key_slope = silu_parts(key_hidden)
    key_act = key_silu.astype(BF)
    miss = chain_sum(dot_t(key_act, w_out_t) - value_part).astype(F32)
    error = (rate * miss).astype(BF)
    back_pre = dot(error, w_out_t)
    back_hidden = (back_pre * key_slope).astype(BF)
    gram = jnp.where(causal, batch_dot("bik,bjk->bij", split(key_mem), split(key_mem)), 0.0).astype(BF)
    new_hidden = key_hidden - join(batch_dot("bij,bjk->bik", gram, split(back_hidden)))
    _, new_silu, new_slope = silu_parts(new_hidden)
    new_act = new_silu.astype(BF)
    pair = jnp.where(causal, batch_dot("bik,bjk->bij", split(new_act), split(key_act)), 0.0).astype(BF)
    update = dot_t(new_act, w_out_t) - join(batch_dot("bij,bjk->bik", pair, split(error)))
    after_mem = after_attn + chain_sum(update).astype(F32)

    r3 = rms(after_mem)
    n3 = (after_mem * r3 * g_ffn).astype(BF)
    gate, up = dot(n3, wg), dot(n3, wu)
    _, gate_silu, gate_slope = silu_parts(gate)
    ffn_act = (gate_silu * up).astype(BF)
    ffn_own = lax.psum_scatter(
        dot_t(ffn_act, wd_t).astype(BF), "tensor", scatter_dimension=1, tiled=True
    )

    d_ffn = dot(d_out_low, wd_t)
    d_gate = (d_ffn * up * gate_slope).astype(BF)
    d_up = (d_ffn * gate_silu).astype(BF)
    d_n3, gw_ffn = chain_sum(
        dot_t(d_gate, wg) + dot_t(d_up, wu),
        2,
        [[(d_out_low, ffn_act)], [(n3, d_gate)], [(n3, d_up)]],
    )
    d_n3 = d_n3.astype(F32)
    gg_ffn = jnp.sum(d_n3 * after_mem * r3, axis=0)
    d_after_mem = d_out_low.astype(F32) + rms_back(after_mem, r3, g_ffn, d_n3)
    d_update = d_after_mem.astype(BF)

    d_pair = jnp.where(
        causal, -batch_dot("bik,bjk->bij", split(d_update), split(error)), 0.0
    ).astype(BF)
    d_new_act = dot(d_update, w_out_t) + join(batch_dot("bij,bjk->bik", d_pair, split(key_act)))
    d_key_act = join(batch_dot("bij,bik->bjk", d_pair, split(new_act)))
    d_new_hidden = (d_new_act * new_slope).astype(BF)
    d_gram = jnp.where(
        causal, -batch_dot("bik,bjk->bij", split(d_new_hidden), split(back_hidden)), 0.0
    ).astype(BF)
    d_back = (-join(batch_dot("bij,bik->bjk", gram, split(d_new_hidden)))).astype(BF).astype(F32)
    d_back_pre = (d_back * key_slope).astype(BF)
    slope_grad = key_s * (1.0 - key_s) * (2.0 + key_hidden * (1.0 - 2.0 * key_s))
    d_hidden_part = d_new_hidden.astype(F32) + d_back * back_pre * slope_grad
    d_error_part = dot_t(d_back_pre, w_out_t) - join(
        batch_dot("bij,bik->bjk", pair, split(d_update))
    )
    share_ffn = lax.psum_scatter(gw_ffn, "dp", scatter_dimension=0, tiled=True)
    d_error = chain_sum(d_error_part).astype(F32)
    d_rate = jnp.sum(d_error * miss, axis=1, keepdims=True)
    d_miss = (rate * d_error).astype(BF)
    d_key_act = d_key_act + dot(d_miss, w_out_t)
    d_key_hidden = (d_hidden_part + d_key_act * key_slope).astype(BF)
    d_key_part = dot_t(d_key_hidden, w_in) + join(
        batch_dot("bij,bjk->bik", d_gram, split(key_mem))
        + batch_dot("bij,bik->bjk", d_gram, split(key_mem))
    )
    d_key_part, ffn_own = together(d_key_part.astype(BF), ffn_own)
    result_own = give_back(own(after_mem) + ffn_own.astype(F32))
    d_key, gw_out_early = chain_sum(
        d_key_part, 6, [[(d_update, new_act), (error, d_back_pre)]]
    )
    d_n2 = dot(d_key, wkm_t) - dot(d_miss, wvm_t)
    d_logit = d_rate * rate * (1.0 - rate_s)
    gg_rate = jnp.sum(n2 * d_logit, axis=0)
    d_n2 = d_n2 + d_logit * rate_w
    gg_mem = jnp.sum(d_n2 * after_attn * r2, axis=0)
    d_after_attn = d_after_mem + rms_back(after_attn, r2, g_mem, d_n2)
    d_attn = d_after_attn.astype(BF)

    d_mixed = dot(d_attn, wo_t).astype(BF)
    d_mixed4 = d_mixed.reshape(batches, rows, heads, HD)
    d_weights = batch_dot("bqhd,bkhd->bhqk", d_mixed4, values)
    d_values = batch_dot("bhqk,bqhd->bkhd", weights_low, d_mixed4)
    d_scores = (
        weights * (d_weights - jnp.sum(weights * d_weights, axis=-1, keepdims=True))
    ).astype(BF)
    d_query = batch_dot("bhqk,bkhd->bqhd", d_scores, keys) * HD ** (-0.5)
    d_keys = batch_dot("bhqk,bqhd->bkhd", d_scores, query4) * HD ** (-0.5)
    d_query = d_query.astype(BF).reshape(count, inner)

    def apart(v):
        v = v.reshape(batches, -1, inner)
        return (
            jnp.sum(v[:, :slots], axis=0).astype(BF),
            join(v[:, slots : slots + rows]).astype(BF),
            join(v[:, slots + rows :]).astype(BF),
        )

    dk_p, dk_m, dk_x = apart(d_keys)
    dv_p, dv_m, dv_x = apart(d_values)
    d_memory_part, share_ffn, result_own = together(
        (dot_t(dk_m, wk) + dot_t(dv_m, wv)).astype(BF), share_ffn, result_own
    )
    output = lax.all_gather(result_own, "tensor", axis=1, tiled=True)
    d_memory, gw_attn = chain_sum(
        d_memory_part,
        3,
        [
            [(d_key, n2_own)],
            [(d_miss, n2_own)],
            [(d_attn, mixed)],
            [(n1, d_query)],
            [(persistent, dk_p), (memory, dk_m), (n1, dk_x)],
            [(persistent, dv_p), (memory, dv_m), (n1, dv_x)],
        ],
    )
    d_n1_part = dot_t(d_query, wq) + dot_t(dk_x, wk) + dot_t(dv_x, wv)
    d_persist_part = dot_t(dk_p, wk) + dot_t(dv_p, wv)

    share_attn = lax.psum_scatter(gw_attn, "dp", scatter_dimension=0, tiled=True)
    d_read = (dot(d_memory, w_out_t) * read_slope).astype(BF)
    d_query_mem, gw_mem = chain_sum(
        dot_t(d_read, w_in),
        4,
        [
            [(key_mem, d_key_hidden), (query_mem, d_read)],
            [(d_miss, key_act), (d_memory, read_low), (gw_out_early,)],
        ],
        inner,
    )
    gw_query_mem = t_dot(d_query_mem, n1_own).astype(BF)
    gw_mem = lax.dynamic_update_slice(gw_mem, gw_query_mem, (0, 2 * hidden))
    share_mem = lax.psum_scatter(gw_mem, "dp", scatter_dimension=0, tiled=True)
    d_n1_part = d_n1_part + in_own(dot(d_query_mem, wqm_t))
    d_n1_part, share_attn, output = together(d_n1_part.astype(BF), share_attn, output)
    last = chain_sum(jnp.concatenate([d_n1_part, d_persist_part.astype(BF)], axis=0), 5)
    d_n1 = last[:count].astype(F32)
    g_persist = last[count:]
    gg_attn = jnp.sum(d_n1 * x * r1, axis=0)
    d_x = d_after_attn + rms_back(x, r1, g_attn, d_n1)

    def cut(share, *widths):
        return [part.astype(F32) for part in cut_apart(share, *widths)]

    s_down, s_gate, s_up = cut(share_ffn, *[w_gate.shape[1]] * 3)
    s_key_mem, s_value_mem, s_output, s_query, s_key, s_value = cut(share_attn, *[inner] * 6)
    s_in, s_out, s_query_mem = cut(share_mem, hidden, hidden, inner)
    grad_vectors = jnp.stack([gg_attn, gg_mem, gg_ffn, gg_rate], axis=1)
    rest = jnp.concatenate(
        [
            g_persist.T,
            grad_vectors.astype(BF),
            jnp.zeros((width, 128 - slots - 4), BF),
        ],
        axis=1,
    ).reshape(ranks, -1, width)
    turned = t_dot(deal_m, d_x.astype(BF)).astype(BF).reshape(ranks, -1, width)
    came = lax.all_to_all(
        jnp.concatenate([turned, rest], axis=1), "dp", split_axis=0, concat_axis=0, tiled=True
    )
    seats = count // ranks
    grad_tokens = t_dot(send_m, came[:, :seats].reshape(count, width)).astype(BF)
    share_rest = jnp.sum(came[:, seats:].astype(F32), axis=0).reshape(shard, -1)
    s_small = share_rest
    s_vectors = s_small[:, slots : slots + 4].T

    return (
        output,
        grad_tokens,
        s_small[:, :slots].T,
        s_vectors[0],
        s_query_mem.T,
        s_in,
        s_out.T,
        s_query,
        s_key,
        s_value,
        s_output.T,
        s_vectors[1],
        s_key_mem.T,
        -s_value_mem.T,
        s_vectors[3],
        s_vectors[2],
        s_gate,
        s_up,
        s_down.T,
    )


def solution(mesh):
    rows = P("dp", None)
    vector = P("dp")
    across = P("tensor", "dp")
    along = P("dp", "tensor")
    return jax.shard_map(
        per_device,
        mesh=mesh,
        in_specs=(
            rows,
            rows,
            vector,
            vector,
            rows,
            P(None, "dp"),
            vector,
            across,
            along,
            across,
            along,
            along,
            along,
            across,
            vector,
            across,
            across,
            vector,
            vector,
            along,
            along,
            across,
        ),
        out_specs=(
            rows,
            rows,
            P(None, "dp"),
            vector,
            across,
            along,
            across,
            along,
            along,
            along,
            across,
            vector,
            across,
            across,
            vector,
            vector,
            along,
            along,
            across,
        ),
        check_vma=False,
    )
```

```python
import functools

import jax
import jax.numpy as jnp
from jax import lax
from jax.experimental import pallas as pl
from jax.experimental.pallas import tpu as pltpu
from jax.sharding import PartitionSpec as P

HD = 96
EPSILON = 1e-06
RATE_SCALE = 8e-05
NEG_LARGE = -1e30
BF = jnp.bfloat16
F32 = jnp.float32
MESH = pl.DeviceIdType.MESH
TILE = 128
GRANT = 1 << 20


def chain_sum_kernel(pieces, layout, x_ref, *refs):
    given = sum(len(widths) for _, parts in layout for widths in parts)
    fills, refs = refs[:given], refs[given:]
    o_ref, refs = refs[0], refs[1:]
    if layout:
        g_ref, refs = refs[0], refs[1:]
    from_outer, from_inner, part, sent_a, got_up, sent_b, got_across, got_total = refs[:8]
    me = lax.axis_index("tensor")
    step = x_ref.shape[0] // pieces
    low = me < 2
    outer = jnp.logical_or(me == 0, me == 3)
    inner = jnp.logical_not(outer)
    outer_peer = jnp.where(low, 0, 3)
    inner_peer = jnp.where(low, 2, 1)
    toward = jnp.where(low, 1, 2)
    barrier = pltpu.get_barrier_semaphore()

    def tell(peer):
        pl.semaphore_signal(barrier, inc=1, device_id={"tensor": peer}, device_id_type=MESH)

    def at(piece):
        return pl.ds(pl.multiple_of(piece * step, step), step)

    def send(src, dst, send_sem, recv_sem, peer):
        return pltpu.make_async_remote_copy(
            src_ref=src,
            dst_ref=dst,
            send_sem=send_sem,
            recv_sem=recv_sem,
            device_id={"tensor": peer},
            device_id_type=MESH,
        )

    def up(p):
        return send(x_ref.at[at(p)], from_outer.at[at(p)], sent_a.at[p], got_up.at[p], toward)

    def across(p):
        return send(part.at[at(p)], from_inner.at[at(p)], sent_b.at[p], got_across.at[p], inner_peer)

    def down(p):
        return send(o_ref.at[at(p)], o_ref.at[at(p)], sent_a.at[p], got_total.at[p], outer_peer)

    def put(tile):
        stage, put_sem = refs[8], refs[9]
        rows = pl.ds(pl.multiple_of(tile * TILE, TILE), TILE)
        slot = lax.rem(tile, 2)
        target = g_ref.at[rows, pl.ds(0, stage.shape[2])]
        return pltpu.make_async_copy(stage.at[slot], target, put_sem.at[slot])

    def fill(tile):
        stage = refs[8]
        columns = pl.ds(pl.multiple_of(tile * TILE, TILE), TILE)
        slot = lax.rem(tile, 2)

        @pl.when(tile >= 2)
        def _():
            put(tile - 2).wait()

        first, offset = 0, 0
        for width, parts in layout:
            for start in range(0, width, 512):
                span = min(512, width - start)
                total, index = None, first
                for part_sizes in parts:
                    if len(part_sizes) == 1:
                        term = fills[index][columns, start : start + span].astype(F32)
                    else:
                        term = lax.dot_general(
                            fills[index][:, columns],
                            fills[index + 1][:, start : start + span],
                            (((0,), (0,)), ((), ())),
                            preferred_element_type=F32,
                        )
                    total = term if total is None else total + term
                    index += len(part_sizes)
                stage[slot, :, offset + start : offset + start + span] = total.astype(BF)
            first, offset = index, offset + width
        put(tile).start()

    @pl.when(outer)
    def _():
        tell(toward)
        pl.semaphore_wait(barrier, 1)

        @pl.loop(0, pieces)
        def _(p):
            up(p).start()

    @pl.when(inner)
    def _():
        tell(outer_peer)
        tell(inner_peer)
        pl.semaphore_wait(barrier, 2)

    def first_add(p):
        up(p).wait_recv()
        part[at(p), :] = (
            x_ref[at(p), :].astype(F32) + from_outer[at(p), :].astype(F32)
        ).astype(part.dtype)
        across(p).start()

    def second_add(p):
        across(p).wait_recv()
        o_ref[at(p), :] = (
            part[at(p), :].astype(F32) + from_inner[at(p), :].astype(F32)
        ).astype(o_ref.dtype)
        down(p).start()

    tiles = g_ref.shape[0] // TILE if layout else 0

    per, lag = 2, 2
    turns = pieces // per

    @pl.loop(0, max(turns + lag, tiles))
    def _(p):
        @pl.when(jnp.logical_and(inner, p < turns))
        def _():
            for k in range(per):
                first_add(p * per + k)

        @pl.when(jnp.logical_and(inner, jnp.logical_and(p >= lag, p < turns + lag)))
        def _():
            for k in range(per):
                second_add((p - lag) * per + k)

        if layout:

            @pl.when(p < tiles)
            def _():
                fill(p)

    if layout:
        put(tiles - 2).wait()
        put(tiles - 1).wait()

    @pl.when(outer)
    def _():
        @pl.loop(0, pieces)
        def _(p):
            down(p).wait_recv()
            up(p).wait_send()

    @pl.when(inner)
    def _():
        @pl.loop(0, pieces)
        def _(p):
            across(p).wait_send()
            down(p).wait_send()


def chain_sum(x, call_id=1, products=(), room=0):
    rows, cols = x.shape
    pieces = rows // 16
    dma = pltpu.SemaphoreType.DMA
    vmem = pl.BlockSpec(memory_space=pltpu.VMEM)
    layout = tuple(
        (pairs[0][1].shape[1], tuple((0,) * len(pair) for pair in pairs)) for pairs in products
    )
    fills = [array for pairs in products for pair in pairs for array in pair]
    out_shape = [jax.ShapeDtypeStruct((rows, cols), BF)]
    out_specs = [vmem]
    scratch = [pltpu.VMEM((rows, cols), BF)] * 3 + [dma((pieces,))] * 5
    grant = 3 * rows * cols * 2 + GRANT
    if products:
        width, high = sum(w for w, _ in layout), products[0][0][0].shape[1]
        out_shape.append(jax.ShapeDtypeStruct((high, width + room), BF))
        out_specs.append(pl.BlockSpec(memory_space=pl.ANY))
        scratch += [pltpu.VMEM((2, TILE, width), BF), dma((2,))]
        grant += 2 * TILE * width * 2 + 4 * GRANT
    out = pl.pallas_call(
        functools.partial(chain_sum_kernel, pieces, layout),
        out_shape=out_shape,
        in_specs=[vmem] * (1 + len(fills)),
        out_specs=out_specs,
        scratch_shapes=scratch,
        compiler_params=pltpu.CompilerParams(
            collective_id=call_id, has_side_effects=True, vmem_limit_bytes=grant
        ),
        cost_estimate=pl.CostEstimate(flops=0, bytes_accessed=10**8, transcendentals=0),
        name="chain_sum",
    )(x.astype(BF), *fills)
    return out if products else out[0]


def line_gather_kernel(pieces, x_ref, o_ref, sent, got, keep):
    me = lax.axis_index("tensor")
    high = x_ref.shape[0]
    step = high // pieces
    last = 3
    barrier = pltpu.get_barrier_semaphore()
    ways = ((0, me < last, 1), (1, me > 0, -1))

    for _, open_, move in ways:

        @pl.when(open_)
        def _():
            pl.semaphore_signal(
                barrier, inc=1, device_id={"tensor": me + move}, device_id_type=MESH
            )

    at_end = jnp.logical_or(me == 0, me == last)

    @pl.when(at_end)
    def _():
        pl.semaphore_wait(barrier, 1)

    @pl.when(jnp.logical_not(at_end))
    def _():
        pl.semaphore_wait(barrier, 2)

    def copy(way, hop, piece, move, block, first=False):
        rows = pl.ds(pl.multiple_of(block * high + piece * step, step), step)
        return pltpu.make_async_remote_copy(
            src_ref=x_ref.at[pl.ds(piece * step, step)] if first else o_ref.at[rows],
            dst_ref=o_ref.at[rows],
            send_sem=sent.at[way, hop, piece],
            recv_sem=got.at[way, hop, piece],
            device_id={"tensor": jnp.clip(me + move, 0, last)},
            device_id_type=MESH,
        )

    def forward(way, move, hop):
        block = me - move * hop
        return jnp.logical_and(
            jnp.logical_and(me + move >= 0, me + move <= last),
            jnp.logical_and(block >= 0, block <= last),
        )

    def comes(way, move, hop):
        block = me - move * (hop + 1)
        return jnp.logical_and(block >= 0, block <= last)

    def own():
        rows = pl.ds(pl.multiple_of(me * high, high), high)
        return pltpu.make_async_copy(x_ref, o_ref.at[rows], keep.at[0])

    for hop in range(last):
        for piece in range(pieces):
            for way, _, move in ways:

                @pl.when(forward(way, move, hop))
                def _():
                    copy(way, hop, piece, move, me - move * hop, hop == 0).start()

        if hop == 0:
            own().start()
        for piece in range(pieces):
            for way, _, move in ways:

                @pl.when(comes(way, move, hop))
                def _():
                    copy(way, hop, piece, move, me - move * (hop + 1)).wait_recv()

    own().wait()
    for hop in range(last):
        for piece in range(pieces):
            for way, _, move in ways:

                @pl.when(forward(way, move, hop))
                def _():
                    copy(way, hop, piece, move, me - move * hop, hop == 0).wait_send()


def line_gather(x, call_id, pieces=2):
    rows, cols = x.shape
    dma = pltpu.SemaphoreType.DMA
    vmem = pl.BlockSpec(memory_space=pltpu.VMEM)
    return pl.pallas_call(
        functools.partial(line_gather_kernel, pieces),
        out_shape=jax.ShapeDtypeStruct((4 * rows, cols), BF),
        in_specs=[vmem],
        out_specs=vmem,
        scratch_shapes=[dma((2, 3, pieces)), dma((2, 3, pieces)), dma((1,))],
        compiler_params=pltpu.CompilerParams(
            collective_id=call_id, has_side_effects=True, vmem_limit_bytes=GRANT
        ),
        cost_estimate=pl.CostEstimate(flops=0, bytes_accessed=5 * 10**7, transcendentals=0),
        name="line_gather",
    )(x)


def dot(left, right):
    return lax.dot_general(left, right, (((1,), (0,)), ((), ())), preferred_element_type=F32)


def dot_t(left, right):
    return lax.dot_general(left, right, (((1,), (1,)), ((), ())), preferred_element_type=F32)


def t_dot(left, right):
    return lax.dot_general(left, right, (((0,), (0,)), ((), ())), preferred_element_type=F32)


def batch_dot(spec, left, right):
    return jnp.einsum(spec, left, right, preferred_element_type=F32)


def cut_apart(whole, *widths):
    out, low = [], 0
    for width in widths:
        out.append(whole[:, low : low + width])
        low += width
    return out


def together(*values):
    return lax.optimization_barrier(values)


def rms(v):
    return lax.rsqrt(jnp.mean(v * v, axis=-1, keepdims=True) + EPSILON)


def rms_back(v, r, gain, grad):
    scaled = grad * gain
    inner = jnp.sum(scaled * v, axis=-1, keepdims=True)
    return r * scaled - v * (r * r * r) * (inner / v.shape[-1])


def silu_parts(z):
    s = jax.nn.sigmoid(z)
    return s, z * s, s * (1.0 + z * (1.0 - s))


def per_device(
    tokens,
    cotangent,
    dest,
    source,
    lengths,
    persist,
    gain_attn,
    w_query_mem,
    mem_in,
    mem_out,
    w_query,
    w_key,
    w_value,
    w_output,
    gain_mem,
    w_key_mem,
    w_value_mem,
    w_rate,
    gain_ffn,
    w_gate,
    w_up,
    w_down,
):
    count, width = tokens.shape
    shard = gain_attn.shape[0]
    ranks = width // shard
    batches, _ = lengths.shape
    rows = count // batches
    hidden = mem_in.shape[1]
    inner = w_query.shape[1]
    heads = inner // HD
    slots = persist.shape[0]
    me = lax.axis_index("tensor")

    def gather_whole(*parts):
        return lax.all_gather(jnp.concatenate(parts, axis=1), "dp", axis=0, tiled=True)

    def gather(*parts):
        return cut_apart(gather_whole(*parts), *[part.shape[1] for part in parts])

    vectors = jnp.stack([gain_attn, gain_mem, gain_ffn, w_rate], axis=1)
    pad = jnp.zeros((shard, 128 - slots - 4), BF)
    small, wqm_t = gather(jnp.concatenate([persist.T, vectors, pad], axis=1), w_query_mem.T)
    tall = line_gather(jnp.concatenate([w_key_mem, w_value_mem], axis=1), 7)
    persistent = small[:, :slots].T
    gains = small[:, slots : slots + 4].astype(F32).T
    g_attn, g_mem, g_ffn, rate_w = (gains[i][None, :] for i in range(4))

    place = jnp.arange(count, dtype=jnp.int32)
    home = dest // count
    earlier = (home[None, :] == home[:, None]) & (place[None, :] < place[:, None])
    sent_at = home * (count // ranks) + jnp.sum(earlier.astype(jnp.int32), axis=1)
    came_at = jnp.sum((source[None, :] < source[:, None]).astype(jnp.int32), axis=1)
    send_m = (sent_at[None, :] == place[:, None]).astype(BF)
    deal_m = (came_at[:, None] == place[None, :]).astype(BF)

    def exchange(v):
        return lax.all_to_all(v, "dp", split_axis=0, concat_axis=0, tiled=True)

    def give_back(v):
        back = lax.all_to_all(
            t_dot(deal_m, v.astype(BF)).astype(BF), "dp", split_axis=0, concat_axis=0, tiled=True
        )
        return t_dot(send_m, back).astype(BF)

    leaving, late_in, late_mem_out = together(dot(send_m, tokens).astype(BF), mem_in, mem_out)
    w_in, w_out_t = gather(late_in, late_mem_out.T)
    arrived, tall = together(exchange(leaving), tall)
    dealt = dot(deal_m, arrived).astype(BF)
    x = dealt.astype(F32)

    position = jnp.arange(rows, dtype=jnp.int32)
    turn = jnp.arange(lengths.shape[1])
    bounds = jnp.sum(
        jnp.where(turn[:, None] <= turn[None, :], lengths[:, :, None], 0), axis=1, dtype=jnp.int32
    )
    segment = jnp.sum((position[None, :, None] >= bounds[:, None, :]).astype(jnp.int32), axis=2)
    causal = (segment[:, :, None] == segment[:, None, :]) & (
        position[None, None, :] <= position[None, :, None]
    )

    def split(v):
        return v.reshape(batches, rows, v.shape[-1])

    def join(v):
        return v.reshape(count, v.shape[-1])

    def own(v):
        return lax.dynamic_slice_in_dim(v, me * inner, inner, 1)

    def in_own(v):
        return lax.dynamic_update_slice_in_dim(
            jnp.zeros((v.shape[0], width), v.dtype), v, me * inner, 1
        )

    r1 = rms(x)
    n1 = (x * r1 * g_attn).astype(BF)
    n1_own = own(n1)
    query_mem = chain_sum(dot_t(n1_own, wqm_t))
    query_mem, late_query, late_key, late_value, late_output = together(
        query_mem, w_query, w_key, w_value, w_output
    )
    w_attn = gather_whole(late_query, late_key, late_value, late_output.T)
    read_s, read_act, read_slope = silu_parts(dot(query_mem, w_in))
    read_low, tall = together(read_act.astype(BF), tall)
    wkm_t, wvm_t = gather(tall[:, :shard].T, tall[:, shard:].T)
    memory = chain_sum(dot_t(read_low, w_out_t))
    memory, w_attn = together(memory, w_attn)
    wq, wk, wv, wo_t = cut_apart(w_attn, inner, inner, inner, inner)
    query = dot(n1, wq).astype(BF)
    key_p, value_p = dot(persistent, wk).astype(BF), dot(persistent, wv).astype(BF)
    key_x, value_x = dot(n1, wk).astype(BF), dot(n1, wv).astype(BF)

    key_m, value_m = dot(memory, wk).astype(BF), dot(memory, wv).astype(BF)

    def context(p, m, t):
        wide = jnp.broadcast_to(p[None], (batches,) + p.shape)
        all_rows = jnp.concatenate([wide, split(m), split(t)], axis=1)
        return all_rows.reshape(batches, -1, heads, HD)

    keys, values = context(key_p, key_m, key_x), context(value_p, value_m, value_x)
    allowed = jnp.concatenate(
        [jnp.ones((batches, rows, slots), dtype=bool), causal, causal], axis=2
    )[:, None]
    query4 = query.reshape(batches, rows, heads, HD)
    scores = batch_dot("bqhd,bkhd->bhqk", query4, keys) * HD ** (-0.5)
    weights = jax.nn.softmax(jnp.where(allowed, scores, NEG_LARGE), axis=-1)
    weights_low = weights.astype(BF)
    mixed = batch_dot("bhqk,bkhd->bqhd", weights_low, values).astype(BF).reshape(count, inner)
    mixed, late_gate, late_up, late_down, later = together(mixed, w_gate, w_up, w_down, cotangent)
    cotangent_arrived = exchange(dot(send_m, later).astype(BF))
    wg, wu, wd_t = gather(late_gate, late_up, late_down.T)
    attended, cotangent_arrived = together(chain_sum(dot_t(mixed, wo_t)), cotangent_arrived)
    after_attn = x + attended.astype(F32)
    d_out_low = dot(deal_m, cotangent_arrived).astype(BF)

    r2 = rms(after_attn)
    n2 = after_attn * r2 * g_mem
    rate_s = jax.nn.sigmoid(jnp.sum(n2 * rate_w, axis=1, keepdims=True))
    rate = RATE_SCALE * rate_s
    n2_low = n2.astype(BF)
    n2_own = own(n2_low)
    key_mem = dot_t(n2_low, wkm_t).astype(BF)
    value_part = dot_t(n2_own, own(wvm_t))
    key_hidden = dot(key_mem, w_in)
    key_s, key_silu, key_slope = silu_parts(key_hidden)
    key_act = key_silu.astype(BF)
    miss = chain_sum(dot_t(key_act, w_out_t) - value_part).astype(F32)
    error = (rate * miss).astype(BF)
    back_pre = dot(error, w_out_t)
    back_hidden = (back_pre * key_slope).astype(BF)
    gram = jnp.where(causal, batch_dot("bik,bjk->bij", split(key_mem), split(key_mem)), 0.0).astype(BF)
    new_hidden = key_hidden - join(batch_dot("bij,bjk->bik", gram, split(back_hidden)))
    _, new_silu, new_slope = silu_parts(new_hidden)
    new_act = new_silu.astype(BF)
    pair = jnp.where(causal, batch_dot("bik,bjk->bij", split(new_act), split(key_act)), 0.0).astype(BF)
    update = dot_t(new_act, w_out_t) - join(batch_dot("bij,bjk->bik", pair, split(error)))
    after_mem = after_attn + chain_sum(update).astype(F32)

    r3 = rms(after_mem)
    n3 = (after_mem * r3 * g_ffn).astype(BF)
    gate, up = dot(n3, wg), dot(n3, wu)
    _, gate_silu, gate_slope = silu_parts(gate)
    ffn_act = (gate_silu * up).astype(BF)
    ffn_own = lax.psum_scatter(
        dot_t(ffn_act, wd_t).astype(BF), "tensor", scatter_dimension=1, tiled=True
    )

    d_ffn = dot(d_out_low, wd_t)
    d_gate = (d_ffn * up * gate_slope).astype(BF)
    d_up = (d_ffn * gate_silu).astype(BF)
    d_n3, gw_ffn = chain_sum(
        dot_t(d_gate, wg) + dot_t(d_up, wu),
        2,
        [[(d_out_low, ffn_act)], [(n3, d_gate)], [(n3, d_up)]],
    )
    d_n3 = d_n3.astype(F32)
    gg_ffn = jnp.sum(d_n3 * after_mem * r3, axis=0)
    d_after_mem = d_out_low.astype(F32) + rms_back(after_mem, r3, g_ffn, d_n3)
    d_update = d_after_mem.astype(BF)

    d_pair = jnp.where(
        causal, -batch_dot("bik,bjk->bij", split(d_update), split(error)), 0.0
    ).astype(BF)
    d_new_act = dot(d_update, w_out_t) + join(batch_dot("bij,bjk->bik", d_pair, split(key_act)))
    d_key_act = join(batch_dot("bij,bik->bjk", d_pair, split(new_act)))
    d_new_hidden = (d_new_act * new_slope).astype(BF)
    d_gram = jnp.where(
        causal, -batch_dot("bik,bjk->bij", split(d_new_hidden), split(back_hidden)), 0.0
    ).astype(BF)
    d_back = (-join(batch_dot("bij,bik->bjk", gram, split(d_new_hidden)))).astype(BF).astype(F32)
    d_back_pre = (d_back * key_slope).astype(BF)
    slope_grad = key_s * (1.0 - key_s) * (2.0 + key_hidden * (1.0 - 2.0 * key_s))
    d_hidden_part = d_new_hidden.astype(F32) + d_back * back_pre * slope_grad
    d_error_part = dot_t(d_back_pre, w_out_t) - join(
        batch_dot("bij,bik->bjk", pair, split(d_update))
    )
    share_ffn = lax.psum_scatter(gw_ffn, "dp", scatter_dimension=0, tiled=True)
    d_error = chain_sum(d_error_part).astype(F32)
    d_rate = jnp.sum(d_error * miss, axis=1, keepdims=True)
    late_rate, ffn_own = together(rate, ffn_own)
    d_miss = (late_rate * d_error).astype(BF)
    d_key_act = d_key_act + dot(d_miss, w_out_t)
    d_key_hidden = (d_hidden_part + d_key_act * key_slope).astype(BF)
    d_key_part = dot_t(d_key_hidden, w_in) + join(
        batch_dot("bij,bjk->bik", d_gram, split(key_mem))
        + batch_dot("bij,bik->bjk", d_gram, split(key_mem))
    )
    result_own = give_back(own(after_mem) + ffn_own.astype(F32))
    d_key, gw_out_early = chain_sum(
        d_key_part, 6, [[(d_update, new_act), (error, d_back_pre)]]
    )
    d_n2 = dot(d_key, wkm_t) - dot(d_miss, wvm_t)
    d_logit = d_rate * rate * (1.0 - rate_s)
    gg_rate = jnp.sum(n2 * d_logit, axis=0)
    d_n2 = d_n2 + d_logit * rate_w
    gg_mem = jnp.sum(d_n2 * after_attn * r2, axis=0)
    late_r2, share_ffn, result_own = together(r2, share_ffn, result_own)
    output = lax.all_gather(result_own, "tensor", axis=1, tiled=True)
    d_after_attn = d_after_mem + rms_back(after_attn, late_r2, g_mem, d_n2)
    d_attn = d_after_attn.astype(BF)

    d_mixed = dot(d_attn, wo_t).astype(BF)
    d_mixed4 = d_mixed.reshape(batches, rows, heads, HD)
    d_weights = batch_dot("bqhd,bkhd->bhqk", d_mixed4, values)
    d_values = batch_dot("bhqk,bqhd->bkhd", weights_low, d_mixed4)
    d_scores = (
        weights * (d_weights - jnp.sum(weights * d_weights, axis=-1, keepdims=True))
    ).astype(BF)
    d_query = batch_dot("bhqk,bkhd->bqhd", d_scores, keys) * HD ** (-0.5)
    d_keys = batch_dot("bhqk,bqhd->bkhd", d_scores, query4) * HD ** (-0.5)
    d_query = d_query.astype(BF).reshape(count, inner)

    def apart(v):
        v = v.reshape(batches, -1, inner)
        return (
            jnp.sum(v[:, :slots], axis=0).astype(BF),
            join(v[:, slots : slots + rows]).astype(BF),
            join(v[:, slots + rows :]).astype(BF),
        )

    dk_p, dk_m, dk_x = apart(d_keys)
    dv_p, dv_m, dv_x = apart(d_values)
    d_memory, gw_attn = chain_sum(
        dot_t(dk_m, wk) + dot_t(dv_m, wv),
        3,
        [
            [(d_key, n2_own)],
            [(d_miss, n2_own)],
            [(d_attn, mixed)],
            [(n1, d_query)],
            [(persistent, dk_p), (memory, dk_m), (n1, dk_x)],
            [(persistent, dv_p), (memory, dv_m), (n1, dv_x)],
        ],
    )
    d_n1_part = dot_t(d_query, wq) + dot_t(dk_x, wk) + dot_t(dv_x, wv)
    d_persist_part = dot_t(dk_p, wk) + dot_t(dv_p, wv)

    share_attn = lax.psum_scatter(gw_attn, "dp", scatter_dimension=0, tiled=True)
    d_read = (dot(d_memory, w_out_t) * read_slope).astype(BF)
    d_query_mem, gw_mem = chain_sum(
        dot_t(d_read, w_in),
        4,
        [
            [(key_mem, d_key_hidden), (query_mem, d_read)],
            [(d_miss, key_act), (d_memory, read_low), (gw_out_early,)],
        ],
        inner,
    )
    gw_query_mem = t_dot(d_query_mem, n1_own).astype(BF)
    gw_mem = lax.dynamic_update_slice(gw_mem, gw_query_mem, (0, 2 * hidden))
    share_mem = lax.psum_scatter(gw_mem, "dp", scatter_dimension=0, tiled=True)
    d_n1_part = d_n1_part + in_own(dot(d_query_mem, wqm_t))
    d_persist_part, share_attn, output = together(d_persist_part.astype(BF), share_attn, output)
    last = chain_sum(jnp.concatenate([d_n1_part.astype(BF), d_persist_part], axis=0), 5)
    d_n1 = last[:count].astype(F32)
    g_persist = last[count:]
    gg_attn = jnp.sum(d_n1 * x * r1, axis=0)
    d_x = d_after_attn + rms_back(x, r1, g_attn, d_n1)

    def cut(share, *widths):
        return [part.astype(F32) for part in cut_apart(share, *widths)]

    s_down, s_gate, s_up = cut(share_ffn, *[w_gate.shape[1]] * 3)
    s_key_mem, s_value_mem, s_output, s_query, s_key, s_value = cut(share_attn, *[inner] * 6)
    s_in, s_out, s_query_mem = cut(share_mem, hidden, hidden, inner)
    grad_vectors = jnp.stack([gg_attn, gg_mem, gg_ffn, gg_rate], axis=1)
    rest = jnp.concatenate(
        [
            g_persist.T,
            grad_vectors.astype(BF),
            jnp.zeros((width, 128 - slots - 4), BF),
        ],
        axis=1,
    ).reshape(ranks, -1, width)
    turned = t_dot(deal_m, d_x.astype(BF)).astype(BF).reshape(ranks, -1, width)
    came = lax.all_to_all(
        jnp.concatenate([turned, rest], axis=1), "dp", split_axis=0, concat_axis=0, tiled=True
    )
    seats = count // ranks
    grad_tokens = t_dot(send_m, came[:, :seats].reshape(count, width)).astype(BF)
    share_rest = jnp.sum(came[:, seats:].astype(F32), axis=0).reshape(shard, -1)
    s_small = share_rest
    s_vectors = s_small[:, slots : slots + 4].T

    return (
        output,
        grad_tokens,
        s_small[:, :slots].T,
        s_vectors[0],
        s_query_mem.T,
        s_in,
        s_out.T,
        s_query,
        s_key,
        s_value,
        s_output.T,
        s_vectors[1],
        s_key_mem.T,
        -s_value_mem.T,
        s_vectors[3],
        s_vectors[2],
        s_gate,
        s_up,
        s_down.T,
    )


def solution(mesh):
    rows = P("dp", None)
    vector = P("dp")
    across = P("tensor", "dp")
    along = P("dp", "tensor")
    return jax.shard_map(
        per_device,
        mesh=mesh,
        in_specs=(
            rows,
            rows,
            vector,
            vector,
            rows,
            P(None, "dp"),
            vector,
            across,
            along,
            across,
            along,
            along,
            along,
            across,
            vector,
            across,
            across,
            vector,
            vector,
            along,
            along,
            across,
        ),
        out_specs=(
            rows,
            rows,
            P(None, "dp"),
            vector,
            across,
            along,
            across,
            along,
            along,
            along,
            across,
            vector,
            across,
            across,
            vector,
            vector,
            along,
            along,
            across,
        ),
        check_vma=False,
    )
```

```python
import functools

import jax
import jax.numpy as jnp
from jax import lax
from jax.experimental import pallas as pl
from jax.experimental.pallas import tpu as pltpu
from jax.sharding import PartitionSpec as P

HD = 96
EPSILON = 1e-06
RATE_SCALE = 8e-05
NEG_LARGE = -1e30
BF = jnp.bfloat16
F32 = jnp.float32
MESH = pl.DeviceIdType.MESH
TILE = 128
GRANT = 1 << 20


def chain_sum_kernel(pieces, layout, x_ref, *refs):
    given = sum(len(widths) for _, parts in layout for widths in parts)
    fills, refs = refs[:given], refs[given:]
    o_ref, refs = refs[0], refs[1:]
    if layout:
        g_ref, refs = refs[0], refs[1:]
    from_outer, from_inner, part, sent_a, got_up, sent_b, got_across, got_total = refs[:8]
    me = lax.axis_index("tensor")
    step = x_ref.shape[0] // pieces
    low = me < 2
    outer = jnp.logical_or(me == 0, me == 3)
    inner = jnp.logical_not(outer)
    outer_peer = jnp.where(low, 0, 3)
    inner_peer = jnp.where(low, 2, 1)
    toward = jnp.where(low, 1, 2)
    barrier = pltpu.get_barrier_semaphore()

    def tell(peer):
        pl.semaphore_signal(barrier, inc=1, device_id={"tensor": peer}, device_id_type=MESH)

    def at(piece):
        return pl.ds(pl.multiple_of(piece * step, step), step)

    def send(src, dst, send_sem, recv_sem, peer):
        return pltpu.make_async_remote_copy(
            src_ref=src,
            dst_ref=dst,
            send_sem=send_sem,
            recv_sem=recv_sem,
            device_id={"tensor": peer},
            device_id_type=MESH,
        )

    def up(p):
        return send(x_ref.at[at(p)], from_outer.at[at(p)], sent_a.at[p], got_up.at[p], toward)

    def across(p):
        return send(part.at[at(p)], from_inner.at[at(p)], sent_b.at[p], got_across.at[p], inner_peer)

    def down(p):
        return send(o_ref.at[at(p)], o_ref.at[at(p)], sent_a.at[p], got_total.at[p], outer_peer)

    def put(tile):
        stage, put_sem = refs[8], refs[9]
        rows = pl.ds(pl.multiple_of(tile * TILE, TILE), TILE)
        slot = lax.rem(tile, 2)
        target = g_ref.at[rows, pl.ds(0, stage.shape[2])]
        return pltpu.make_async_copy(stage.at[slot], target, put_sem.at[slot])

    def fill(tile):
        stage = refs[8]
        columns = pl.ds(pl.multiple_of(tile * TILE, TILE), TILE)
        slot = lax.rem(tile, 2)

        @pl.when(tile >= 2)
        def _():
            put(tile - 2).wait()

        first, offset = 0, 0
        for width, parts in layout:
            for start in range(0, width, 512):
                span = min(512, width - start)
                total, index = None, first
                for part_sizes in parts:
                    if len(part_sizes) == 1:
                        term = fills[index][columns, start : start + span].astype(F32)
                    else:
                        term = lax.dot_general(
                            fills[index][:, columns],
                            fills[index + 1][:, start : start + span],
                            (((0,), (0,)), ((), ())),
                            preferred_element_type=F32,
                        )
                    total = term if total is None else total + term
                    index += len(part_sizes)
                stage[slot, :, offset + start : offset + start + span] = total.astype(BF)
            first, offset = index, offset + width
        put(tile).start()

    @pl.when(outer)
    def _():
        tell(toward)
        pl.semaphore_wait(barrier, 1)

        @pl.loop(0, pieces)
        def _(p):
            up(p).start()

    @pl.when(inner)
    def _():
        tell(outer_peer)
        tell(inner_peer)
        pl.semaphore_wait(barrier, 2)

    def first_add(p):
        up(p).wait_recv()
        part[at(p), :] = (
            x_ref[at(p), :].astype(F32) + from_outer[at(p), :].astype(F32)
        ).astype(part.dtype)
        across(p).start()

    def second_add(p):
        across(p).wait_recv()
        o_ref[at(p), :] = (
            part[at(p), :].astype(F32) + from_inner[at(p), :].astype(F32)
        ).astype(o_ref.dtype)
        down(p).start()

    tiles = g_ref.shape[0] // TILE if layout else 0

    per, lag = 2, 2
    turns = pieces // per

    @pl.loop(0, max(turns + lag, tiles))
    def _(p):
        @pl.when(jnp.logical_and(inner, p < turns))
        def _():
            for k in range(per):
                first_add(p * per + k)

        @pl.when(jnp.logical_and(inner, jnp.logical_and(p >= lag, p < turns + lag)))
        def _():
            for k in range(per):
                second_add((p - lag) * per + k)

        if layout:

            @pl.when(p < tiles)
            def _():
                fill(p)

    if layout:
        put(tiles - 2).wait()
        put(tiles - 1).wait()

    @pl.when(outer)
    def _():
        @pl.loop(0, pieces)
        def _(p):
            down(p).wait_recv()
            up(p).wait_send()

    @pl.when(inner)
    def _():
        @pl.loop(0, pieces)
        def _(p):
            across(p).wait_send()
            down(p).wait_send()


def chain_sum(x, call_id=1, products=(), room=0):
    rows, cols = x.shape
    pieces = rows // 16
    dma = pltpu.SemaphoreType.DMA
    vmem = pl.BlockSpec(memory_space=pltpu.VMEM)
    layout = tuple(
        (pairs[0][1].shape[1], tuple((0,) * len(pair) for pair in pairs)) for pairs in products
    )
    fills = [array for pairs in products for pair in pairs for array in pair]
    out_shape = [jax.ShapeDtypeStruct((rows, cols), BF)]
    out_specs = [vmem]
    scratch = [pltpu.VMEM((rows, cols), BF)] * 3 + [dma((pieces,))] * 5
    grant = 3 * rows * cols * 2 + GRANT
    if products:
        width, high = sum(w for w, _ in layout), products[0][0][0].shape[1]
        out_shape.append(jax.ShapeDtypeStruct((high, width + room), BF))
        out_specs.append(pl.BlockSpec(memory_space=pl.ANY))
        scratch += [pltpu.VMEM((2, TILE, width), BF), dma((2,))]
        grant += 2 * TILE * width * 2 + 4 * GRANT
    out = pl.pallas_call(
        functools.partial(chain_sum_kernel, pieces, layout),
        out_shape=out_shape,
        in_specs=[vmem] * (1 + len(fills)),
        out_specs=out_specs,
        scratch_shapes=scratch,
        compiler_params=pltpu.CompilerParams(
            collective_id=call_id, has_side_effects=True, vmem_limit_bytes=grant
        ),
        cost_estimate=pl.CostEstimate(flops=0, bytes_accessed=10**8, transcendentals=0),
        name="chain_sum",
    )(x.astype(BF), *fills)
    return out if products else out[0]


def line_gather_kernel(pieces, side, x_ref, o_ref, sent, got, keep):
    me = lax.axis_index("tensor")
    high, wide = x_ref.shape
    step = high // pieces
    last = 3

    def place(block, low, size):
        if side:
            return o_ref.at[pl.ds(low, size), pl.ds(pl.multiple_of(block * wide, wide), wide)]
        return o_ref.at[pl.ds(pl.multiple_of(block * high + low, size), size)]

    barrier = pltpu.get_barrier_semaphore()
    ways = ((0, me < last, 1), (1, me > 0, -1))

    for _, open_, move in ways:

        @pl.when(open_)
        def _():
            pl.semaphore_signal(
                barrier, inc=1, device_id={"tensor": me + move}, device_id_type=MESH
            )

    at_end = jnp.logical_or(me == 0, me == last)

    @pl.when(at_end)
    def _():
        pl.semaphore_wait(barrier, 1)

    @pl.when(jnp.logical_not(at_end))
    def _():
        pl.semaphore_wait(barrier, 2)

    def copy(way, hop, piece, move, block, first=False):
        there = place(block, piece * step, step)
        return pltpu.make_async_remote_copy(
            src_ref=x_ref.at[pl.ds(piece * step, step)] if first else there,
            dst_ref=there,
            send_sem=sent.at[way, hop, piece],
            recv_sem=got.at[way, hop, piece],
            device_id={"tensor": jnp.clip(me + move, 0, last)},
            device_id_type=MESH,
        )

    def forward(way, move, hop):
        block = me - move * hop
        return jnp.logical_and(
            jnp.logical_and(me + move >= 0, me + move <= last),
            jnp.logical_and(block >= 0, block <= last),
        )

    def comes(way, move, hop):
        block = me - move * (hop + 1)
        return jnp.logical_and(block >= 0, block <= last)

    def own():
        return pltpu.make_async_copy(x_ref, place(me, 0, high), keep.at[0])

    for hop in range(last):
        for piece in range(pieces):
            for way, _, move in ways:

                @pl.when(forward(way, move, hop))
                def _():
                    copy(way, hop, piece, move, me - move * hop, hop == 0).start()

        if hop == 0:
            own().start()
        for piece in range(pieces):
            for way, _, move in ways:

                @pl.when(comes(way, move, hop))
                def _():
                    copy(way, hop, piece, move, me - move * (hop + 1)).wait_recv()

    own().wait()
    for hop in range(last):
        for piece in range(pieces):
            for way, _, move in ways:

                @pl.when(forward(way, move, hop))
                def _():
                    copy(way, hop, piece, move, me - move * hop, hop == 0).wait_send()


def line_gather(x, call_id, side=False, pieces=2):
    rows, cols = x.shape
    shape = (rows, 4 * cols) if side else (4 * rows, cols)
    dma = pltpu.SemaphoreType.DMA
    vmem = pl.BlockSpec(memory_space=pltpu.VMEM)
    return pl.pallas_call(
        functools.partial(line_gather_kernel, pieces, side),
        out_shape=jax.ShapeDtypeStruct(shape, BF),
        in_specs=[vmem],
        out_specs=vmem,
        scratch_shapes=[dma((2, 3, pieces)), dma((2, 3, pieces)), dma((1,))],
        compiler_params=pltpu.CompilerParams(
            collective_id=call_id, has_side_effects=True, vmem_limit_bytes=GRANT
        ),
        cost_estimate=pl.CostEstimate(flops=0, bytes_accessed=5 * 10**7, transcendentals=0),
        name="line_gather",
    )(x)


def dot(left, right):
    return lax.dot_general(left, right, (((1,), (0,)), ((), ())), preferred_element_type=F32)


def dot_t(left, right):
    return lax.dot_general(left, right, (((1,), (1,)), ((), ())), preferred_element_type=F32)


def t_dot(left, right):
    return lax.dot_general(left, right, (((0,), (0,)), ((), ())), preferred_element_type=F32)


def batch_dot(spec, left, right):
    return jnp.einsum(spec, left, right, preferred_element_type=F32)


def cut_apart(whole, *widths):
    out, low = [], 0
    for width in widths:
        out.append(whole[:, low : low + width])
        low += width
    return out


def by_head(v, heads):
    column = lax.broadcasted_iota(jnp.int32, v.shape, 1)
    zero = jnp.zeros_like(v)
    return jnp.concatenate(
        [
            jnp.where(jnp.logical_and(column >= h * HD, column < (h + 1) * HD), v, zero)
            for h in range(heads)
        ],
        axis=0,
    )


def from_heads(v, heads):
    rows = v.shape[0] // heads
    column = lax.broadcasted_iota(jnp.int32, (rows, v.shape[1]), 1)
    out = jnp.zeros((rows, v.shape[1]), v.dtype)
    for h in range(heads):
        here = jnp.logical_and(column >= h * HD, column < (h + 1) * HD)
        out = jnp.where(here, v[h * rows : (h + 1) * rows], out)
    return out


def batch_parts(qkv_ref, mask_ref, batch, slots):
    batches, rows, _ = mask_ref.shape
    inner = qkv_ref.shape[1] // 3
    heads = inner // HD
    mem = slots + batch * rows
    tok = slots + (batches + batch) * rows

    def context(low):
        cols = slice(low, low + inner)
        return jnp.concatenate(
            [qkv_ref[:slots, cols], qkv_ref[mem : mem + rows, cols], qkv_ref[tok : tok + rows, cols]],
            axis=0,
        )

    query = by_head(qkv_ref[tok : tok + rows, :inner], heads)
    keys, values = context(inner), context(2 * inner)
    scores = dot_t(query, keys) * HD ** (-0.5)
    allowed = jnp.concatenate([mask_ref[batch]] * heads, axis=0)
    scores = jnp.where(allowed > 0.5, scores, NEG_LARGE)
    high = jnp.max(scores, axis=1, keepdims=True)
    raised = jnp.exp(scores - high)
    weights = raised / jnp.sum(raised, axis=1, keepdims=True)
    return query, keys, values, weights, heads


def attend_kernel(slots, qkv_ref, mask_ref, o_ref):
    batches, rows, _ = mask_ref.shape
    for batch in range(batches):
        _, _, values, weights, heads = batch_parts(qkv_ref, mask_ref, batch, slots)
        mixed = from_heads(dot(weights.astype(BF), values), heads)
        o_ref[batch * rows : (batch + 1) * rows, :] = mixed.astype(BF)


def attend_back_kernel(slots, qkv_ref, mask_ref, d_ref, o_ref):
    batches, rows, _ = mask_ref.shape
    inner = d_ref.shape[1]
    o_ref[: slots + batches * rows, :inner] = jnp.zeros((slots + batches * rows, inner), BF)
    d_keys_p, d_values_p = jnp.zeros((slots, inner), F32), jnp.zeros((slots, inner), F32)
    for batch in range(batches):
        query, keys, values, weights, heads = batch_parts(qkv_ref, mask_ref, batch, slots)
        mem = slots + batch * rows
        tok = slots + (batches + batch) * rows
        d_mixed = by_head(d_ref[batch * rows : (batch + 1) * rows, :], heads)
        d_weights = dot_t(d_mixed, values)
        d_values = t_dot(weights.astype(BF), d_mixed)
        even = jnp.sum(weights * d_weights, axis=1, keepdims=True)
        d_scores = (weights * (d_weights - even)).astype(BF)
        d_query = from_heads(dot(d_scores, keys), heads) * HD ** (-0.5)
        d_keys = t_dot(d_scores, query) * HD ** (-0.5)
        o_ref[tok : tok + rows, :inner] = d_query.astype(BF)
        d_keys_p, d_values_p = d_keys_p + d_keys[:slots], d_values_p + d_values[:slots]
        for low, grad in ((inner, d_keys), (2 * inner, d_values)):
            o_ref[mem : mem + rows, low : low + inner] = grad[slots : slots + rows].astype(BF)
            o_ref[tok : tok + rows, low : low + inner] = grad[slots + rows :].astype(BF)
    o_ref[:slots, inner : 2 * inner] = d_keys_p.astype(BF)
    o_ref[:slots, 2 * inner :] = d_values_p.astype(BF)


def local_call(body, shape, *operands):
    vmem = pl.BlockSpec(memory_space=pltpu.VMEM)
    return pl.pallas_call(
        body,
        out_shape=jax.ShapeDtypeStruct(shape, BF),
        in_specs=[vmem] * len(operands),
        out_specs=vmem,
        compiler_params=pltpu.CompilerParams(vmem_limit_bytes=16 * GRANT),
        cost_estimate=pl.CostEstimate(flops=0, bytes_accessed=2 * 10**7, transcendentals=0),
        name="attend",
    )(*operands)


def together(*values):
    return lax.optimization_barrier(values)


def rms(v):
    return lax.rsqrt(jnp.mean(v * v, axis=-1, keepdims=True) + EPSILON)


def rms_back(v, r, gain, grad):
    scaled = grad * gain
    inner = jnp.sum(scaled * v, axis=-1, keepdims=True)
    return r * scaled - v * (r * r * r) * (inner / v.shape[-1])


def silu_parts(z):
    s = jax.nn.sigmoid(z)
    return s, z * s, s * (1.0 + z * (1.0 - s))


def per_device(
    tokens,
    cotangent,
    dest,
    source,
    lengths,
    persist,
    gain_attn,
    w_query_mem,
    mem_in,
    mem_out,
    w_query,
    w_key,
    w_value,
    w_output,
    gain_mem,
    w_key_mem,
    w_value_mem,
    w_rate,
    gain_ffn,
    w_gate,
    w_up,
    w_down,
):
    count, width = tokens.shape
    shard = gain_attn.shape[0]
    ranks = width // shard
    batches, _ = lengths.shape
    rows = count // batches
    hidden = mem_in.shape[1]
    inner = w_query.shape[1]
    heads = inner // HD
    slots = persist.shape[0]
    me = lax.axis_index("tensor")

    def gather_whole(*parts):
        return lax.all_gather(jnp.concatenate(parts, axis=1), "dp", axis=0, tiled=True)

    def gather(*parts):
        return cut_apart(gather_whole(*parts), *[part.shape[1] for part in parts])

    vectors = jnp.stack([gain_attn, gain_mem, gain_ffn, w_rate], axis=1)
    pad = jnp.zeros((shard, 128 - slots - 4), BF)
    small, wqm_t = gather(jnp.concatenate([persist.T, vectors, pad], axis=1), w_query_mem.T)
    tall = line_gather(jnp.concatenate([w_key_mem, w_value_mem], axis=1), 7)
    persistent = small[:, :slots].T
    gains = small[:, slots : slots + 4].astype(F32).T
    g_attn, g_mem, g_ffn, rate_w = (gains[i][None, :] for i in range(4))

    place = jnp.arange(count, dtype=jnp.int32)
    home = dest // count
    earlier = (home[None, :] == home[:, None]) & (place[None, :] < place[:, None])
    sent_at = home * (count // ranks) + jnp.sum(earlier.astype(jnp.int32), axis=1)
    came_at = jnp.sum((source[None, :] < source[:, None]).astype(jnp.int32), axis=1)
    send_m = (sent_at[None, :] == place[:, None]).astype(BF)
    deal_m = (came_at[:, None] == place[None, :]).astype(BF)

    def exchange(v):
        return lax.all_to_all(v, "dp", split_axis=0, concat_axis=0, tiled=True)

    leaving, late_in, late_mem_out = together(dot(send_m, tokens).astype(BF), mem_in, mem_out)
    w_in, w_out_t = gather(late_in, late_mem_out.T)
    arrived, tall = together(exchange(leaving), tall)
    dealt = dot(deal_m, arrived).astype(BF)
    x = dealt.astype(F32)

    position = jnp.arange(rows, dtype=jnp.int32)
    turn = jnp.arange(lengths.shape[1])
    bounds = jnp.sum(
        jnp.where(turn[:, None] <= turn[None, :], lengths[:, :, None], 0), axis=1, dtype=jnp.int32
    )
    segment = jnp.sum((position[None, :, None] >= bounds[:, None, :]).astype(jnp.int32), axis=2)
    causal = (segment[:, :, None] == segment[:, None, :]) & (
        position[None, None, :] <= position[None, :, None]
    )

    def split(v):
        return v.reshape(batches, rows, v.shape[-1])

    def join(v):
        return v.reshape(count, v.shape[-1])

    def own(v):
        return lax.dynamic_slice_in_dim(v, me * inner, inner, 1)

    def in_own(v):
        return lax.dynamic_update_slice_in_dim(
            jnp.zeros((v.shape[0], width), v.dtype), v, me * inner, 1
        )

    r1 = rms(x)
    n1 = (x * r1 * g_attn).astype(BF)
    n1_own = own(n1)
    query_mem = chain_sum(dot_t(n1_own, wqm_t))
    query_mem, late_query, late_key, late_value, late_output = together(
        query_mem, w_query, w_key, w_value, w_output
    )
    w_attn = gather_whole(late_query, late_key, late_value, late_output.T)
    read_s, read_act, read_slope = silu_parts(dot(query_mem, w_in))
    read_low, tall = together(read_act.astype(BF), tall)
    wkm_t, wvm_t = gather(tall[:, :shard].T, tall[:, shard:].T)
    memory = chain_sum(dot_t(read_low, w_out_t))
    memory, w_attn = together(memory, w_attn)
    w_qkv, wo_t = cut_apart(w_attn, 3 * inner, inner)
    w_kv = w_attn[:, inner : 3 * inner]
    all_rows = jnp.concatenate([persistent, memory, n1], axis=0)
    qkv = dot(all_rows, w_qkv).astype(BF)
    allowed = jnp.concatenate(
        [jnp.ones((batches, rows, slots), F32), causal.astype(F32), causal.astype(F32)], axis=2
    )
    mixed = local_call(functools.partial(attend_kernel, slots), (count, inner), qkv, allowed)
    mixed, late_gate, late_up, late_down, later = together(mixed, w_gate, w_up, w_down, cotangent)
    cotangent_arrived = exchange(dot(send_m, later).astype(BF))
    wg, wu, wd_t = gather(late_gate, late_up, late_down.T)
    attended, cotangent_arrived = together(chain_sum(dot_t(mixed, wo_t)), cotangent_arrived)
    after_attn = x + attended.astype(F32)
    d_out_low = dot(deal_m, cotangent_arrived).astype(BF)

    r2 = rms(after_attn)
    n2 = after_attn * r2 * g_mem
    rate_s = jax.nn.sigmoid(jnp.sum(n2 * rate_w, axis=1, keepdims=True))
    rate = RATE_SCALE * rate_s
    n2_low = n2.astype(BF)
    n2_own = own(n2_low)
    key_mem = dot_t(n2_low, wkm_t).astype(BF)
    value_part = dot_t(n2_own, own(wvm_t))
    key_hidden = dot(key_mem, w_in)
    key_s, key_silu, key_slope = silu_parts(key_hidden)
    key_act = key_silu.astype(BF)
    miss = chain_sum(dot_t(key_act, w_out_t) - value_part).astype(F32)
    error = (rate * miss).astype(BF)
    back_pre = dot(error, w_out_t)
    back_hidden = (back_pre * key_slope).astype(BF)
    gram = jnp.where(causal, batch_dot("bik,bjk->bij", split(key_mem), split(key_mem)), 0.0).astype(BF)
    new_hidden = key_hidden - join(batch_dot("bij,bjk->bik", gram, split(back_hidden)))
    _, new_silu, new_slope = silu_parts(new_hidden)
    new_act = new_silu.astype(BF)
    pair = jnp.where(causal, batch_dot("bik,bjk->bij", split(new_act), split(key_act)), 0.0).astype(BF)
    update = dot_t(new_act, w_out_t) - join(batch_dot("bij,bjk->bik", pair, split(error)))
    after_mem = after_attn + chain_sum(update).astype(F32)

    r3 = rms(after_mem)
    n3 = (after_mem * r3 * g_ffn).astype(BF)
    gate, up = dot(n3, wg), dot(n3, wu)
    _, gate_silu, gate_slope = silu_parts(gate)
    ffn_act = (gate_silu * up).astype(BF)
    ffn_part = dot_t(ffn_act, wd_t).astype(BF)

    d_ffn = dot(d_out_low, wd_t)
    d_gate = (d_ffn * up * gate_slope).astype(BF)
    d_up = (d_ffn * gate_silu).astype(BF)
    d_n3, gw_ffn = chain_sum(
        dot_t(d_gate, wg) + dot_t(d_up, wu),
        2,
        [[(d_out_low, ffn_act)], [(n3, d_gate)], [(n3, d_up)]],
    )
    d_n3 = d_n3.astype(F32)
    gg_ffn = jnp.sum(d_n3 * after_mem * r3, axis=0)
    d_after_mem = d_out_low.astype(F32) + rms_back(after_mem, r3, g_ffn, d_n3)
    d_update = d_after_mem.astype(BF)

    d_pair = jnp.where(
        causal, -batch_dot("bik,bjk->bij", split(d_update), split(error)), 0.0
    ).astype(BF)
    d_new_act = dot(d_update, w_out_t) + join(batch_dot("bij,bjk->bik", d_pair, split(key_act)))
    d_key_act = join(batch_dot("bij,bik->bjk", d_pair, split(new_act)))
    d_new_hidden = (d_new_act * new_slope).astype(BF)
    d_gram = jnp.where(
        causal, -batch_dot("bik,bjk->bij", split(d_new_hidden), split(back_hidden)), 0.0
    ).astype(BF)
    d_back = (-join(batch_dot("bij,bik->bjk", gram, split(d_new_hidden)))).astype(BF).astype(F32)
    d_back_pre = (d_back * key_slope).astype(BF)
    slope_grad = key_s * (1.0 - key_s) * (2.0 + key_hidden * (1.0 - 2.0 * key_s))
    d_hidden_part = d_new_hidden.astype(F32) + d_back * back_pre * slope_grad
    d_error_part = dot_t(d_back_pre, w_out_t) - join(
        batch_dot("bij,bik->bjk", pair, split(d_update))
    )
    share_ffn = lax.psum_scatter(gw_ffn, "dp", scatter_dimension=0, tiled=True)
    d_error = chain_sum(d_error_part).astype(F32)
    d_rate = jnp.sum(d_error * miss, axis=1, keepdims=True)
    d_miss = (rate * d_error).astype(BF)
    d_key_act = d_key_act + dot(d_miss, w_out_t)
    d_key_hidden = (d_hidden_part + d_key_act * key_slope).astype(BF)
    d_key_part = dot_t(d_key_hidden, w_in) + join(
        batch_dot("bij,bjk->bik", d_gram, split(key_mem))
        + batch_dot("bij,bik->bjk", d_gram, split(key_mem))
    )
    d_key, gw_out_early = chain_sum(
        d_key_part, 6, [[(d_update, new_act), (error, d_back_pre)]]
    )
    d_key, ffn_part = together(d_key, ffn_part)
    ffn_own = lax.psum_scatter(ffn_part, "tensor", scatter_dimension=1, tiled=True)
    d_n2 = dot(d_key, wkm_t) - dot(d_miss, wvm_t)
    d_logit = d_rate * rate * (1.0 - rate_s)
    gg_rate = jnp.sum(n2 * d_logit, axis=0)
    d_n2 = d_n2 + d_logit * rate_w
    gg_mem = jnp.sum(d_n2 * after_attn * r2, axis=0)
    late_r2, share_ffn = together(r2, share_ffn)
    d_after_attn = d_after_mem + rms_back(after_attn, late_r2, g_mem, d_n2)
    d_attn = d_after_attn.astype(BF)

    d_mixed = dot(d_attn, wo_t).astype(BF)
    d_qkv = local_call(
        functools.partial(attend_back_kernel, slots), qkv.shape, qkv, allowed, d_mixed
    )
    d_persist_rows, d_memory_rows, d_rows = (
        d_qkv[:slots],
        d_qkv[slots : slots + count],
        d_qkv[slots + count :],
    )
    d_memory, gw_attn = chain_sum(
        dot_t(d_memory_rows[:, inner:], w_kv),
        3,
        [
            [(d_key, n2_own)],
            [(d_miss, n2_own)],
            [(d_attn, mixed)],
            [(all_rows, d_qkv)],
        ],
    )
    d_n1_part = dot_t(d_rows, w_qkv)
    d_persist_part = dot_t(d_persist_rows[:, inner:], w_kv)

    share_attn = lax.psum_scatter(gw_attn, "dp", scatter_dimension=0, tiled=True)
    d_memory, ffn_own = together(d_memory, ffn_own)
    result_own = (own(after_mem) + ffn_own.astype(F32)).astype(BF)
    result_back = exchange(t_dot(deal_m, result_own).astype(BF))
    d_read = (dot(d_memory, w_out_t) * read_slope).astype(BF)
    d_query_mem, gw_mem = chain_sum(
        dot_t(d_read, w_in),
        4,
        [
            [(key_mem, d_key_hidden), (query_mem, d_read)],
            [(d_miss, key_act), (d_memory, read_low), (gw_out_early,)],
        ],
        inner,
    )
    gw_query_mem = t_dot(d_query_mem, n1_own).astype(BF)
    gw_mem = lax.dynamic_update_slice(gw_mem, gw_query_mem, (0, 2 * hidden))
    share_mem = lax.psum_scatter(gw_mem, "dp", scatter_dimension=0, tiled=True)
    d_n1_part = d_n1_part + in_own(dot(d_query_mem, wqm_t))
    d_persist_part, share_attn = together(d_persist_part.astype(BF), share_attn)
    last = chain_sum(jnp.concatenate([d_n1_part.astype(BF), d_persist_part], axis=0), 5)
    last, result_back = together(last, result_back)
    d_n1 = last[:count].astype(F32)
    g_persist = last[count:]
    gg_attn = jnp.sum(d_n1 * x * r1, axis=0)
    d_x = d_after_attn + rms_back(x, r1, g_attn, d_n1)

    def cut(share, *widths):
        return [part.astype(F32) for part in cut_apart(share, *widths)]

    s_down, s_gate, s_up = cut(share_ffn, *[w_gate.shape[1]] * 3)
    s_key_mem, s_value_mem, s_output, s_query, s_key, s_value = cut(share_attn, *[inner] * 6)
    s_in, s_out, s_query_mem = cut(share_mem, hidden, hidden, inner)
    grad_vectors = jnp.stack([gg_attn, gg_mem, gg_ffn, gg_rate], axis=1)
    rest = jnp.concatenate(
        [
            g_persist.T,
            grad_vectors.astype(BF),
            jnp.zeros((width, 128 - slots - 4), BF),
        ],
        axis=1,
    ).reshape(ranks, -1, width)
    turned = t_dot(deal_m, d_x.astype(BF)).astype(BF).reshape(ranks, -1, width)
    came = lax.all_to_all(
        jnp.concatenate([turned, rest], axis=1), "dp", split_axis=0, concat_axis=0, tiled=True
    )
    output = line_gather(t_dot(send_m, result_back).astype(BF), 8, True)
    came, output = together(came, output)
    seats = count // ranks
    grad_tokens = t_dot(send_m, came[:, :seats].reshape(count, width)).astype(BF)
    share_rest = jnp.sum(came[:, seats:].astype(F32), axis=0).reshape(shard, -1)
    s_small = share_rest
    s_vectors = s_small[:, slots : slots + 4].T

    return (
        output,
        grad_tokens,
        s_small[:, :slots].T,
        s_vectors[0],
        s_query_mem.T,
        s_in,
        s_out.T,
        s_query,
        s_key,
        s_value,
        s_output.T,
        s_vectors[1],
        s_key_mem.T,
        -s_value_mem.T,
        s_vectors[3],
        s_vectors[2],
        s_gate,
        s_up,
        s_down.T,
    )


def solution(mesh):
    rows = P("dp", None)
    vector = P("dp")
    across = P("tensor", "dp")
    along = P("dp", "tensor")
    return jax.shard_map(
        per_device,
        mesh=mesh,
        in_specs=(
            rows,
            rows,
            vector,
            vector,
            rows,
            P(None, "dp"),
            vector,
            across,
            along,
            across,
            along,
            along,
            along,
            across,
            vector,
            across,
            across,
            vector,
            vector,
            along,
            along,
            across,
        ),
        out_specs=(
            rows,
            rows,
            P(None, "dp"),
            vector,
            across,
            along,
            across,
            along,
            along,
            along,
            across,
            vector,
            across,
            across,
            vector,
            vector,
            along,
            along,
            across,
        ),
        check_vma=False,
    )
```

```python
import functools

import jax
import jax.numpy as jnp
from jax import lax
from jax.experimental import pallas as pl
from jax.experimental.pallas import tpu as pltpu
from jax.sharding import PartitionSpec as P

HD = 96
EPSILON = 1e-06
RATE_SCALE = 8e-05
NEG_LARGE = -1e30
BF = jnp.bfloat16
F32 = jnp.float32
MESH = pl.DeviceIdType.MESH
TILE = 128
GRANT = 1 << 20


def chain_sum_kernel(pieces, layout, x_ref, *refs):
    given = sum(len(widths) for _, parts in layout for widths in parts)
    fills, refs = refs[:given], refs[given:]
    o_ref, refs = refs[0], refs[1:]
    if layout:
        g_ref, refs = refs[0], refs[1:]
    from_outer, from_inner, part, sent_a, got_up, sent_b, got_across, got_total = refs[:8]
    me = lax.axis_index("tensor")
    step = x_ref.shape[0] // pieces
    low = me < 2
    outer = jnp.logical_or(me == 0, me == 3)
    inner = jnp.logical_not(outer)
    outer_peer = jnp.where(low, 0, 3)
    inner_peer = jnp.where(low, 2, 1)
    toward = jnp.where(low, 1, 2)
    barrier = pltpu.get_barrier_semaphore()

    def tell(peer):
        pl.semaphore_signal(barrier, inc=1, device_id={"tensor": peer}, device_id_type=MESH)

    def at(piece):
        return pl.ds(pl.multiple_of(piece * step, step), step)

    def send(src, dst, send_sem, recv_sem, peer):
        return pltpu.make_async_remote_copy(
            src_ref=src,
            dst_ref=dst,
            send_sem=send_sem,
            recv_sem=recv_sem,
            device_id={"tensor": peer},
            device_id_type=MESH,
        )

    def up(p):
        return send(x_ref.at[at(p)], from_outer.at[at(p)], sent_a.at[p], got_up.at[p], toward)

    def across(p):
        return send(part.at[at(p)], from_inner.at[at(p)], sent_b.at[p], got_across.at[p], inner_peer)

    def down(p):
        return send(o_ref.at[at(p)], o_ref.at[at(p)], sent_a.at[p], got_total.at[p], outer_peer)

    def put(tile):
        stage, put_sem = refs[8], refs[9]
        rows = pl.ds(pl.multiple_of(tile * TILE, TILE), TILE)
        slot = lax.rem(tile, 2)
        target = g_ref.at[rows, pl.ds(0, stage.shape[2])]
        return pltpu.make_async_copy(stage.at[slot], target, put_sem.at[slot])

    def fill(tile):
        stage = refs[8]
        columns = pl.ds(pl.multiple_of(tile * TILE, TILE), TILE)
        slot = lax.rem(tile, 2)

        @pl.when(tile >= 2)
        def _():
            put(tile - 2).wait()

        first, offset = 0, 0
        for width, parts in layout:
            for start in range(0, width, 512):
                span = min(512, width - start)
                total, index = None, first
                for part_sizes in parts:
                    if len(part_sizes) == 1:
                        term = fills[index][columns, start : start + span].astype(F32)
                    else:
                        term = lax.dot_general(
                            fills[index][:, columns],
                            fills[index + 1][:, start : start + span],
                            (((0,), (0,)), ((), ())),
                            preferred_element_type=F32,
                        )
                    total = term if total is None else total + term
                    index += len(part_sizes)
                stage[slot, :, offset + start : offset + start + span] = total.astype(BF)
            first, offset = index, offset + width
        put(tile).start()

    @pl.when(outer)
    def _():
        tell(toward)
        pl.semaphore_wait(barrier, 1)

        @pl.loop(0, pieces)
        def _(p):
            up(p).start()

    @pl.when(inner)
    def _():
        tell(outer_peer)
        tell(inner_peer)
        pl.semaphore_wait(barrier, 2)

    def first_add(p):
        up(p).wait_recv()
        part[at(p), :] = (
            x_ref[at(p), :].astype(F32) + from_outer[at(p), :].astype(F32)
        ).astype(part.dtype)
        across(p).start()

    def second_add(p):
        across(p).wait_recv()
        o_ref[at(p), :] = (
            part[at(p), :].astype(F32) + from_inner[at(p), :].astype(F32)
        ).astype(o_ref.dtype)
        down(p).start()

    tiles = g_ref.shape[0] // TILE if layout else 0

    per, lag = 2, 2
    turns = pieces // per

    @pl.loop(0, max(turns + lag, tiles))
    def _(p):
        @pl.when(jnp.logical_and(inner, p < turns))
        def _():
            for k in range(per):
                first_add(p * per + k)

        @pl.when(jnp.logical_and(inner, jnp.logical_and(p >= lag, p < turns + lag)))
        def _():
            for k in range(per):
                second_add((p - lag) * per + k)

        if layout:

            @pl.when(p < tiles)
            def _():
                fill(p)

    if layout:
        put(tiles - 2).wait()
        put(tiles - 1).wait()

    @pl.when(outer)
    def _():
        @pl.loop(0, pieces)
        def _(p):
            down(p).wait_recv()
            up(p).wait_send()

    @pl.when(inner)
    def _():
        @pl.loop(0, pieces)
        def _(p):
            across(p).wait_send()
            down(p).wait_send()


def chain_sum(x, call_id=1, products=(), room=0):
    rows, cols = x.shape
    pieces = rows // 16
    dma = pltpu.SemaphoreType.DMA
    vmem = pl.BlockSpec(memory_space=pltpu.VMEM)
    layout = tuple(
        (pairs[0][1].shape[1], tuple((0,) * len(pair) for pair in pairs)) for pairs in products
    )
    fills = [array for pairs in products for pair in pairs for array in pair]
    out_shape = [jax.ShapeDtypeStruct((rows, cols), BF)]
    out_specs = [vmem]
    scratch = [pltpu.VMEM((rows, cols), BF)] * 3 + [dma((pieces,))] * 5
    grant = 3 * rows * cols * 2 + GRANT
    if products:
        width, high = sum(w for w, _ in layout), products[0][0][0].shape[1]
        out_shape.append(jax.ShapeDtypeStruct((high, width + room), BF))
        out_specs.append(pl.BlockSpec(memory_space=pl.ANY))
        scratch += [pltpu.VMEM((2, TILE, width), BF), dma((2,))]
        grant += 2 * TILE * width * 2 + 4 * GRANT
    out = pl.pallas_call(
        functools.partial(chain_sum_kernel, pieces, layout),
        out_shape=out_shape,
        in_specs=[vmem] * (1 + len(fills)),
        out_specs=out_specs,
        scratch_shapes=scratch,
        compiler_params=pltpu.CompilerParams(
            collective_id=call_id, has_side_effects=True, vmem_limit_bytes=grant
        ),
        cost_estimate=pl.CostEstimate(flops=0, bytes_accessed=10**8, transcendentals=0),
        name="chain_sum",
    )(x.astype(BF), *fills)
    return out if products else out[0]


def line_gather_kernel(pieces, side, x_ref, o_ref, sent, got, keep):
    me = lax.axis_index("tensor")
    high, wide = x_ref.shape
    step = high // pieces
    last = 3

    def place(block, low, size):
        if side:
            return o_ref.at[pl.ds(low, size), pl.ds(pl.multiple_of(block * wide, wide), wide)]
        return o_ref.at[pl.ds(pl.multiple_of(block * high + low, size), size)]

    barrier = pltpu.get_barrier_semaphore()
    ways = ((0, me < last, 1), (1, me > 0, -1))

    for _, open_, move in ways:

        @pl.when(open_)
        def _():
            pl.semaphore_signal(
                barrier, inc=1, device_id={"tensor": me + move}, device_id_type=MESH
            )

    at_end = jnp.logical_or(me == 0, me == last)

    @pl.when(at_end)
    def _():
        pl.semaphore_wait(barrier, 1)

    @pl.when(jnp.logical_not(at_end))
    def _():
        pl.semaphore_wait(barrier, 2)

    def copy(way, hop, piece, move, block, first=False):
        there = place(block, piece * step, step)
        return pltpu.make_async_remote_copy(
            src_ref=x_ref.at[pl.ds(piece * step, step)] if first else there,
            dst_ref=there,
            send_sem=sent.at[way, hop, piece],
            recv_sem=got.at[way, hop, piece],
            device_id={"tensor": jnp.clip(me + move, 0, last)},
            device_id_type=MESH,
        )

    def forward(way, move, hop):
        block = me - move * hop
        return jnp.logical_and(
            jnp.logical_and(me + move >= 0, me + move <= last),
            jnp.logical_and(block >= 0, block <= last),
        )

    def comes(way, move, hop):
        block = me - move * (hop + 1)
        return jnp.logical_and(block >= 0, block <= last)

    def own():
        return pltpu.make_async_copy(x_ref, place(me, 0, high), keep.at[0])

    for hop in range(last):
        for piece in range(pieces):
            for way, _, move in ways:

                @pl.when(forward(way, move, hop))
                def _():
                    copy(way, hop, piece, move, me - move * hop, hop == 0).start()

        if hop == 0:
            own().start()
        for piece in range(pieces):
            for way, _, move in ways:

                @pl.when(comes(way, move, hop))
                def _():
                    copy(way, hop, piece, move, me - move * (hop + 1)).wait_recv()

    own().wait()
    for hop in range(last):
        for piece in range(pieces):
            for way, _, move in ways:

                @pl.when(forward(way, move, hop))
                def _():
                    copy(way, hop, piece, move, me - move * hop, hop == 0).wait_send()


def line_gather(x, call_id, side=False, pieces=4):
    rows, cols = x.shape
    shape = (rows, 4 * cols) if side else (4 * rows, cols)
    dma = pltpu.SemaphoreType.DMA
    vmem = pl.BlockSpec(memory_space=pltpu.VMEM)
    return pl.pallas_call(
        functools.partial(line_gather_kernel, pieces, side),
        out_shape=jax.ShapeDtypeStruct(shape, BF),
        in_specs=[vmem],
        out_specs=vmem,
        scratch_shapes=[dma((2, 3, pieces)), dma((2, 3, pieces)), dma((1,))],
        compiler_params=pltpu.CompilerParams(
            collective_id=call_id, has_side_effects=True, vmem_limit_bytes=GRANT
        ),
        cost_estimate=pl.CostEstimate(flops=0, bytes_accessed=5 * 10**7, transcendentals=0),
        name="line_gather",
    )(x)


def dot(left, right):
    return lax.dot_general(left, right, (((1,), (0,)), ((), ())), preferred_element_type=F32)


def dot_t(left, right):
    return lax.dot_general(left, right, (((1,), (1,)), ((), ())), preferred_element_type=F32)


def t_dot(left, right):
    return lax.dot_general(left, right, (((0,), (0,)), ((), ())), preferred_element_type=F32)


def batch_dot(spec, left, right):
    return jnp.einsum(spec, left, right, preferred_element_type=F32)


def cut_apart(whole, *widths):
    out, low = [], 0
    for width in widths:
        out.append(whole[:, low : low + width])
        low += width
    return out


def by_head(v, heads):
    column = lax.broadcasted_iota(jnp.int32, v.shape, 1)
    zero = jnp.zeros_like(v)
    return jnp.concatenate(
        [
            jnp.where(jnp.logical_and(column >= h * HD, column < (h + 1) * HD), v, zero)
            for h in range(heads)
        ],
        axis=0,
    )


def from_heads(v, heads):
    rows = v.shape[0] // heads
    column = lax.broadcasted_iota(jnp.int32, (rows, v.shape[1]), 1)
    out = jnp.zeros((rows, v.shape[1]), v.dtype)
    for h in range(heads):
        here = jnp.logical_and(column >= h * HD, column < (h + 1) * HD)
        out = jnp.where(here, v[h * rows : (h + 1) * rows], out)
    return out


def batch_parts(qkv_ref, mask_ref, batch, slots):
    batches, rows, _ = mask_ref.shape
    inner = qkv_ref.shape[1] // 3
    heads = inner // HD
    mem = slots + batch * rows
    tok = slots + (batches + batch) * rows

    def context(low):
        cols = slice(low, low + inner)
        return jnp.concatenate(
            [qkv_ref[:slots, cols], qkv_ref[mem : mem + rows, cols], qkv_ref[tok : tok + rows, cols]],
            axis=0,
        )

    query = by_head(qkv_ref[tok : tok + rows, :inner], heads)
    keys, values = context(inner), context(2 * inner)
    scores = dot_t(query, keys) * HD ** (-0.5)
    allowed = jnp.concatenate([mask_ref[batch]] * heads, axis=0)
    scores = jnp.where(allowed > 0.5, scores, NEG_LARGE)
    high = jnp.max(scores, axis=1, keepdims=True)
    raised = jnp.exp(scores - high)
    weights = raised / jnp.sum(raised, axis=1, keepdims=True)
    return query, keys, values, weights, heads


def attend_kernel(slots, qkv_ref, mask_ref, o_ref):
    batches, rows, _ = mask_ref.shape
    for batch in range(batches):
        _, _, values, weights, heads = batch_parts(qkv_ref, mask_ref, batch, slots)
        mixed = from_heads(dot(weights.astype(BF), values), heads)
        o_ref[batch * rows : (batch + 1) * rows, :] = mixed.astype(BF)


def attend_back_kernel(slots, qkv_ref, mask_ref, d_ref, o_ref):
    batches, rows, _ = mask_ref.shape
    inner = d_ref.shape[1]
    o_ref[: slots + batches * rows, :inner] = jnp.zeros((slots + batches * rows, inner), BF)
    d_keys_p, d_values_p = jnp.zeros((slots, inner), F32), jnp.zeros((slots, inner), F32)
    for batch in range(batches):
        query, keys, values, weights, heads = batch_parts(qkv_ref, mask_ref, batch, slots)
        mem = slots + batch * rows
        tok = slots + (batches + batch) * rows
        d_mixed = by_head(d_ref[batch * rows : (batch + 1) * rows, :], heads)
        d_weights = dot_t(d_mixed, values)
        d_values = t_dot(weights.astype(BF), d_mixed)
        even = jnp.sum(weights * d_weights, axis=1, keepdims=True)
        d_scores = (weights * (d_weights - even)).astype(BF)
        d_query = from_heads(dot(d_scores, keys), heads) * HD ** (-0.5)
        d_keys = t_dot(d_scores, query) * HD ** (-0.5)
        o_ref[tok : tok + rows, :inner] = d_query.astype(BF)
        d_keys_p, d_values_p = d_keys_p + d_keys[:slots], d_values_p + d_values[:slots]
        for low, grad in ((inner, d_keys), (2 * inner, d_values)):
            o_ref[mem : mem + rows, low : low + inner] = grad[slots : slots + rows].astype(BF)
            o_ref[tok : tok + rows, low : low + inner] = grad[slots + rows :].astype(BF)
    o_ref[:slots, inner : 2 * inner] = d_keys_p.astype(BF)
    o_ref[:slots, 2 * inner :] = d_values_p.astype(BF)


def local_call(body, shape, *operands):
    vmem = pl.BlockSpec(memory_space=pltpu.VMEM)
    return pl.pallas_call(
        body,
        out_shape=jax.ShapeDtypeStruct(shape, BF),
        in_specs=[vmem] * len(operands),
        out_specs=vmem,
        compiler_params=pltpu.CompilerParams(vmem_limit_bytes=16 * GRANT),
        cost_estimate=pl.CostEstimate(flops=0, bytes_accessed=2 * 10**7, transcendentals=0),
        name="attend",
    )(*operands)


def together(*values):
    return lax.optimization_barrier(values)


def rms(v):
    return lax.rsqrt(jnp.mean(v * v, axis=-1, keepdims=True) + EPSILON)


def rms_back(v, r, gain, grad):
    scaled = grad * gain
    inner = jnp.sum(scaled * v, axis=-1, keepdims=True)
    return r * scaled - v * (r * r * r) * (inner / v.shape[-1])


def silu_parts(z):
    s = jax.nn.sigmoid(z)
    return s, z * s, s * (1.0 + z * (1.0 - s))


def per_device(
    tokens,
    cotangent,
    dest,
    source,
    lengths,
    persist,
    gain_attn,
    w_query_mem,
    mem_in,
    mem_out,
    w_query,
    w_key,
    w_value,
    w_output,
    gain_mem,
    w_key_mem,
    w_value_mem,
    w_rate,
    gain_ffn,
    w_gate,
    w_up,
    w_down,
):
    count, width = tokens.shape
    shard = gain_attn.shape[0]
    ranks = width // shard
    batches, _ = lengths.shape
    rows = count // batches
    hidden = mem_in.shape[1]
    inner = w_query.shape[1]
    heads = inner // HD
    slots = persist.shape[0]
    me = lax.axis_index("tensor")

    def gather_whole(*parts):
        return lax.all_gather(jnp.concatenate(parts, axis=1), "dp", axis=0, tiled=True)

    def gather(*parts):
        return cut_apart(gather_whole(*parts), *[part.shape[1] for part in parts])

    vectors = jnp.stack([gain_attn, gain_mem, gain_ffn, w_rate], axis=1)
    pad = jnp.zeros((shard, 128 - slots - 4), BF)
    small = jnp.concatenate([persist.T, vectors, pad], axis=1)
    tall = line_gather(jnp.concatenate([w_key_mem, w_value_mem], axis=1), 7)
    place = jnp.arange(count, dtype=jnp.int32)
    home = dest // count
    earlier = (home[None, :] == home[:, None]) & (place[None, :] < place[:, None])
    sent_at = home * (count // ranks) + jnp.sum(earlier.astype(jnp.int32), axis=1)
    came_at = jnp.sum((source[None, :] < source[:, None]).astype(jnp.int32), axis=1)
    send_m = (sent_at[None, :] == place[:, None]).astype(BF)
    deal_m = (came_at[:, None] == place[None, :]).astype(BF)

    def exchange(v):
        return lax.all_to_all(v, "dp", split_axis=0, concat_axis=0, tiled=True)

    def fold(v):
        return v.reshape(width // v.shape[-1], -1, v.shape[-1]).swapaxes(0, 1).reshape(-1, width)

    def unfold(v, columns):
        return v.reshape(-1, width // columns, columns).swapaxes(0, 1).reshape(-1, columns)

    w_in, w_out_t = gather(mem_in, mem_out.T)
    seats = count // ranks
    leaving = dot(send_m, tokens).astype(BF).reshape(ranks, seats, width)
    same = jnp.concatenate([fold(w_query_mem.T), fold(small)], axis=0)
    high = seats + shard * w_query_mem.shape[0] // width
    arrived, tall = together(
        exchange(jnp.concatenate([leaving, jnp.broadcast_to(same, (ranks,) + same.shape)], axis=1)),
        tall,
    )
    dealt = dot(deal_m, arrived[:, :seats].reshape(count, width)).astype(BF)
    wqm_t = jax.vmap(lambda v: unfold(v, inner))(arrived[:, seats:high]).reshape(width, inner)
    small = jax.vmap(lambda v: unfold(v, 128))(arrived[:, high:]).reshape(width, 128)
    persistent = small[:, :slots].T
    gains = small[:, slots : slots + 4].astype(F32).T
    g_attn, g_mem, g_ffn, rate_w = (gains[i][None, :] for i in range(4))

    x = dealt.astype(F32)

    position = jnp.arange(rows, dtype=jnp.int32)
    turn = jnp.arange(lengths.shape[1])
    bounds = jnp.sum(
        jnp.where(turn[:, None] <= turn[None, :], lengths[:, :, None], 0), axis=1, dtype=jnp.int32
    )
    segment = jnp.sum((position[None, :, None] >= bounds[:, None, :]).astype(jnp.int32), axis=2)
    causal = (segment[:, :, None] == segment[:, None, :]) & (
        position[None, None, :] <= position[None, :, None]
    )

    def split(v):
        return v.reshape(batches, rows, v.shape[-1])

    def join(v):
        return v.reshape(count, v.shape[-1])

    def own(v):
        return lax.dynamic_slice_in_dim(v, me * inner, inner, 1)

    def in_own(v):
        return lax.dynamic_update_slice_in_dim(
            jnp.zeros((v.shape[0], width), v.dtype), v, me * inner, 1
        )

    r1 = rms(x)
    n1, late_query, late_key, late_value, late_output = together(
        (x * r1 * g_attn).astype(BF), w_query, w_key, w_value, w_output
    )
    w_attn = gather_whole(late_query, late_key, late_value, late_output.T)
    n1_own = own(n1)
    query_mem = chain_sum(dot_t(n1_own, wqm_t))
    query_mem, tall = together(query_mem, tall)
    wkm_t, wvm_t = gather(tall[:, :shard].T, tall[:, shard:].T)
    read_s, read_act, read_slope = silu_parts(dot(query_mem, w_in))
    read_low = read_act.astype(BF)
    memory = chain_sum(dot_t(read_low, w_out_t))
    memory, w_attn = together(memory, w_attn)
    w_qkv, wo_t = cut_apart(w_attn, 3 * inner, inner)
    w_kv = w_attn[:, inner : 3 * inner]
    (all_rows,) = together(jnp.concatenate([persistent, memory, n1], axis=0))
    qkv = dot(all_rows, w_qkv).astype(BF)
    allowed = jnp.concatenate(
        [jnp.ones((batches, rows, slots), F32), causal.astype(F32), causal.astype(F32)], axis=2
    )
    mixed = local_call(functools.partial(attend_kernel, slots), (count, inner), qkv, allowed)
    mixed, late_gate, late_up, late_down, later = together(mixed, w_gate, w_up, w_down, cotangent)
    cotangent_arrived = exchange(dot(send_m, later).astype(BF))
    wg, wu, wd_t = gather(late_gate, late_up, late_down.T)
    attended, cotangent_arrived = together(chain_sum(dot_t(mixed, wo_t)), cotangent_arrived)
    after_attn = x + attended.astype(F32)
    d_out_low = dot(deal_m, cotangent_arrived).astype(BF)

    r2 = rms(after_attn)
    n2 = after_attn * r2 * g_mem
    rate_s = jax.nn.sigmoid(jnp.sum(n2 * rate_w, axis=1, keepdims=True))
    rate = RATE_SCALE * rate_s
    n2_low = n2.astype(BF)
    n2_own = own(n2_low)
    key_mem = dot_t(n2_low, wkm_t).astype(BF)
    value_part = dot_t(n2_own, own(wvm_t))
    key_hidden = dot(key_mem, w_in)
    key_s, key_silu, key_slope = silu_parts(key_hidden)
    key_act = key_silu.astype(BF)
    miss = chain_sum(dot_t(key_act, w_out_t) - value_part).astype(F32)
    error = (rate * miss).astype(BF)
    back_pre = dot(error, w_out_t)
    back_hidden = (back_pre * key_slope).astype(BF)
    gram = jnp.where(causal, batch_dot("bik,bjk->bij", split(key_mem), split(key_mem)), 0.0).astype(BF)
    new_hidden = key_hidden - join(batch_dot("bij,bjk->bik", gram, split(back_hidden)))
    _, new_silu, new_slope = silu_parts(new_hidden)
    new_act = new_silu.astype(BF)
    pair = jnp.where(causal, batch_dot("bik,bjk->bij", split(new_act), split(key_act)), 0.0).astype(BF)
    update = dot_t(new_act, w_out_t) - join(batch_dot("bij,bjk->bik", pair, split(error)))
    after_mem = after_attn + chain_sum(update).astype(F32)

    r3 = rms(after_mem)
    n3 = (after_mem * r3 * g_ffn).astype(BF)
    gate, up = dot(n3, wg), dot(n3, wu)
    _, gate_silu, gate_slope = silu_parts(gate)
    ffn_act = (gate_silu * up).astype(BF)
    ffn_part = dot_t(ffn_act, wd_t).astype(BF)

    d_ffn = dot(d_out_low, wd_t)
    d_gate = (d_ffn * up * gate_slope).astype(BF)
    d_up, ffn_part = together((d_ffn * gate_silu).astype(BF), ffn_part)
    d_n3, gw_ffn = chain_sum(
        dot_t(d_gate, wg) + dot_t(d_up, wu),
        2,
        [[(d_out_low, ffn_act)], [(n3, d_gate)], [(n3, d_up)]],
    )
    d_n3 = d_n3.astype(F32)
    gg_ffn = jnp.sum(d_n3 * after_mem * r3, axis=0)
    d_after_mem = d_out_low.astype(F32) + rms_back(after_mem, r3, g_ffn, d_n3)
    d_update = d_after_mem.astype(BF)

    d_pair = jnp.where(
        causal, -batch_dot("bik,bjk->bij", split(d_update), split(error)), 0.0
    ).astype(BF)
    d_new_act = dot(d_update, w_out_t) + join(batch_dot("bij,bjk->bik", d_pair, split(key_act)))
    d_key_act = join(batch_dot("bij,bik->bjk", d_pair, split(new_act)))
    d_new_hidden = (d_new_act * new_slope).astype(BF)
    d_gram = jnp.where(
        causal, -batch_dot("bik,bjk->bij", split(d_new_hidden), split(back_hidden)), 0.0
    ).astype(BF)
    d_back = (-join(batch_dot("bij,bik->bjk", gram, split(d_new_hidden)))).astype(BF).astype(F32)
    d_back_pre = (d_back * key_slope).astype(BF)
    slope_grad = key_s * (1.0 - key_s) * (2.0 + key_hidden * (1.0 - 2.0 * key_s))
    d_hidden_part = d_new_hidden.astype(F32) + d_back * back_pre * slope_grad
    d_error_part = dot_t(d_back_pre, w_out_t) - join(
        batch_dot("bij,bik->bjk", pair, split(d_update))
    )
    share_ffn = lax.psum_scatter(gw_ffn, "dp", scatter_dimension=0, tiled=True)
    d_error = chain_sum(d_error_part).astype(F32)
    d_rate = jnp.sum(d_error * miss, axis=1, keepdims=True)
    d_miss = (rate * d_error).astype(BF)
    d_key_act = d_key_act + dot(d_miss, w_out_t)
    d_key_hidden = (d_hidden_part + d_key_act * key_slope).astype(BF)
    d_key_part = dot_t(d_key_hidden, w_in) + join(
        batch_dot("bij,bjk->bik", d_gram, split(key_mem))
        + batch_dot("bij,bik->bjk", d_gram, split(key_mem))
    )
    d_key, gw_out_early = chain_sum(
        d_key_part, 6, [[(d_update, new_act), (error, d_back_pre)]]
    )
    d_key, ffn_part = together(d_key, ffn_part)
    ffn_own = lax.psum_scatter(ffn_part, "tensor", scatter_dimension=1, tiled=True)
    d_n2 = dot(d_key, wkm_t) - dot(d_miss, wvm_t)
    d_logit = d_rate * rate * (1.0 - rate_s)
    gg_rate = jnp.sum(n2 * d_logit, axis=0)
    d_n2 = d_n2 + d_logit * rate_w
    gg_mem = jnp.sum(d_n2 * after_attn * r2, axis=0)
    late_r2, share_ffn = together(r2, share_ffn)
    d_after_attn = d_after_mem + rms_back(after_attn, late_r2, g_mem, d_n2)
    d_attn = d_after_attn.astype(BF)

    d_mixed = dot(d_attn, wo_t).astype(BF)
    d_qkv = local_call(
        functools.partial(attend_back_kernel, slots), qkv.shape, qkv, allowed, d_mixed
    )
    d_persist_rows, d_memory_rows, d_rows = (
        d_qkv[:slots],
        d_qkv[slots : slots + count],
        d_qkv[slots + count :],
    )
    d_memory, gw_attn = chain_sum(
        dot_t(d_memory_rows[:, inner:], w_kv),
        3,
        [
            [(d_key, n2_own)],
            [(d_miss, n2_own)],
            [(d_attn, mixed)],
            [(all_rows, d_qkv)],
        ],
    )
    d_n1_part = dot_t(d_rows, w_qkv)
    d_persist_part = dot_t(d_persist_rows[:, inner:], w_kv)

    share_attn = lax.psum_scatter(gw_attn, "dp", scatter_dimension=0, tiled=True)
    d_memory, ffn_own = together(d_memory, ffn_own)
    result_own = (own(after_mem) + ffn_own.astype(F32)).astype(BF)
    result_back = exchange(t_dot(deal_m, result_own).astype(BF))
    d_read = (dot(d_memory, w_out_t) * read_slope).astype(BF)
    d_query_mem, gw_mem = chain_sum(
        dot_t(d_read, w_in),
        4,
        [
            [(key_mem, d_key_hidden), (query_mem, d_read)],
            [(d_miss, key_act), (d_memory, read_low), (gw_out_early,)],
        ],
        inner,
    )
    gw_query_mem = t_dot(d_query_mem, n1_own).astype(BF)
    gw_mem = lax.dynamic_update_slice(gw_mem, gw_query_mem, (0, 2 * hidden))
    share_mem = lax.psum_scatter(gw_mem, "dp", scatter_dimension=0, tiled=True)
    d_n1_part = d_n1_part + in_own(dot(d_query_mem, wqm_t))
    d_persist_part, share_attn = together(d_persist_part.astype(BF), share_attn)
    last = chain_sum(jnp.concatenate([d_n1_part.astype(BF), d_persist_part], axis=0), 5)
    last, result_back = together(last, result_back)
    d_n1 = last[:count].astype(F32)
    g_persist = last[count:]
    gg_attn = jnp.sum(d_n1 * x * r1, axis=0)
    d_x = d_after_attn + rms_back(x, r1, g_attn, d_n1)

    def cut(share, *widths):
        return [part.astype(F32) for part in cut_apart(share, *widths)]

    s_down, s_gate, s_up = cut(share_ffn, *[w_gate.shape[1]] * 3)
    s_key_mem, s_value_mem, s_output, s_query, s_key, s_value = cut(share_attn, *[inner] * 6)
    s_in, s_out, s_query_mem = cut(share_mem, hidden, hidden, inner)
    grad_vectors = jnp.stack([gg_attn, gg_mem, gg_ffn, gg_rate], axis=1)
    rest = jnp.concatenate(
        [
            g_persist.T,
            grad_vectors.astype(BF),
            jnp.zeros((width, 128 - slots - 4), BF),
        ],
        axis=1,
    ).reshape(ranks, shard, -1)
    rest = jax.vmap(fold)(rest)
    turned = t_dot(deal_m, d_x.astype(BF)).astype(BF).reshape(ranks, -1, width)
    came = lax.all_to_all(
        jnp.concatenate([turned, rest], axis=1), "dp", split_axis=0, concat_axis=0, tiled=True
    )
    output = line_gather(t_dot(send_m, result_back).astype(BF), 8, True)
    came, output = together(came, output)
    grad_tokens = t_dot(send_m, came[:, :seats].reshape(count, width)).astype(BF)
    share_rest = unfold(jnp.sum(came[:, seats:].astype(F32), axis=0), 128)
    s_small = share_rest
    s_vectors = s_small[:, slots : slots + 4].T

    return (
        output,
        grad_tokens,
        s_small[:, :slots].T,
        s_vectors[0],
        s_query_mem.T,
        s_in,
        s_out.T,
        s_query,
        s_key,
        s_value,
        s_output.T,
        s_vectors[1],
        s_key_mem.T,
        -s_value_mem.T,
        s_vectors[3],
        s_vectors[2],
        s_gate,
        s_up,
        s_down.T,
    )


def solution(mesh):
    rows = P("dp", None)
    vector = P("dp")
    across = P("tensor", "dp")
    along = P("dp", "tensor")
    return jax.shard_map(
        per_device,
        mesh=mesh,
        in_specs=(
            rows,
            rows,
            vector,
            vector,
            rows,
            P(None, "dp"),
            vector,
            across,
            along,
            across,
            along,
            along,
            along,
            across,
            vector,
            across,
            across,
            vector,
            vector,
            along,
            along,
            across,
        ),
        out_specs=(
            rows,
            rows,
            P(None, "dp"),
            vector,
            across,
            along,
            across,
            along,
            along,
            along,
            across,
            vector,
            across,
            across,
            vector,
            vector,
            along,
            along,
            across,
        ),
        check_vma=False,
    )
```

```python
import functools

import jax
import jax.numpy as jnp
from jax import lax
from jax.experimental import pallas as pl
from jax.experimental.pallas import tpu as pltpu
from jax.sharding import PartitionSpec as P

HD = 96
EPSILON = 1e-06
RATE_SCALE = 8e-05
NEG_LARGE = -1e30
BF = jnp.bfloat16
F32 = jnp.float32
MESH = pl.DeviceIdType.MESH
TILE = 128
GRANT = 1 << 20


def chain_sum_kernel(pieces, layout, x_ref, *refs):
    given = sum(len(widths) for _, parts in layout for widths in parts)
    fills, refs = refs[:given], refs[given:]
    o_ref, refs = refs[0], refs[1:]
    if layout:
        g_ref, refs = refs[0], refs[1:]
    from_outer, from_inner, part, sent_a, got_up, sent_b, got_across, got_total = refs[:8]
    me = lax.axis_index("tensor")
    step = x_ref.shape[0] // pieces
    low = me < 2
    outer = jnp.logical_or(me == 0, me == 3)
    inner = jnp.logical_not(outer)
    outer_peer = jnp.where(low, 0, 3)
    inner_peer = jnp.where(low, 2, 1)
    toward = jnp.where(low, 1, 2)
    barrier = pltpu.get_barrier_semaphore()

    def tell(peer):
        pl.semaphore_signal(barrier, inc=1, device_id={"tensor": peer}, device_id_type=MESH)

    def at(piece):
        return pl.ds(pl.multiple_of(piece * step, step), step)

    def send(src, dst, send_sem, recv_sem, peer):
        return pltpu.make_async_remote_copy(
            src_ref=src,
            dst_ref=dst,
            send_sem=send_sem,
            recv_sem=recv_sem,
            device_id={"tensor": peer},
            device_id_type=MESH,
        )

    def up(p):
        return send(x_ref.at[at(p)], from_outer.at[at(p)], sent_a.at[p], got_up.at[p], toward)

    def across(p):
        return send(part.at[at(p)], from_inner.at[at(p)], sent_b.at[p], got_across.at[p], inner_peer)

    def down(p):
        return send(o_ref.at[at(p)], o_ref.at[at(p)], sent_a.at[p], got_total.at[p], outer_peer)

    def put(tile):
        stage, put_sem = refs[8], refs[9]
        rows = pl.ds(pl.multiple_of(tile * TILE, TILE), TILE)
        slot = lax.rem(tile, 2)
        return pltpu.make_async_copy(stage.at[slot], g_ref.at[rows], put_sem.at[slot])

    def fill(tile):
        stage = refs[8]
        columns = pl.ds(pl.multiple_of(tile * TILE, TILE), TILE)
        slot = lax.rem(tile, 2)

        @pl.when(tile >= 2)
        def _():
            put(tile - 2).wait()

        first, offset = 0, 0
        for width, parts in layout:
            for start in range(0, width, 512):
                span = min(512, width - start)
                total, index = None, first
                for part_sizes in parts:
                    if len(part_sizes) == 1:
                        term = fills[index][columns, start : start + span].astype(F32)
                    else:
                        term = lax.dot_general(
                            fills[index][:, columns],
                            fills[index + 1][:, start : start + span],
                            (((0,), (0,)), ((), ())),
                            preferred_element_type=F32,
                        )
                    total = term if total is None else total + term
                    index += len(part_sizes)
                stage[slot, :, offset + start : offset + start + span] = total.astype(BF)
            first, offset = index, offset + width
        put(tile).start()

    @pl.when(outer)
    def _():
        tell(toward)
        pl.semaphore_wait(barrier, 1)

        @pl.loop(0, pieces)
        def _(p):
            up(p).start()

    @pl.when(inner)
    def _():
        tell(outer_peer)
        tell(inner_peer)
        pl.semaphore_wait(barrier, 2)

    def first_add(p):
        up(p).wait_recv()
        part[at(p), :] = (
            x_ref[at(p), :].astype(F32) + from_outer[at(p), :].astype(F32)
        ).astype(part.dtype)
        across(p).start()

    def second_add(p):
        across(p).wait_recv()
        o_ref[at(p), :] = (
            part[at(p), :].astype(F32) + from_inner[at(p), :].astype(F32)
        ).astype(o_ref.dtype)
        down(p).start()

    tiles = g_ref.shape[0] // TILE if layout else 0

    per, lag = 2, 2
    turns = pieces // per

    @pl.loop(0, max(turns + lag, tiles))
    def _(p):
        @pl.when(jnp.logical_and(inner, p < turns))
        def _():
            for k in range(per):
                first_add(p * per + k)

        @pl.when(jnp.logical_and(inner, jnp.logical_and(p >= lag, p < turns + lag)))
        def _():
            for k in range(per):
                second_add((p - lag) * per + k)

        if layout:

            @pl.when(p < tiles)
            def _():
                fill(p)

    if layout:
        put(tiles - 2).wait()
        put(tiles - 1).wait()

    @pl.when(outer)
    def _():
        @pl.loop(0, pieces)
        def _(p):
            down(p).wait_recv()
            up(p).wait_send()

    @pl.when(inner)
    def _():
        @pl.loop(0, pieces)
        def _(p):
            across(p).wait_send()
            down(p).wait_send()


def chain_sum(x, call_id=1, products=(), near=False):
    rows, cols = x.shape
    pieces = rows // 16
    dma = pltpu.SemaphoreType.DMA
    vmem = pl.BlockSpec(memory_space=pltpu.VMEM)
    layout = tuple(
        (pairs[0][1].shape[1], tuple((0,) * len(pair) for pair in pairs)) for pairs in products
    )
    fills = [array for pairs in products for pair in pairs for array in pair]
    out_shape = [jax.ShapeDtypeStruct((rows, cols), BF)]
    out_specs = [vmem]
    scratch = [pltpu.VMEM((rows, cols), BF)] * 3 + [dma((pieces,))] * 5
    grant = 3 * rows * cols * 2 + GRANT
    if products:
        width, high = sum(w for w, _ in layout), products[0][0][0].shape[1]
        out_shape.append(jax.ShapeDtypeStruct((high, width), BF))
        out_specs.append(pl.BlockSpec(memory_space=pl.ANY if near else pltpu.HBM))
        scratch += [pltpu.VMEM((2, TILE, width), BF), dma((2,))]
        grant += 2 * TILE * width * 2 + 4 * GRANT
    out = pl.pallas_call(
        functools.partial(chain_sum_kernel, pieces, layout),
        out_shape=out_shape,
        in_specs=[vmem] * (1 + len(fills)),
        out_specs=out_specs,
        scratch_shapes=scratch,
        compiler_params=pltpu.CompilerParams(
            collective_id=call_id, has_side_effects=True, vmem_limit_bytes=grant
        ),
        cost_estimate=pl.CostEstimate(flops=0, bytes_accessed=10**8, transcendentals=0),
        name="chain_sum",
    )(x.astype(BF), *fills)
    return out if products else out[0]


def line_gather_kernel(pieces, side, x_ref, o_ref, sent, got, keep):
    me = lax.axis_index("tensor")
    high, wide = x_ref.shape
    step = high // pieces
    last = 3

    def place(block, low, size):
        if side:
            return o_ref.at[pl.ds(low, size), pl.ds(pl.multiple_of(block * wide, wide), wide)]
        return o_ref.at[pl.ds(pl.multiple_of(block * high + low, size), size)]

    barrier = pltpu.get_barrier_semaphore()
    ways = ((0, me < last, 1), (1, me > 0, -1))

    for _, open_, move in ways:

        @pl.when(open_)
        def _():
            pl.semaphore_signal(
                barrier, inc=1, device_id={"tensor": me + move}, device_id_type=MESH
            )

    at_end = jnp.logical_or(me == 0, me == last)

    @pl.when(at_end)
    def _():
        pl.semaphore_wait(barrier, 1)

    @pl.when(jnp.logical_not(at_end))
    def _():
        pl.semaphore_wait(barrier, 2)

    def copy(way, hop, piece, move, block, first=False):
        there = place(block, piece * step, step)
        return pltpu.make_async_remote_copy(
            src_ref=x_ref.at[pl.ds(piece * step, step)] if first else there,
            dst_ref=there,
            send_sem=sent.at[way, hop, piece],
            recv_sem=got.at[way, hop, piece],
            device_id={"tensor": jnp.clip(me + move, 0, last)},
            device_id_type=MESH,
        )

    def forward(way, move, hop):
        block = me - move * hop
        return jnp.logical_and(
            jnp.logical_and(me + move >= 0, me + move <= last),
            jnp.logical_and(block >= 0, block <= last),
        )

    def comes(way, move, hop):
        block = me - move * (hop + 1)
        return jnp.logical_and(block >= 0, block <= last)

    def own():
        return pltpu.make_async_copy(x_ref, place(me, 0, high), keep.at[0])

    for hop in range(last):
        for piece in range(pieces):
            for way, _, move in ways:

                @pl.when(forward(way, move, hop))
                def _():
                    copy(way, hop, piece, move, me - move * hop, hop == 0).start()

        if hop == 0:
            own().start()
        for piece in range(pieces):
            for way, _, move in ways:

                @pl.when(comes(way, move, hop))
                def _():
                    copy(way, hop, piece, move, me - move * (hop + 1)).wait_recv()

    own().wait()
    for hop in range(last):
        for piece in range(pieces):
            for way, _, move in ways:

                @pl.when(forward(way, move, hop))
                def _():
                    copy(way, hop, piece, move, me - move * hop, hop == 0).wait_send()


def line_gather(x, call_id, side=False, pieces=2):
    rows, cols = x.shape
    shape = (rows, 4 * cols) if side else (4 * rows, cols)
    dma = pltpu.SemaphoreType.DMA
    vmem = pl.BlockSpec(memory_space=pltpu.VMEM)
    return pl.pallas_call(
        functools.partial(line_gather_kernel, pieces, side),
        out_shape=jax.ShapeDtypeStruct(shape, BF),
        in_specs=[vmem],
        out_specs=vmem,
        scratch_shapes=[dma((2, 3, pieces)), dma((2, 3, pieces)), dma((1,))],
        compiler_params=pltpu.CompilerParams(
            collective_id=call_id, has_side_effects=True, vmem_limit_bytes=GRANT
        ),
        cost_estimate=pl.CostEstimate(flops=0, bytes_accessed=5 * 10**7, transcendentals=0),
        name="line_gather",
    )(x)


def dot(left, right):
    return lax.dot_general(left, right, (((1,), (0,)), ((), ())), preferred_element_type=F32)


def dot_t(left, right):
    return lax.dot_general(left, right, (((1,), (1,)), ((), ())), preferred_element_type=F32)


def t_dot(left, right):
    return lax.dot_general(left, right, (((0,), (0,)), ((), ())), preferred_element_type=F32)


def batch_dot(spec, left, right):
    return jnp.einsum(spec, left, right, preferred_element_type=F32)


def cut_apart(whole, *widths):
    out, low = [], 0
    for width in widths:
        out.append(whole[:, low : low + width])
        low += width
    return out


def by_head(v, heads):
    column = lax.broadcasted_iota(jnp.int32, v.shape, 1)
    zero = jnp.zeros_like(v)
    return jnp.concatenate(
        [
            jnp.where(jnp.logical_and(column >= h * HD, column < (h + 1) * HD), v, zero)
            for h in range(heads)
        ],
        axis=0,
    )


def from_heads(v, heads):
    rows = v.shape[0] // heads
    column = lax.broadcasted_iota(jnp.int32, (rows, v.shape[1]), 1)
    out = jnp.zeros((rows, v.shape[1]), v.dtype)
    for h in range(heads):
        here = jnp.logical_and(column >= h * HD, column < (h + 1) * HD)
        out = jnp.where(here, v[h * rows : (h + 1) * rows], out)
    return out


def batch_parts(qkv_ref, mask_ref, batch, slots):
    batches, rows, _ = mask_ref.shape
    inner = qkv_ref.shape[1] // 3
    heads = inner // HD
    mem = slots + batch * rows
    tok = slots + (batches + batch) * rows

    def context(low):
        cols = slice(low, low + inner)
        return jnp.concatenate(
            [qkv_ref[:slots, cols], qkv_ref[mem : mem + rows, cols], qkv_ref[tok : tok + rows, cols]],
            axis=0,
        )

    query = by_head(qkv_ref[tok : tok + rows, :inner], heads)
    keys, values = context(inner), context(2 * inner)
    scores = dot_t(query, keys) * HD ** (-0.5)
    allowed = jnp.concatenate([mask_ref[batch]] * heads, axis=0)
    scores = jnp.where(allowed > 0.5, scores, NEG_LARGE)
    high = jnp.max(scores, axis=1, keepdims=True)
    raised = jnp.exp(scores - high)
    weights = raised / jnp.sum(raised, axis=1, keepdims=True)
    return query, keys, values, weights, heads


def attend_kernel(slots, qkv_ref, mask_ref, o_ref):
    batches, rows, _ = mask_ref.shape
    for batch in range(batches):
        _, _, values, weights, heads = batch_parts(qkv_ref, mask_ref, batch, slots)
        mixed = from_heads(dot(weights.astype(BF), values), heads)
        o_ref[batch * rows : (batch + 1) * rows, :] = mixed.astype(BF)


def attend_back_kernel(slots, qkv_ref, mask_ref, d_ref, o_ref):
    batches, rows, _ = mask_ref.shape
    inner = d_ref.shape[1]
    o_ref[: slots + batches * rows, :inner] = jnp.zeros((slots + batches * rows, inner), BF)
    d_keys_p, d_values_p = jnp.zeros((slots, inner), F32), jnp.zeros((slots, inner), F32)
    for batch in range(batches):
        query, keys, values, weights, heads = batch_parts(qkv_ref, mask_ref, batch, slots)
        mem = slots + batch * rows
        tok = slots + (batches + batch) * rows
        d_mixed = by_head(d_ref[batch * rows : (batch + 1) * rows, :], heads)
        d_weights = dot_t(d_mixed, values)
        d_values = t_dot(weights.astype(BF), d_mixed)
        even = jnp.sum(weights * d_weights, axis=1, keepdims=True)
        d_scores = (weights * (d_weights - even)).astype(BF)
        d_query = from_heads(dot(d_scores, keys), heads) * HD ** (-0.5)
        d_keys = t_dot(d_scores, query) * HD ** (-0.5)
        o_ref[tok : tok + rows, :inner] = d_query.astype(BF)
        d_keys_p, d_values_p = d_keys_p + d_keys[:slots], d_values_p + d_values[:slots]
        for low, grad in ((inner, d_keys), (2 * inner, d_values)):
            o_ref[mem : mem + rows, low : low + inner] = grad[slots : slots + rows].astype(BF)
            o_ref[tok : tok + rows, low : low + inner] = grad[slots + rows :].astype(BF)
    o_ref[:slots, inner : 2 * inner] = d_keys_p.astype(BF)
    o_ref[:slots, 2 * inner :] = d_values_p.astype(BF)


def local_call(body, shape, *operands):
    vmem = pl.BlockSpec(memory_space=pltpu.VMEM)
    return pl.pallas_call(
        body,
        out_shape=jax.ShapeDtypeStruct(shape, BF),
        in_specs=[vmem] * len(operands),
        out_specs=vmem,
        compiler_params=pltpu.CompilerParams(vmem_limit_bytes=16 * GRANT),
        cost_estimate=pl.CostEstimate(flops=0, bytes_accessed=2 * 10**7, transcendentals=0),
        name="attend",
    )(*operands)


def together(*values):
    return lax.optimization_barrier(values)


def rms(v):
    return lax.rsqrt(jnp.mean(v * v, axis=-1, keepdims=True) + EPSILON)


def rms_back(v, r, gain, grad):
    scaled = grad * gain
    inner = jnp.sum(scaled * v, axis=-1, keepdims=True)
    return r * scaled - v * (r * r * r) * (inner / v.shape[-1])


def silu_parts(z):
    s = jax.nn.sigmoid(z)
    return s, z * s, s * (1.0 + z * (1.0 - s))


def per_device(
    tokens,
    cotangent,
    dest,
    source,
    lengths,
    persist,
    gain_attn,
    w_query_mem,
    mem_in,
    mem_out,
    w_query,
    w_key,
    w_value,
    w_output,
    gain_mem,
    w_key_mem,
    w_value_mem,
    w_rate,
    gain_ffn,
    w_gate,
    w_up,
    w_down,
):
    count, width = tokens.shape
    shard = gain_attn.shape[0]
    ranks = width // shard
    batches, _ = lengths.shape
    rows = count // batches
    hidden = mem_in.shape[1]
    inner = w_query.shape[1]
    heads = inner // HD
    slots = persist.shape[0]
    me = lax.axis_index("tensor")

    def gather_whole(*parts):
        return lax.all_gather(jnp.concatenate(parts, axis=1), "dp", axis=0, tiled=True)

    def gather(*parts):
        return cut_apart(gather_whole(*parts), *[part.shape[1] for part in parts])

    vectors = jnp.stack([gain_attn, gain_mem, gain_ffn, w_rate], axis=1)
    pad = jnp.zeros((shard, 128 - slots - 4), BF)
    small, wqm_t = gather(jnp.concatenate([persist.T, vectors, pad], axis=1), w_query_mem.T)
    tall = line_gather(jnp.concatenate([w_key_mem, w_value_mem], axis=1), 7)
    persistent = small[:, :slots].T
    gains = small[:, slots : slots + 4].astype(F32).T
    g_attn, g_mem, g_ffn, rate_w = (gains[i][None, :] for i in range(4))

    place = jnp.arange(count, dtype=jnp.int32)
    home = dest // count
    earlier = (home[None, :] == home[:, None]) & (place[None, :] < place[:, None])
    sent_at = home * (count // ranks) + jnp.sum(earlier.astype(jnp.int32), axis=1)
    came_at = jnp.sum((source[None, :] < source[:, None]).astype(jnp.int32), axis=1)
    send_m = (sent_at[None, :] == place[:, None]).astype(BF)
    deal_m = (came_at[:, None] == place[None, :]).astype(BF)

    def exchange(v):
        return lax.all_to_all(v, "dp", split_axis=0, concat_axis=0, tiled=True)

    leaving, late_in, late_mem_out = together(dot(send_m, tokens).astype(BF), mem_in, mem_out)
    w_in, w_out_t = gather(late_in, late_mem_out.T)
    arrived, tall = together(exchange(leaving), tall)
    dealt = dot(deal_m, arrived).astype(BF)
    x = dealt.astype(F32)

    position = jnp.arange(rows, dtype=jnp.int32)
    turn = jnp.arange(lengths.shape[1])
    bounds = jnp.sum(
        jnp.where(turn[:, None] <= turn[None, :], lengths[:, :, None], 0), axis=1, dtype=jnp.int32
    )
    segment = jnp.sum((position[None, :, None] >= bounds[:, None, :]).astype(jnp.int32), axis=2)
    causal = (segment[:, :, None] == segment[:, None, :]) & (
        position[None, None, :] <= position[None, :, None]
    )

    def split(v):
        return v.reshape(batches, rows, v.shape[-1])

    def join(v):
        return v.reshape(count, v.shape[-1])

    def own(v):
        return lax.dynamic_slice_in_dim(v, me * inner, inner, 1)

    def in_own(v):
        return lax.dynamic_update_slice_in_dim(
            jnp.zeros((v.shape[0], width), v.dtype), v, me * inner, 1
        )

    r1 = rms(x)
    n1 = (x * r1 * g_attn).astype(BF)
    n1_own = own(n1)
    query_mem = chain_sum(dot_t(n1_own, wqm_t))
    query_mem, late_query, late_key, late_value, late_output = together(
        query_mem, w_query, w_key, w_value, w_output
    )
    w_attn = gather_whole(late_query, late_key, late_value, late_output.T)
    read_s, read_act, read_slope = silu_parts(dot(query_mem, w_in))
    read_low, tall = together(read_act.astype(BF), tall)
    wkm_t, wvm_t = gather(tall[:, :shard].T, tall[:, shard:].T)
    memory = chain_sum(dot_t(read_low, w_out_t))
    memory, w_attn = together(memory, w_attn)
    w_qkv, wo_t = cut_apart(w_attn, 3 * inner, inner)
    w_kv = w_attn[:, inner : 3 * inner]
    (all_rows,) = together(jnp.concatenate([persistent, memory, n1], axis=0))
    qkv = dot(all_rows, w_qkv).astype(BF)
    allowed = jnp.concatenate(
        [jnp.ones((batches, rows, slots), F32), causal.astype(F32), causal.astype(F32)], axis=2
    )
    mixed = local_call(functools.partial(attend_kernel, slots), (count, inner), qkv, allowed)
    mixed, late_gate, late_up, late_down = together(mixed, w_gate, w_up, w_down)
    wg, wu, wd_t = gather(late_gate, late_up, late_down.T)
    after_attn = x + chain_sum(dot_t(mixed, wo_t)).astype(F32)

    r2 = rms(after_attn)
    n2 = after_attn * r2 * g_mem
    rate_s = jax.nn.sigmoid(jnp.sum(n2 * rate_w, axis=1, keepdims=True))
    rate_s, later = together(rate_s, cotangent)
    cotangent_arrived = exchange(dot(send_m, later).astype(BF))
    rate = RATE_SCALE * rate_s
    n2_low = n2.astype(BF)
    n2_own = own(n2_low)
    key_mem = dot_t(n2_low, wkm_t).astype(BF)
    value_part = dot_t(n2_own, own(wvm_t))
    key_hidden = dot(key_mem, w_in)
    key_s, key_silu, key_slope = silu_parts(key_hidden)
    key_act = key_silu.astype(BF)
    miss, cotangent_arrived = together(
        chain_sum(dot_t(key_act, w_out_t) - value_part), cotangent_arrived
    )
    miss = miss.astype(F32)
    d_out_low = dot(deal_m, cotangent_arrived).astype(BF)
    error = (rate * miss).astype(BF)
    back_pre = dot(error, w_out_t)
    back_hidden = (back_pre * key_slope).astype(BF)
    gram = jnp.where(causal, batch_dot("bik,bjk->bij", split(key_mem), split(key_mem)), 0.0).astype(BF)
    new_hidden = key_hidden - join(batch_dot("bij,bjk->bik", gram, split(back_hidden)))
    _, new_silu, new_slope = silu_parts(new_hidden)
    new_act = new_silu.astype(BF)
    pair = jnp.where(causal, batch_dot("bik,bjk->bij", split(new_act), split(key_act)), 0.0).astype(BF)
    update = dot_t(new_act, w_out_t) - join(batch_dot("bij,bjk->bik", pair, split(error)))
    after_mem = after_attn + chain_sum(update).astype(F32)

    r3 = rms(after_mem)
    n3 = (after_mem * r3 * g_ffn).astype(BF)
    gate, up = dot(n3, wg), dot(n3, wu)
    _, gate_silu, gate_slope = silu_parts(gate)
    ffn_act = (gate_silu * up).astype(BF)
    ffn_part = dot_t(ffn_act, wd_t).astype(BF)

    d_ffn = dot(d_out_low, wd_t)
    d_gate = (d_ffn * up * gate_slope).astype(BF)
    d_up, ffn_part = together((d_ffn * gate_silu).astype(BF), ffn_part)
    d_n3, gw_ffn = chain_sum(
        dot_t(d_gate, wg) + dot_t(d_up, wu),
        2,
        [[(d_out_low, ffn_act)], [(n3, d_gate)], [(n3, d_up)]],
    )
    d_n3 = d_n3.astype(F32)
    gg_ffn = jnp.sum(d_n3 * after_mem * r3, axis=0)
    d_after_mem = d_out_low.astype(F32) + rms_back(after_mem, r3, g_ffn, d_n3)
    d_update = d_after_mem.astype(BF)

    d_pair = jnp.where(
        causal, -batch_dot("bik,bjk->bij", split(d_update), split(error)), 0.0
    ).astype(BF)
    d_new_act = dot(d_update, w_out_t) + join(batch_dot("bij,bjk->bik", d_pair, split(key_act)))
    d_key_act = join(batch_dot("bij,bik->bjk", d_pair, split(new_act)))
    d_new_hidden = (d_new_act * new_slope).astype(BF)
    d_gram = jnp.where(
        causal, -batch_dot("bik,bjk->bij", split(d_new_hidden), split(back_hidden)), 0.0
    ).astype(BF)
    d_back = (-join(batch_dot("bij,bik->bjk", gram, split(d_new_hidden)))).astype(BF).astype(F32)
    d_back_pre = (d_back * key_slope).astype(BF)
    slope_grad = key_s * (1.0 - key_s) * (2.0 + key_hidden * (1.0 - 2.0 * key_s))
    d_hidden_part = d_new_hidden.astype(F32) + d_back * back_pre * slope_grad
    d_error_part = dot_t(d_back_pre, w_out_t) - join(
        batch_dot("bij,bik->bjk", pair, split(d_update))
    )
    share_ffn = lax.psum_scatter(gw_ffn, "dp", scatter_dimension=0, tiled=True)
    d_error = chain_sum(d_error_part).astype(F32)
    d_rate = jnp.sum(d_error * miss, axis=1, keepdims=True)
    d_miss = (rate * d_error).astype(BF)
    d_key_act = d_key_act + dot(d_miss, w_out_t)
    d_key_hidden = (d_hidden_part + d_key_act * key_slope).astype(BF)
    d_key_part = dot_t(d_key_hidden, w_in) + join(
        batch_dot("bij,bjk->bik", d_gram, split(key_mem))
        + batch_dot("bij,bik->bjk", d_gram, split(key_mem))
    )
    d_key, gw_out_early = chain_sum(
        d_key_part, 6, [[(d_update, new_act), (error, d_back_pre)]], True
    )
    d_key, ffn_part = together(d_key, ffn_part)
    ffn_own = lax.psum_scatter(ffn_part, "tensor", scatter_dimension=1, tiled=True)
    d_n2 = dot(d_key, wkm_t) - dot(d_miss, wvm_t)
    d_logit = d_rate * rate * (1.0 - rate_s)
    gg_rate = jnp.sum(n2 * d_logit, axis=0)
    d_n2 = d_n2 + d_logit * rate_w
    gg_mem = jnp.sum(d_n2 * after_attn * r2, axis=0)
    late_r2, share_ffn = together(r2, share_ffn)
    d_after_attn = d_after_mem + rms_back(after_attn, late_r2, g_mem, d_n2)
    d_attn = d_after_attn.astype(BF)

    d_mixed = dot(d_attn, wo_t).astype(BF)
    d_qkv = local_call(
        functools.partial(attend_back_kernel, slots), qkv.shape, qkv, allowed, d_mixed
    )
    d_rows = d_qkv[slots + count :]
    d_context, gw_attn = chain_sum(
        dot_t(d_qkv[: slots + count, inner:], w_kv),
        3,
        [
            [(d_key, n2_own)],
            [(d_miss, n2_own)],
            [(d_attn, mixed)],
            [(all_rows, d_qkv)],
        ],
    )
    d_n1_part = dot_t(d_rows, w_qkv)

    share_attn = lax.psum_scatter(gw_attn, "dp", scatter_dimension=0, tiled=True)
    d_context, ffn_own = together(d_context, ffn_own)
    g_persist, d_memory = d_context[:slots], d_context[slots:]
    result_own = (own(after_mem) + ffn_own.astype(F32)).astype(BF)
    turned_result = t_dot(deal_m, result_own).astype(BF)
    d_read = (dot(d_memory, w_out_t) * read_slope).astype(BF)
    d_query_mem, gw_mem = chain_sum(
        dot_t(d_read, w_in),
        4,
        [
            [(key_mem, d_key_hidden), (query_mem, d_read)],
            [(d_miss, key_act), (d_memory, read_low), (gw_out_early,)],
        ],
    )
    share_mem = lax.psum_scatter(gw_mem, "dp", scatter_dimension=0, tiled=True)
    seats = count // ranks
    gw_query_mem = t_dot(d_query_mem, n1_own).astype(BF).reshape(ranks, shard, inner)
    result_back = exchange(
        jnp.concatenate([turned_result.reshape(ranks, seats, inner), gw_query_mem], axis=1)
    )
    late_wqm_t, share_attn = together(wqm_t, share_attn)
    d_n1_part = d_n1_part + in_own(dot(d_query_mem, late_wqm_t))
    last = chain_sum(d_n1_part)
    last, result_back = together(last, result_back)
    d_n1 = last.astype(F32)
    s_query_mem = jnp.sum(result_back[:, seats:].astype(F32), axis=0)
    result_back = result_back[:, :seats].reshape(count, inner)
    gg_attn = jnp.sum(d_n1 * x * r1, axis=0)
    d_x = d_after_attn + rms_back(x, r1, g_attn, d_n1)

    def cut(share, *widths):
        return [part.astype(F32) for part in cut_apart(share, *widths)]

    s_down, s_gate, s_up = cut(share_ffn, *[w_gate.shape[1]] * 3)
    s_key_mem, s_value_mem, s_output, s_query, s_key, s_value = cut(share_attn, *[inner] * 6)
    s_in, s_out = cut(share_mem, hidden, hidden)
    grad_vectors = jnp.stack([gg_attn, gg_mem, gg_ffn, gg_rate], axis=1)
    rest = jnp.concatenate(
        [
            g_persist.T,
            grad_vectors.astype(BF),
            jnp.zeros((width, 128 - slots - 4), BF),
        ],
        axis=1,
    ).reshape(ranks, -1, width)
    turned = t_dot(deal_m, d_x.astype(BF)).astype(BF).reshape(ranks, -1, width)
    came = lax.all_to_all(
        jnp.concatenate([turned, rest], axis=1), "dp", split_axis=0, concat_axis=0, tiled=True
    )
    output = line_gather(t_dot(send_m, result_back).astype(BF), 8, True)
    came, output = together(came, output)
    grad_tokens = t_dot(send_m, came[:, :seats].reshape(count, width)).astype(BF)
    share_rest = jnp.sum(came[:, seats:].astype(F32), axis=0).reshape(shard, -1)
    s_small = share_rest
    s_vectors = s_small[:, slots : slots + 4].T

    return (
        output,
        grad_tokens,
        s_small[:, :slots].T,
        s_vectors[0],
        s_query_mem.T,
        s_in,
        s_out.T,
        s_query,
        s_key,
        s_value,
        s_output.T,
        s_vectors[1],
        s_key_mem.T,
        -s_value_mem.T,
        s_vectors[3],
        s_vectors[2],
        s_gate,
        s_up,
        s_down.T,
    )


def solution(mesh):
    rows = P("dp", None)
    vector = P("dp")
    across = P("tensor", "dp")
    along = P("dp", "tensor")
    return jax.shard_map(
        per_device,
        mesh=mesh,
        in_specs=(
            rows,
            rows,
            vector,
            vector,
            rows,
            P(None, "dp"),
            vector,
            across,
            along,
            across,
            along,
            along,
            along,
            across,
            vector,
            across,
            across,
            vector,
            vector,
            along,
            along,
            across,
        ),
        out_specs=(
            rows,
            rows,
            P(None, "dp"),
            vector,
            across,
            along,
            across,
            along,
            along,
            along,
            across,
            vector,
            across,
            across,
            vector,
            vector,
            along,
            along,
            across,
        ),
        check_vma=False,
    )
```

```python
import functools

import jax
import jax.numpy as jnp
from jax import lax
from jax.experimental import pallas as pl
from jax.experimental.pallas import tpu as pltpu
from jax.sharding import PartitionSpec as P

HD = 96
EPSILON = 1e-06
RATE_SCALE = 8e-05
NEG_LARGE = -1e30
BF = jnp.bfloat16
F32 = jnp.float32
MESH = pl.DeviceIdType.MESH
TILE = 128
GRANT = 1 << 20


def chain_sum_kernel(pieces, layout, x_ref, *refs):
    given = sum(len(widths) for _, parts in layout for widths in parts)
    fills, refs = refs[:given], refs[given:]
    o_ref, refs = refs[0], refs[1:]
    if layout:
        g_ref, refs = refs[0], refs[1:]
    from_outer, from_inner, part, sent_a, got_up, sent_b, got_across, got_total = refs[:8]
    me = lax.axis_index("tensor")
    step = x_ref.shape[0] // pieces
    low = me < 2
    outer = jnp.logical_or(me == 0, me == 3)
    inner = jnp.logical_not(outer)
    outer_peer = jnp.where(low, 0, 3)
    inner_peer = jnp.where(low, 2, 1)
    toward = jnp.where(low, 1, 2)
    barrier = pltpu.get_barrier_semaphore()

    def tell(peer):
        pl.semaphore_signal(barrier, inc=1, device_id={"tensor": peer}, device_id_type=MESH)

    def at(piece):
        return pl.ds(pl.multiple_of(piece * step, step), step)

    def send(src, dst, send_sem, recv_sem, peer):
        return pltpu.make_async_remote_copy(
            src_ref=src,
            dst_ref=dst,
            send_sem=send_sem,
            recv_sem=recv_sem,
            device_id={"tensor": peer},
            device_id_type=MESH,
        )

    def up(p):
        return send(x_ref.at[at(p)], from_outer.at[at(p)], sent_a.at[p], got_up.at[p], toward)

    def across(p):
        return send(part.at[at(p)], from_inner.at[at(p)], sent_b.at[p], got_across.at[p], inner_peer)

    def down(p):
        return send(o_ref.at[at(p)], o_ref.at[at(p)], sent_a.at[p], got_total.at[p], outer_peer)

    def put(tile):
        stage, put_sem = refs[8], refs[9]
        rows = pl.ds(pl.multiple_of(tile * TILE, TILE), TILE)
        slot = lax.rem(tile, 2)
        target = g_ref.at[rows, pl.ds(0, stage.shape[2])]
        return pltpu.make_async_copy(stage.at[slot], target, put_sem.at[slot])

    def fill(tile):
        stage = refs[8]
        columns = pl.ds(pl.multiple_of(tile * TILE, TILE), TILE)
        slot = lax.rem(tile, 2)

        @pl.when(tile >= 2)
        def _():
            put(tile - 2).wait()

        first, offset = 0, 0
        for width, parts in layout:
            for start in range(0, width, 512):
                span = min(512, width - start)
                total, index = None, first
                for part_sizes in parts:
                    if len(part_sizes) == 1:
                        term = fills[index][columns, start : start + span].astype(F32)
                    else:
                        term = lax.dot_general(
                            fills[index][:, columns],
                            fills[index + 1][:, start : start + span],
                            (((0,), (0,)), ((), ())),
                            preferred_element_type=F32,
                        )
                    total = term if total is None else total + term
                    index += len(part_sizes)
                stage[slot, :, offset + start : offset + start + span] = total.astype(BF)
            first, offset = index, offset + width
        put(tile).start()

    @pl.when(outer)
    def _():
        tell(toward)
        pl.semaphore_wait(barrier, 1)

        @pl.loop(0, pieces)
        def _(p):
            up(p).start()

    @pl.when(inner)
    def _():
        tell(outer_peer)
        tell(inner_peer)
        pl.semaphore_wait(barrier, 2)

    def first_add(p):
        up(p).wait_recv()
        part[at(p), :] = (
            x_ref[at(p), :].astype(F32) + from_outer[at(p), :].astype(F32)
        ).astype(part.dtype)
        across(p).start()

    def second_add(p):
        across(p).wait_recv()
        o_ref[at(p), :] = (
            part[at(p), :].astype(F32) + from_inner[at(p), :].astype(F32)
        ).astype(o_ref.dtype)
        down(p).start()

    tiles = g_ref.shape[0] // TILE if layout else 0

    per, lag = 2, 2
    turns = pieces // per

    @pl.loop(0, max(turns + lag, tiles))
    def _(p):
        @pl.when(jnp.logical_and(inner, p < turns))
        def _():
            for k in range(per):
                first_add(p * per + k)

        @pl.when(jnp.logical_and(inner, jnp.logical_and(p >= lag, p < turns + lag)))
        def _():
            for k in range(per):
                second_add((p - lag) * per + k)

        if layout:

            @pl.when(p < tiles)
            def _():
                fill(p)

    if layout:
        put(tiles - 2).wait()
        put(tiles - 1).wait()

    @pl.when(outer)
    def _():
        @pl.loop(0, pieces)
        def _(p):
            down(p).wait_recv()
            up(p).wait_send()

    @pl.when(inner)
    def _():
        @pl.loop(0, pieces)
        def _(p):
            across(p).wait_send()
            down(p).wait_send()


def chain_sum(x, call_id=1, products=(), room=0):
    rows, cols = x.shape
    pieces = rows // 16
    dma = pltpu.SemaphoreType.DMA
    vmem = pl.BlockSpec(memory_space=pltpu.VMEM)
    layout = tuple(
        (pairs[0][1].shape[1], tuple((0,) * len(pair) for pair in pairs)) for pairs in products
    )
    fills = [array for pairs in products for pair in pairs for array in pair]
    out_shape = [jax.ShapeDtypeStruct((rows, cols), BF)]
    out_specs = [vmem]
    scratch = [pltpu.VMEM((rows, cols), BF)] * 3 + [dma((pieces,))] * 5
    grant = 3 * rows * cols * 2 + GRANT
    if products:
        width, high = sum(w for w, _ in layout), products[0][0][0].shape[1]
        out_shape.append(jax.ShapeDtypeStruct((high, width + room), BF))
        out_specs.append(pl.BlockSpec(memory_space=pl.ANY))
        scratch += [pltpu.VMEM((2, TILE, width), BF), dma((2,))]
        grant += 2 * TILE * width * 2 + 4 * GRANT
    out = pl.pallas_call(
        functools.partial(chain_sum_kernel, pieces, layout),
        out_shape=out_shape,
        in_specs=[vmem] * (1 + len(fills)),
        out_specs=out_specs,
        scratch_shapes=scratch,
        compiler_params=pltpu.CompilerParams(
            collective_id=call_id, has_side_effects=True, vmem_limit_bytes=grant
        ),
        cost_estimate=pl.CostEstimate(flops=0, bytes_accessed=10**8, transcendentals=0),
        name="chain_sum",
    )(x.astype(BF), *fills)
    return out if products else out[0]


def line_gather_kernel(pieces, side, x_ref, o_ref, sent, got, keep):
    me = lax.axis_index("tensor")
    high, wide = x_ref.shape
    step = high // pieces
    last = 3

    def place(block, low, size):
        if side:
            return o_ref.at[pl.ds(low, size), pl.ds(pl.multiple_of(block * wide, wide), wide)]
        return o_ref.at[pl.ds(pl.multiple_of(block * high + low, size), size)]

    barrier = pltpu.get_barrier_semaphore()
    ways = ((0, me < last, 1), (1, me > 0, -1))

    for _, open_, move in ways:

        @pl.when(open_)
        def _():
            pl.semaphore_signal(
                barrier, inc=1, device_id={"tensor": me + move}, device_id_type=MESH
            )

    at_end = jnp.logical_or(me == 0, me == last)

    @pl.when(at_end)
    def _():
        pl.semaphore_wait(barrier, 1)

    @pl.when(jnp.logical_not(at_end))
    def _():
        pl.semaphore_wait(barrier, 2)

    def copy(way, hop, piece, move, block, first=False):
        there = place(block, piece * step, step)
        return pltpu.make_async_remote_copy(
            src_ref=x_ref.at[pl.ds(piece * step, step)] if first else there,
            dst_ref=there,
            send_sem=sent.at[way, hop, piece],
            recv_sem=got.at[way, hop, piece],
            device_id={"tensor": jnp.clip(me + move, 0, last)},
            device_id_type=MESH,
        )

    def forward(way, move, hop):
        block = me - move * hop
        return jnp.logical_and(
            jnp.logical_and(me + move >= 0, me + move <= last),
            jnp.logical_and(block >= 0, block <= last),
        )

    def comes(way, move, hop):
        block = me - move * (hop + 1)
        return jnp.logical_and(block >= 0, block <= last)

    def own():
        return pltpu.make_async_copy(x_ref, place(me, 0, high), keep.at[0])

    for hop in range(last):
        for piece in range(pieces):
            for way, _, move in ways:

                @pl.when(forward(way, move, hop))
                def _():
                    copy(way, hop, piece, move, me - move * hop, hop == 0).start()

        if hop == 0:
            own().start()
        for piece in range(pieces):
            for way, _, move in ways:

                @pl.when(comes(way, move, hop))
                def _():
                    copy(way, hop, piece, move, me - move * (hop + 1)).wait_recv()

    own().wait()
    for hop in range(last):
        for piece in range(pieces):
            for way, _, move in ways:

                @pl.when(forward(way, move, hop))
                def _():
                    copy(way, hop, piece, move, me - move * hop, hop == 0).wait_send()


def line_gather(x, call_id, side=False, pieces=2):
    rows, cols = x.shape
    shape = (rows, 4 * cols) if side else (4 * rows, cols)
    dma = pltpu.SemaphoreType.DMA
    vmem = pl.BlockSpec(memory_space=pltpu.VMEM)
    return pl.pallas_call(
        functools.partial(line_gather_kernel, pieces, side),
        out_shape=jax.ShapeDtypeStruct(shape, BF),
        in_specs=[vmem],
        out_specs=vmem,
        scratch_shapes=[dma((2, 3, pieces)), dma((2, 3, pieces)), dma((1,))],
        compiler_params=pltpu.CompilerParams(
            collective_id=call_id, has_side_effects=True, vmem_limit_bytes=GRANT
        ),
        cost_estimate=pl.CostEstimate(flops=0, bytes_accessed=5 * 10**7, transcendentals=0),
        name="line_gather",
    )(x)


def dot(left, right):
    return lax.dot_general(left, right, (((1,), (0,)), ((), ())), preferred_element_type=F32)


def dot_t(left, right):
    return lax.dot_general(left, right, (((1,), (1,)), ((), ())), preferred_element_type=F32)


def t_dot(left, right):
    return lax.dot_general(left, right, (((0,), (0,)), ((), ())), preferred_element_type=F32)


def batch_dot(spec, left, right):
    return jnp.einsum(spec, left, right, preferred_element_type=F32)


def cut_apart(whole, *widths):
    out, low = [], 0
    for width in widths:
        out.append(whole[:, low : low + width])
        low += width
    return out


def by_head(v, heads):
    column = lax.broadcasted_iota(jnp.int32, v.shape, 1)
    zero = jnp.zeros_like(v)
    return jnp.concatenate(
        [
            jnp.where(jnp.logical_and(column >= h * HD, column < (h + 1) * HD), v, zero)
            for h in range(heads)
        ],
        axis=0,
    )


def from_heads(v, heads):
    rows = v.shape[0] // heads
    column = lax.broadcasted_iota(jnp.int32, (rows, v.shape[1]), 1)
    out = jnp.zeros((rows, v.shape[1]), v.dtype)
    for h in range(heads):
        here = jnp.logical_and(column >= h * HD, column < (h + 1) * HD)
        out = jnp.where(here, v[h * rows : (h + 1) * rows], out)
    return out


def batch_parts(qkv_ref, mask_ref, batch, slots):
    batches, rows, _ = mask_ref.shape
    inner = qkv_ref.shape[1] // 3
    heads = inner // HD
    mem = slots + batch * rows
    tok = slots + (batches + batch) * rows

    def context(low):
        cols = slice(low, low + inner)
        return jnp.concatenate(
            [qkv_ref[:slots, cols], qkv_ref[mem : mem + rows, cols], qkv_ref[tok : tok + rows, cols]],
            axis=0,
        )

    query = by_head(qkv_ref[tok : tok + rows, :inner], heads)
    keys, values = context(inner), context(2 * inner)
    scores = dot_t(query, keys) * HD ** (-0.5)
    allowed = jnp.concatenate([mask_ref[batch]] * heads, axis=0)
    scores = jnp.where(allowed > 0.5, scores, NEG_LARGE)
    high = jnp.max(scores, axis=1, keepdims=True)
    raised = jnp.exp(scores - high)
    weights = raised / jnp.sum(raised, axis=1, keepdims=True)
    return query, keys, values, weights, heads


def attend_kernel(slots, qkv_ref, mask_ref, o_ref):
    batches, rows, _ = mask_ref.shape
    for batch in range(batches):
        _, _, values, weights, heads = batch_parts(qkv_ref, mask_ref, batch, slots)
        mixed = from_heads(dot(weights.astype(BF), values), heads)
        o_ref[batch * rows : (batch + 1) * rows, :] = mixed.astype(BF)


def attend_back_kernel(slots, qkv_ref, mask_ref, d_ref, o_ref):
    batches, rows, _ = mask_ref.shape
    inner = d_ref.shape[1]
    o_ref[: slots + batches * rows, :inner] = jnp.zeros((slots + batches * rows, inner), BF)
    d_keys_p, d_values_p = jnp.zeros((slots, inner), F32), jnp.zeros((slots, inner), F32)
    for batch in range(batches):
        query, keys, values, weights, heads = batch_parts(qkv_ref, mask_ref, batch, slots)
        mem = slots + batch * rows
        tok = slots + (batches + batch) * rows
        d_mixed = by_head(d_ref[batch * rows : (batch + 1) * rows, :], heads)
        d_weights = dot_t(d_mixed, values)
        d_values = t_dot(weights.astype(BF), d_mixed)
        even = jnp.sum(weights * d_weights, axis=1, keepdims=True)
        d_scores = (weights * (d_weights - even)).astype(BF)
        d_query = from_heads(dot(d_scores, keys), heads) * HD ** (-0.5)
        d_keys = t_dot(d_scores, query) * HD ** (-0.5)
        o_ref[tok : tok + rows, :inner] = d_query.astype(BF)
        d_keys_p, d_values_p = d_keys_p + d_keys[:slots], d_values_p + d_values[:slots]
        for low, grad in ((inner, d_keys), (2 * inner, d_values)):
            o_ref[mem : mem + rows, low : low + inner] = grad[slots : slots + rows].astype(BF)
            o_ref[tok : tok + rows, low : low + inner] = grad[slots + rows :].astype(BF)
    o_ref[:slots, inner : 2 * inner] = d_keys_p.astype(BF)
    o_ref[:slots, 2 * inner :] = d_values_p.astype(BF)


def local_call(body, shape, *operands):
    vmem = pl.BlockSpec(memory_space=pltpu.VMEM)
    return pl.pallas_call(
        body,
        out_shape=jax.ShapeDtypeStruct(shape, BF),
        in_specs=[vmem] * len(operands),
        out_specs=vmem,
        compiler_params=pltpu.CompilerParams(vmem_limit_bytes=16 * GRANT),
        cost_estimate=pl.CostEstimate(flops=0, bytes_accessed=2 * 10**7, transcendentals=0),
        name="attend",
    )(*operands)


def together(*values):
    return lax.optimization_barrier(values)


def rms(v):
    return lax.rsqrt(jnp.mean(v * v, axis=-1, keepdims=True) + EPSILON)


def rms_back(v, r, gain, grad):
    scaled = grad * gain
    inner = jnp.sum(scaled * v, axis=-1, keepdims=True)
    return r * scaled - v * (r * r * r) * (inner / v.shape[-1])


def silu_parts(z):
    s = jax.nn.sigmoid(z)
    return s, z * s, s * (1.0 + z * (1.0 - s))


def per_device(
    tokens,
    cotangent,
    dest,
    source,
    lengths,
    persist,
    gain_attn,
    w_query_mem,
    mem_in,
    mem_out,
    w_query,
    w_key,
    w_value,
    w_output,
    gain_mem,
    w_key_mem,
    w_value_mem,
    w_rate,
    gain_ffn,
    w_gate,
    w_up,
    w_down,
):
    count, width = tokens.shape
    shard = gain_attn.shape[0]
    ranks = width // shard
    batches, _ = lengths.shape
    rows = count // batches
    hidden = mem_in.shape[1]
    inner = w_query.shape[1]
    heads = inner // HD
    slots = persist.shape[0]
    me = lax.axis_index("tensor")

    def gather_whole(*parts):
        return lax.all_gather(jnp.concatenate(parts, axis=1), "dp", axis=0, tiled=True)

    def gather(*parts):
        return cut_apart(gather_whole(*parts), *[part.shape[1] for part in parts])

    vectors = jnp.stack([gain_attn, gain_mem, gain_ffn, w_rate], axis=1)
    pad = jnp.zeros((shard, 128 - slots - 4), BF)
    small, wqm_t = gather(jnp.concatenate([persist.T, vectors, pad], axis=1), w_query_mem.T)
    tall = line_gather(jnp.concatenate([w_key_mem, w_value_mem], axis=1), 7)
    persistent = small[:, :slots].T
    gains = small[:, slots : slots + 4].astype(F32).T
    g_attn, g_mem, g_ffn, rate_w = (gains[i][None, :] for i in range(4))

    place = jnp.arange(count, dtype=jnp.int32)
    home = dest // count
    earlier = (home[None, :] == home[:, None]) & (place[None, :] < place[:, None])
    sent_at = home * (count // ranks) + jnp.sum(earlier.astype(jnp.int32), axis=1)
    came_at = jnp.sum((source[None, :] < source[:, None]).astype(jnp.int32), axis=1)
    send_m = (sent_at[None, :] == place[:, None]).astype(BF)
    deal_m = (came_at[:, None] == place[None, :]).astype(BF)

    def exchange(v):
        return lax.all_to_all(v, "dp", split_axis=0, concat_axis=0, tiled=True)

    leaving, late_in, late_mem_out = together(dot(send_m, tokens).astype(BF), mem_in, mem_out)
    w_in, w_out_t = gather(late_in, late_mem_out.T)
    arrived, tall = together(exchange(leaving), tall)
    dealt = dot(deal_m, arrived).astype(BF)
    x = dealt.astype(F32)

    position = jnp.arange(rows, dtype=jnp.int32)
    turn = jnp.arange(lengths.shape[1])
    bounds = jnp.sum(
        jnp.where(turn[:, None] <= turn[None, :], lengths[:, :, None], 0), axis=1, dtype=jnp.int32
    )
    segment = jnp.sum((position[None, :, None] >= bounds[:, None, :]).astype(jnp.int32), axis=2)
    causal = (segment[:, :, None] == segment[:, None, :]) & (
        position[None, None, :] <= position[None, :, None]
    )

    def split(v):
        return v.reshape(batches, rows, v.shape[-1])

    def join(v):
        return v.reshape(count, v.shape[-1])

    def own(v):
        return lax.dynamic_slice_in_dim(v, me * inner, inner, 1)

    def in_own(v):
        return lax.dynamic_update_slice_in_dim(
            jnp.zeros((v.shape[0], width), v.dtype), v, me * inner, 1
        )

    r1 = rms(x)
    n1, late_query, late_key, late_value, late_output = together(
        (x * r1 * g_attn).astype(BF), w_query, w_key, w_value, w_output
    )
    w_attn = gather_whole(late_query, late_key, late_value, late_output.T)
    n1_own = own(n1)
    query_mem = chain_sum(dot_t(n1_own, wqm_t))
    query_mem, tall = together(query_mem, tall)
    wkm_t, wvm_t = gather(tall[:, :shard].T, tall[:, shard:].T)
    read_s, read_act, read_slope = silu_parts(dot(query_mem, w_in))
    read_low = read_act.astype(BF)
    memory = chain_sum(dot_t(read_low, w_out_t))
    memory, w_attn = together(memory, w_attn)
    w_qkv, wo_t = cut_apart(w_attn, 3 * inner, inner)
    w_kv = w_attn[:, inner : 3 * inner]
    (all_rows,) = together(jnp.concatenate([persistent, memory, n1], axis=0))
    qkv = dot(all_rows, w_qkv).astype(BF)
    allowed = jnp.concatenate(
        [jnp.ones((batches, rows, slots), F32), causal.astype(F32), causal.astype(F32)], axis=2
    )
    mixed = local_call(functools.partial(attend_kernel, slots), (count, inner), qkv, allowed)
    mixed, late_gate, late_up, late_down, later = together(mixed, w_gate, w_up, w_down, cotangent)
    cotangent_arrived = exchange(dot(send_m, later).astype(BF))
    wg, wu, wd_t = gather(late_gate, late_up, late_down.T)
    attended, cotangent_arrived = together(chain_sum(dot_t(mixed, wo_t)), cotangent_arrived)
    after_attn = x + attended.astype(F32)
    d_out_low = dot(deal_m, cotangent_arrived).astype(BF)

    r2 = rms(after_attn)
    n2 = after_attn * r2 * g_mem
    rate_s = jax.nn.sigmoid(jnp.sum(n2 * rate_w, axis=1, keepdims=True))
    rate = RATE_SCALE * rate_s
    n2_low = n2.astype(BF)
    n2_own = own(n2_low)
    key_mem = dot_t(n2_low, wkm_t).astype(BF)
    value_part = dot_t(n2_own, own(wvm_t))
    key_hidden = dot(key_mem, w_in)
    key_s, key_silu, key_slope = silu_parts(key_hidden)
    key_act = key_silu.astype(BF)
    miss = chain_sum(dot_t(key_act, w_out_t) - value_part).astype(F32)
    error = (rate * miss).astype(BF)
    back_pre = dot(error, w_out_t)
    back_hidden = (back_pre * key_slope).astype(BF)
    gram = jnp.where(causal, batch_dot("bik,bjk->bij", split(key_mem), split(key_mem)), 0.0).astype(BF)
    new_hidden = key_hidden - join(batch_dot("bij,bjk->bik", gram, split(back_hidden)))
    _, new_silu, new_slope = silu_parts(new_hidden)
    new_act = new_silu.astype(BF)
    pair = jnp.where(causal, batch_dot("bik,bjk->bij", split(new_act), split(key_act)), 0.0).astype(BF)
    update = dot_t(new_act, w_out_t) - join(batch_dot("bij,bjk->bik", pair, split(error)))
    after_mem = after_attn + chain_sum(update).astype(F32)

    r3 = rms(after_mem)
    n3 = (after_mem * r3 * g_ffn).astype(BF)
    gate, up = dot(n3, wg), dot(n3, wu)
    _, gate_silu, gate_slope = silu_parts(gate)
    ffn_act = (gate_silu * up).astype(BF)
    ffn_part = dot_t(ffn_act, wd_t).astype(BF)

    d_ffn = dot(d_out_low, wd_t)
    d_gate = (d_ffn * up * gate_slope).astype(BF)
    d_up = (d_ffn * gate_silu).astype(BF)
    d_n3, gw_ffn = chain_sum(
        dot_t(d_gate, wg) + dot_t(d_up, wu),
        2,
        [[(d_out_low, ffn_act)], [(n3, d_gate)], [(n3, d_up)]],
    )
    d_n3 = d_n3.astype(F32)
    gg_ffn = jnp.sum(d_n3 * after_mem * r3, axis=0)
    d_after_mem = d_out_low.astype(F32) + rms_back(after_mem, r3, g_ffn, d_n3)
    d_update = d_after_mem.astype(BF)

    d_pair = jnp.where(
        causal, -batch_dot("bik,bjk->bij", split(d_update), split(error)), 0.0
    ).astype(BF)
    d_new_act = dot(d_update, w_out_t) + join(batch_dot("bij,bjk->bik", d_pair, split(key_act)))
    d_key_act = join(batch_dot("bij,bik->bjk", d_pair, split(new_act)))
    d_new_hidden = (d_new_act * new_slope).astype(BF)
    d_gram = jnp.where(
        causal, -batch_dot("bik,bjk->bij", split(d_new_hidden), split(back_hidden)), 0.0
    ).astype(BF)
    d_back = (-join(batch_dot("bij,bik->bjk", gram, split(d_new_hidden)))).astype(BF).astype(F32)
    d_back_pre = (d_back * key_slope).astype(BF)
    slope_grad = key_s * (1.0 - key_s) * (2.0 + key_hidden * (1.0 - 2.0 * key_s))
    d_hidden_part = d_new_hidden.astype(F32) + d_back * back_pre * slope_grad
    d_error_part = dot_t(d_back_pre, w_out_t) - join(
        batch_dot("bij,bik->bjk", pair, split(d_update))
    )
    share_ffn = lax.psum_scatter(gw_ffn, "dp", scatter_dimension=0, tiled=True)
    d_error = chain_sum(d_error_part).astype(F32)
    d_rate = jnp.sum(d_error * miss, axis=1, keepdims=True)
    d_miss = (rate * d_error).astype(BF)
    d_key_act = d_key_act + dot(d_miss, w_out_t)
    d_key_hidden = (d_hidden_part + d_key_act * key_slope).astype(BF)
    d_key_part = dot_t(d_key_hidden, w_in) + join(
        batch_dot("bij,bjk->bik", d_gram, split(key_mem))
        + batch_dot("bij,bik->bjk", d_gram, split(key_mem))
    )
    d_key, gw_out_early = chain_sum(
        d_key_part, 6, [[(d_update, new_act), (error, d_back_pre)]]
    )
    d_key, ffn_part = together(d_key, ffn_part)
    ffn_own = lax.psum_scatter(ffn_part, "tensor", scatter_dimension=1, tiled=True)
    d_n2 = dot(d_key, wkm_t) - dot(d_miss, wvm_t)
    d_logit = d_rate * rate * (1.0 - rate_s)
    gg_rate = jnp.sum(n2 * d_logit, axis=0)
    d_n2 = d_n2 + d_logit * rate_w
    gg_mem = jnp.sum(d_n2 * after_attn * r2, axis=0)
    late_r2, share_ffn = together(r2, share_ffn)
    d_after_attn = d_after_mem + rms_back(after_attn, late_r2, g_mem, d_n2)
    d_attn = d_after_attn.astype(BF)

    d_mixed = dot(d_attn, wo_t).astype(BF)
    d_qkv = local_call(
        functools.partial(attend_back_kernel, slots), qkv.shape, qkv, allowed, d_mixed
    )
    d_rows = d_qkv[slots + count :]
    d_context = dot_t(d_qkv[: slots + count, inner:], w_kv).astype(BF)
    d_persist_part = d_context[:slots]
    d_memory, gw_attn = chain_sum(
        d_context[slots:],
        3,
        [
            [(d_key, n2_own)],
            [(d_miss, n2_own)],
            [(d_attn, mixed)],
            [(all_rows, d_qkv)],
        ],
    )
    d_n1_part = dot_t(d_rows, w_qkv)

    share_attn = lax.psum_scatter(gw_attn, "dp", scatter_dimension=0, tiled=True)
    d_memory, ffn_own = together(d_memory, ffn_own)
    result_own = (own(after_mem) + ffn_own.astype(F32)).astype(BF)
    result_back = exchange(t_dot(deal_m, result_own).astype(BF))
    d_read = (dot(d_memory, w_out_t) * read_slope).astype(BF)
    d_query_mem, gw_mem = chain_sum(
        dot_t(d_read, w_in),
        4,
        [
            [(key_mem, d_key_hidden), (query_mem, d_read)],
            [(d_miss, key_act), (d_memory, read_low), (gw_out_early,)],
        ],
        inner,
    )
    gw_query_mem = t_dot(d_query_mem, n1_own).astype(BF)
    gw_mem = lax.dynamic_update_slice(gw_mem, gw_query_mem, (0, 2 * hidden))
    share_mem = lax.psum_scatter(gw_mem, "dp", scatter_dimension=0, tiled=True)
    d_n1_part = d_n1_part + in_own(dot(d_query_mem, wqm_t))
    d_persist_part, share_attn = together(d_persist_part.astype(BF), share_attn)
    last = chain_sum(jnp.concatenate([d_n1_part.astype(BF), d_persist_part], axis=0), 5)
    last, result_back = together(last, result_back)
    d_n1 = last[:count].astype(F32)
    g_persist = last[count:]
    gg_attn = jnp.sum(d_n1 * x * r1, axis=0)
    d_x = d_after_attn + rms_back(x, r1, g_attn, d_n1)

    def cut(share, *widths):
        return [part.astype(F32) for part in cut_apart(share, *widths)]

    s_down, s_gate, s_up = cut(share_ffn, *[w_gate.shape[1]] * 3)
    s_key_mem, s_value_mem, s_output, s_query, s_key, s_value = cut(share_attn, *[inner] * 6)
    s_in, s_out, s_query_mem = cut(share_mem, hidden, hidden, inner)
    grad_vectors = jnp.stack([gg_attn, gg_mem, gg_ffn, gg_rate], axis=1)
    rest = jnp.concatenate(
        [
            g_persist.T,
            grad_vectors.astype(BF),
            jnp.zeros((width, 128 - slots - 4), BF),
        ],
        axis=1,
    ).reshape(ranks, -1, width)
    turned = t_dot(deal_m, d_x.astype(BF)).astype(BF).reshape(ranks, -1, width)
    came = lax.all_to_all(
        jnp.concatenate([turned, rest], axis=1), "dp", split_axis=0, concat_axis=0, tiled=True
    )
    output = line_gather(t_dot(send_m, result_back).astype(BF), 8, True)
    came, output = together(came, output)
    seats = count // ranks
    grad_tokens = t_dot(send_m, came[:, :seats].reshape(count, width)).astype(BF)
    share_rest = jnp.sum(came[:, seats:].astype(F32), axis=0).reshape(shard, -1)
    s_small = share_rest
    s_vectors = s_small[:, slots : slots + 4].T

    return (
        output,
        grad_tokens,
        s_small[:, :slots].T,
        s_vectors[0],
        s_query_mem.T,
        s_in,
        s_out.T,
        s_query,
        s_key,
        s_value,
        s_output.T,
        s_vectors[1],
        s_key_mem.T,
        -s_value_mem.T,
        s_vectors[3],
        s_vectors[2],
        s_gate,
        s_up,
        s_down.T,
    )


def solution(mesh):
    rows = P("dp", None)
    vector = P("dp")
    across = P("tensor", "dp")
    along = P("dp", "tensor")
    return jax.shard_map(
        per_device,
        mesh=mesh,
        in_specs=(
            rows,
            rows,
            vector,
            vector,
            rows,
            P(None, "dp"),
            vector,
            across,
            along,
            across,
            along,
            along,
            along,
            across,
            vector,
            across,
            across,
            vector,
            vector,
            along,
            along,
            across,
        ),
        out_specs=(
            rows,
            rows,
            P(None, "dp"),
            vector,
            across,
            along,
            across,
            along,
            along,
            along,
            across,
            vector,
            across,
            across,
            vector,
            vector,
            along,
            along,
            across,
        ),
        check_vma=False,
    )
```
